128 devices in a mesh: dp: 16 (over y_lo, x, core), tensor: 8 (over y_hi, z).
Axes of the slice: x: 4, y: 4 (y_hi: 2, y_lo: 2; y = y_hi * 2 + y_lo), z: 4, core: 2. Of those that a mesh axis runs over, the one named last changes fastest.
Arguments:
- tokens: bfloat16 [12288, 2048], P('dp'), may hold values from -6 to 6
- cotangent: bfloat16 [12288, 2048], P('dp'), may hold values from -6 to 6
- segments: int32 [12288], replicated, may hold values from 0 to 15, never falling along the last dimension, each value on 1 to 1537 neighbouring positions
- attn_norm_gain: float32 [2048], P('dp'), may hold values from 0.5 to 1.5
- attn_norm_bias: float32 [2048], P('dp'), may hold values from -1.25 to 1.25
- query_weight: float32 [2048, 2048], P('dp', 'tensor'), may hold values from -0.125 to 0.125
- query_bias: float32 [16, 128], P('tensor', 'dp'), may hold values from -1.25 to 1.25
- kv_weight: float32 [2048, 256], P('dp'), may hold values from -0.125 to 0.125
- value_bias: float32 [128], P('dp'), may hold values from -1.25 to 1.25
- out_weight: float32 [2048, 2048], P('tensor', 'dp'), may hold values from -0.5 to 0.5
- out_bias: float32 [2048], P('dp'), may hold values from -1.25 to 1.25
- mlp_norm_gain: float32 [2048], P('dp'), may hold values from 0.5 to 1.5
- mlp_norm_bias: float32 [2048], P('dp'), may hold values from -1.25 to 1.25
- up_weight: float32 [2048, 8192], P('dp', 'tensor'), may hold values from -0.125 to 0.125
- up_bias: float32 [64, 128], P('tensor', 'dp'), may hold values from -1.25 to 1.25
- down_weight: float32 [8192, 2048], P('tensor', 'dp'), may hold values from -0.0625 to 0.0625
- down_bias: float32 [2048], P('dp'), may hold values from -1.25 to 1.25
Outputs:
- output: bfloat16 [12288, 2048], P('dp')
- input_grad: float32 [12288, 2048], P('dp')
- attn_norm_gain_grad: float32 [2048], P('dp')
- attn_norm_bias_grad: float32 [2048], P('dp')
- query_weight_grad: float32 [2048, 2048], P('dp', 'tensor')
- query_bias_grad: float32 [16, 128], P('tensor', 'dp')
- kv_weight_grad: float32 [2048, 256], P('dp')
- value_bias_grad: float32 [128], P('dp')
- out_weight_grad: float32 [2048, 2048], P('tensor', 'dp')
- out_bias_grad: float32 [2048], P('dp')
- mlp_norm_gain_grad: float32 [2048], P('dp')
- mlp_norm_bias_grad: float32 [2048], P('dp')
- up_weight_grad: float32 [2048, 8192], P('dp', 'tensor')
- up_bias_grad: float32 [64, 128], P('tensor', 'dp')
- down_weight_grad: float32 [8192, 2048], P('tensor', 'dp')
- down_bias_grad: float32 [2048], P('dp')
The draws below stay inside these ranges and needn't reach their ends.
Inputs may be any that keep to these rules, and one draw needn't show every extreme that they name: `segments`: segment numbers never fall along the stream; every document spans 1 to 1537 consecutive tokens, and some document spans exactly 1537.
All inputs are finite; a program needn't handle non-finite values.
Results may differ from the reference program's by a relative error of at most 0.03.
Values may be sent and summed in bfloat16 or wider, within the bound.
A program may use at most 192 MiB of HBM per device.

```python
import math
import jax
import jax.numpy as jnp
import numpy as np
from jax import lax

D = 2048
HEADS = 16
HD = 128
FF = 8192
TOK_DEV = 768
TOKENS = 12288
MAXDOC = 1537
DOCS = 16


def level_of(stream_key, shape, split, low, largest):
    factor_of = 1.0
    for axis_at, shards_of in split:
        heights = jax.random.uniform(jax.random.fold_in(jax.random.fold_in(stream_key, 6), axis_at), (shards_of,), jnp.float32, low / len(split), largest / len(split))
        factor_of = factor_of * jnp.repeat(jnp.exp(heights), shape[axis_at] // shards_of).reshape((-1,) + (1,) * (len(shape) - 1 - axis_at))
    return factor_of


def split_up(amount, total, bound, slope):
    weights = [(1 << 20) // math.isqrt(standing ** slope) + 1 for standing in range(2, amount + 1)]
    spare, given = total - bound - (amount - 1), [1] * (amount - 1)
    while spare > 0:
        candidates = [i for i in range(amount - 1) if given[i] < bound]
        pool, left = sum([weights[i] for i in candidates]), spare
        for i in candidates:
            more = min(bound - given[i], max(1, left * weights[i] // pool), spare)
            given[i] = given[i] + more
            spare = spare - more
    return np.array([bound] + given)


def ragged_sizes(rng, number_of, total, limit, slope):
    if number_of == 2:
        one = jax.random.randint(rng, (), max(1, total - limit), min(limit, total - 1) + 1)
        return jnp.stack([one, total - one])
    tallies = jnp.asarray(split_up(number_of, total, limit, slope), jnp.int32)
    couples = (number_of - 1) // 2
    donor, taker = tallies[1:1 + 2 * couples:2], tallies[2:2 + 2 * couples:2]
    margin = jnp.minimum(donor - 1, limit - taker)
    moved = jax.random.randint(jax.random.fold_in(rng, 1), (couples,), 0, 1 << 20) % (margin + 1)
    tallies = tallies.at[1:1 + 2 * couples:2].set(donor - moved).at[2:2 + 2 * couples:2].set(taker + moved)
    return tallies[jax.random.permutation(jax.random.fold_in(rng, 2), number_of)]


def centred(own_key, extent, scale, bound, pieces=(), kind=jnp.bfloat16):
    values = scale * jax.random.normal(own_key, extent, jnp.float32)
    if pieces:
        values = values * level_of(own_key, extent, pieces, -0.22, 0.18)
    return jnp.clip(values, -bound, bound).astype(kind)


def setup_inputs(seed: int = 0) -> dict:
    key_of = jax.random.split(jax.random.key(seed), 18)
    return {
        "tokens": centred(key_of[0], (TOKENS, D), 1.0, 6.0, ((0, 16),)),
        "cotangent": centred(key_of[1], (TOKENS, D), 1.0, 6.0, ((0, 16),)),
        "segments": jnp.searchsorted(jnp.cumsum(ragged_sizes(key_of[2], DOCS, TOKENS, MAXDOC, 0)), jnp.arange(TOKENS), side="right").astype(jnp.int32),
        "attn_norm_gain": jnp.clip(1.0 + 0.1 * jax.random.normal(key_of[3], (D,), jnp.float32), 0.5, 1.5),
        "attn_norm_bias": centred(key_of[4], (D,), 0.2, 1.25, ((0, 16),), jnp.float32),
        "query_weight": centred(key_of[5], (D, D), D ** -0.5, 0.125, ((0, 16), (1, 8)), jnp.float32),
        "query_bias": centred(key_of[6], (HEADS, HD), 0.2, 1.25, ((0, 8), (1, 16)), jnp.float32),
        "kv_weight": centred(key_of[7], (D, 2 * HD), D ** -0.5, 0.125, ((0, 16),), jnp.float32),
        "value_bias": centred(key_of[8], (HD,), 0.2, 1.25, ((0, 16),), jnp.float32),
        "out_weight": centred(key_of[9], (D, D), (D // 16) ** -0.5, 0.5, ((0, 8), (1, 16)), jnp.float32),
        "out_bias": centred(key_of[10], (D,), 0.2, 1.25, ((0, 16),), jnp.float32),
        "mlp_norm_gain": jnp.clip(1.0 + 0.1 * jax.random.normal(key_of[11], (D,), jnp.float32), 0.5, 1.5),
        "mlp_norm_bias": centred(key_of[12], (D,), 0.2, 1.25, ((0, 16),), jnp.float32),
        "up_weight": centred(key_of[13], (D, FF), D ** -0.5, 0.125, ((0, 16), (1, 8)), jnp.float32),
        "up_bias": centred(key_of[14], (FF // HD, HD), 0.2, 1.25, ((0, 8), (1, 16)), jnp.float32),
        "down_weight": centred(key_of[15], (FF, D), FF ** -0.5, 0.0625, ((0, 8), (1, 16)), jnp.float32),
        "down_bias": centred(key_of[16], (D,), 0.2, 1.25, ((0, 16),), jnp.float32),
    }


@jax.custom_vjp
def low(v):
    return lax.optimization_barrier(v.astype(jnp.bfloat16)).astype(jnp.float32)

@jax.custom_vjp
def low_back(v):
    return v

def low_keep(v):
    return (low(v), None)

def low_pass(kept, grad):
    return (grad,)

def back_keep(v):
    return (v, None)

def back_low(kept, grad):
    return (low(grad),)
low.defvjp(low_keep, low_pass)
low_back.defvjp(back_keep, back_low)
EPS = 1e-05
NEG = -1e+30
HIGH = lax.Precision.HIGHEST

def norm_rows(values, gain, shift):
    center = values - lax.optimization_barrier(jnp.mean(values, axis=-1, keepdims=True))
    spread = lax.optimization_barrier(jnp.mean(center * center, axis=-1, keepdims=True))
    return center * lax.rsqrt(spread + EPS) * gain + shift

def gelu_tanh(upward):
    inner = 0.7978845608028654 * (upward + 0.044715 * upward * upward * upward)
    return 0.5 * upward * (1.0 + jnp.tanh(inner))

def matmul(left, right):
    return jnp.dot(left, right, precision=HIGH, preferred_element_type=jnp.float32)

def reference(tokens, cotangent, segments, attn_norm_gain, attn_norm_bias, query_weight, query_bias, kv_weight, value_bias, out_weight, out_bias, mlp_norm_gain, mlp_norm_bias, up_weight, up_bias, down_weight, down_bias):
    scale = 1.0 / math.sqrt(HD)
    positions = jnp.arange(TOKENS, dtype=jnp.int32)

    def attend(block_query, start, keys, values):
        rows = start + jnp.arange(TOK_DEV, dtype=jnp.int32)
        query_seg = lax.dynamic_slice_in_dim(segments, start, TOK_DEV)
        allowed = (query_seg[:, None] == segments[None, :]) & (positions[None, :] <= rows[:, None])
        scores = jnp.einsum('qhd,kd->hqk', block_query, keys, precision=HIGH) * scale
        scores = low_back(scores)
        scores = jnp.where(allowed[None], scores, NEG)
        top = lax.optimization_barrier(jnp.max(scores, axis=-1, keepdims=True))
        weights = jnp.exp(scores - top)
        probs = weights / lax.optimization_barrier(jnp.sum(weights, axis=-1, keepdims=True))
        return jnp.einsum('hqk,kd->qhd', low(probs), values, precision=HIGH)

    def layer(inputs, gain_one, shift_one, query_w, query_b, kv_w, value_b, out_w, out_b, gain_two, shift_two, up_w, up_b, down_w, down_b):
        gain_one = low(gain_one)
        shift_one = low(shift_one)
        query_w = low(query_w)
        query_b = low(query_b)
        kv_w = low(kv_w)
        value_b = low(value_b)
        out_w = low(out_w)
        out_b = low(out_b)
        gain_two = low(gain_two)
        shift_two = low(shift_two)
        up_w = low(up_w)
        up_b = low(up_b)
        down_w = low(down_w)
        down_b = low(down_b)
        normed_one = low(norm_rows(inputs, gain_one, shift_one))
        query = low(low_back(matmul(normed_one, query_w) + query_b.reshape(D)))
        keyval = matmul(normed_one, kv_w) + jnp.concatenate([jnp.zeros((HD,), jnp.float32), value_b])
        keyval = low(low_back(keyval))
        keys = keyval[:, :HD]
        values = keyval[:, HD:]
        blocks = query.reshape(TOKENS // TOK_DEV, TOK_DEV, HEADS, HD)
        starts = jnp.arange(TOKENS // TOK_DEV, dtype=jnp.int32) * TOK_DEV

        def one_block(pair):
            return attend(pair[0], pair[1], keys, values)
        mixed = lax.map(jax.checkpoint(one_block), (blocks, starts))
        attended = low(low_back(mixed.reshape(TOKENS, D)))
        attn_branch = low_back(matmul(attended, out_w) + out_b)
        middle = inputs + attn_branch
        normed_two = low(norm_rows(middle, gain_two, shift_two))
        upward = low_back(matmul(normed_two, up_w) + up_b.reshape(FF))
        hidden = low(gelu_tanh(upward))
        mlp_branch = low_back(matmul(hidden, down_w) + down_b)
        return middle + mlp_branch
    result, backward = jax.vjp(layer, tokens.astype(jnp.float32), attn_norm_gain, attn_norm_bias, query_weight, query_bias, kv_weight, value_bias, out_weight, out_bias, mlp_norm_gain, mlp_norm_bias, up_weight, up_bias, down_weight, down_bias)
    grads = backward(cotangent.astype(jnp.float32))
    return (result.astype(jnp.bfloat16), grads[0], grads[1], grads[2], grads[3], grads[4], grads[5], grads[6], grads[7], grads[8], grads[9], grads[10], grads[11], grads[12], grads[13], grads[14])
```

```python
import functools
import math

import jax
import jax.numpy as jnp
from jax import lax
from jax.experimental import pallas as pl
from jax.experimental.pallas import tpu as pltpu
from jax.sharding import PartitionSpec as P

HD = 128
EPS = 1e-05
NEG = -1e30
MESH = pl.DeviceIdType.MESH
bf16 = jnp.bfloat16
f32 = jnp.float32


class Place:
    def __init__(self):
        dp = lax.axis_index("dp")
        tensor = lax.axis_index("tensor")
        self.core = dp % 2
        self.x = (dp // 2) % 4
        self.y = (tensor // 4) * 2 + dp // 8
        self.z = tensor % 4

    def dev(self, x=None, y=None, z=None, core=None):
        x = self.x if x is None else x
        y = self.y if y is None else y
        z = self.z if z is None else z
        core = self.core if core is None else core
        return ((y % 2) * 8 + x * 2 + core, (y // 2) * 4 + z)

    def sibling(self):
        return self.dev(core=1 - self.core)

    def ring(self, axis):
        return Ring(self, axis)


class Ring:
    def __init__(self, place, axis):
        self.p = getattr(place, axis)
        self.plus = place.dev(**{axis: (self.p + 1) % 4})
        self.minus = place.dev(**{axis: (self.p + 3) % 4})
        self.after = (self.p + 1) % 4
        self.before = (self.p + 3) % 4
        self.across = (self.p + 2) % 4


class Net:
    def __init__(self, ssem, rsem, lsem):
        self.ssem, self.rsem, self.lsem = ssem, rsem, lsem
        self.n = 0
        self.m = 0
        self.sent = []
        self.todo = []

    def send(self, src, dst, dev):
        i = self.n
        self.n += 1
        copy = pltpu.make_async_remote_copy(
            src_ref=src,
            dst_ref=dst,
            send_sem=self.ssem.at[i],
            recv_sem=self.rsem.at[i],
            device_id=dev,
            device_id_type=MESH,
        )
        copy.start()
        self.sent.append(copy)
        return copy

    def local(self, src, dst):
        i = self.m
        self.m += 1
        copy = pltpu.make_async_copy(src, dst, self.lsem.at[i])
        copy.start()
        return copy

    def run(self, *gens):
        self.todo.extend(gens)
        while self.todo:
            for gen in list(self.todo):
                try:
                    next(gen)
                except StopIteration:
                    self.todo.remove(gen)
        for copy in self.sent:
            copy.wait_send()


def greet(devices):
    barrier = pltpu.get_barrier_semaphore()
    for device in devices:
        pl.semaphore_signal(barrier, inc=1, device_id=device, device_id_type=MESH)
    pl.semaphore_wait(barrier, len(devices))


def rows_half(ref, which):
    n = ref.shape[-2] // 2
    if len(ref.shape) == 2:
        return ref.at[pl.ds(which * n, n), :]
    return ref.at[:, pl.ds(which * n, n), :]


def lane_step(shape):
    return max(16, min(shape[0], 32768 // shape[1]))


def over_rows(rows, step, fn):
    def one(i, carry):
        fn(pl.ds(pl.multiple_of(i * step, step), step))
        return carry

    lax.fori_loop(0, rows // step, one, 0)


def add_into(dst, *srcs, out=None):
    out = dst if out is None else out
    rows, step = dst.shape[0], lane_step(dst.shape)
    if rows % step:
        step = 16 if rows % 16 == 0 else rows

    def one(at):
        total = dst[at, :].astype(f32)
        for src in srcs:
            total = total + src[at, :].astype(f32)
        out[at, :] = total.astype(out.dtype)

    over_rows(rows, step, one)


def ag_ring(net, ring, slot, own, have=None):
    have = have or (lambda pos: None)
    c0 = net.send(own, slot(ring.p), ring.plus)
    c1 = net.send(own, slot(ring.p), ring.minus)
    yield
    c0.wait_recv()
    one = rows_half(slot(ring.before), 0)
    c2 = net.send(one, one, ring.plus)
    have(ring.before)
    c1.wait_recv()
    two = rows_half(slot(ring.after), 1)
    c3 = net.send(two, two, ring.minus)
    have(ring.after)
    yield
    c2.wait_recv()
    c3.wait_recv()
    have(ring.across)


def ag2d(net, place, own, slot, first, second):
    sib = place.sibling()
    pairs = []

    def give(a, b, src=None):
        ref = slot(a, b)
        pairs.append(net.send(ref if src is None else src, ref, sib))

    def column(a, src):
        return ag_ring(net, second, lambda b: slot(a, b), src, lambda b: give(a, b))

    def main():
        keep = net.local(own, slot(first.p, second.p))
        c0 = net.send(own, slot(first.p, second.p), first.plus)
        c1 = net.send(own, slot(first.p, second.p), first.minus)
        net.todo.append(column(first.p, own))
        give(first.p, second.p, own)
        yield
        c0.wait_recv()
        one = rows_half(slot(first.before, second.p), 0)
        c2 = net.send(one, one, first.plus)
        net.todo.append(column(first.before, slot(first.before, second.p)))
        c1.wait_recv()
        two = rows_half(slot(first.after, second.p), 1)
        c3 = net.send(two, two, first.minus)
        net.todo.append(column(first.after, slot(first.after, second.p)))
        give(first.before, second.p)
        give(first.after, second.p)
        yield
        c2.wait_recv()
        c3.wait_recv()
        net.todo.append(column(first.across, slot(first.across, second.p)))
        give(first.across, second.p)
        keep.wait()
        while len(pairs) < 16:
            yield
        for pair in pairs:
            pair.wait_recv()

    return main()


def rs_ring(net, ring, src, ra, rb, done):
    across, after, before = src(ring.across), src(ring.after), src(ring.before)
    a0 = net.send(rows_half(across, 0), ra(0), ring.plus)
    a1 = net.send(rows_half(across, 1), ra(1), ring.minus)
    b0 = net.send(rows_half(after, 1), rows_half(rb(0), 1), ring.plus)
    b1 = net.send(rows_half(before, 0), rows_half(rb(1), 0), ring.minus)
    yield
    a0.wait_recv()
    add_into(ra(0), rows_half(after, 0))
    b2 = net.send(ra(0), rows_half(rb(0), 0), ring.plus)
    a1.wait_recv()
    add_into(ra(1), rows_half(before, 1))
    b3 = net.send(ra(1), rows_half(rb(1), 1), ring.minus)
    yield
    for copy in (b0, b1, b2, b3):
        copy.wait_recv()
    done(src(ring.p), rb(0), rb(1))


def rs2d(net, place, part, first, second, bufs, out):
    r0, rv, ra, rb, r1, sa, sb = bufs
    sib = place.sibling()
    firsts = (first.across, first.after, first.before, first.p)
    seconds = (second.across, second.after, second.before, second.p)
    come, keep = {}, {}
    for i, a in enumerate(firsts):
        for j, b in enumerate(seconds):
            come[i, j] = net.send(part(a, b, 1 - place.core), rv.at[i, j], sib)
            keep[i, j] = net.local(part(a, b, place.core), r0.at[i, j])

    def pair(i, j):
        come[i, j].wait_recv()
        keep[i, j].wait()
        add_into(r0.at[i, j], rv.at[i, j])

    yield
    halves, wholes = {}, {}
    for j in range(4):
        pair(0, j)
        halves[0, j] = net.send(rows_half(r0.at[0, j], 0), ra.at[0, j], first.plus)
        halves[1, j] = net.send(rows_half(r0.at[0, j], 1), ra.at[1, j], first.minus)
    yield
    for j in range(4):
        pair(1, j)
        wholes[0, j] = net.send(rows_half(r0.at[1, j], 1), rows_half(rb.at[0, j], 1), first.plus)
        pair(2, j)
        wholes[1, j] = net.send(rows_half(r0.at[2, j], 0), rows_half(rb.at[1, j], 0), first.minus)
    yield
    for j in range(4):
        halves[0, j].wait_recv()
        add_into(ra.at[0, j], rows_half(r0.at[1, j], 0))
        wholes[2, j] = net.send(ra.at[0, j], rows_half(rb.at[0, j], 0), first.plus)
        halves[1, j].wait_recv()
        add_into(ra.at[1, j], rows_half(r0.at[2, j], 1))
        wholes[3, j] = net.send(ra.at[1, j], rows_half(rb.at[1, j], 1), first.minus)
        pair(3, j)
    yield

    def settle(j):
        for k in range(4):
            wholes[k, j].wait_recv()
        add_into(r0.at[3, j], rb.at[0, j], rb.at[1, j], out=r1.at[j])

    settle(0)
    a0 = net.send(rows_half(r1.at[0], 0), sa.at[0], second.plus)
    a1 = net.send(rows_half(r1.at[0], 1), sa.at[1], second.minus)
    settle(1)
    b0 = net.send(rows_half(r1.at[1], 1), rows_half(sb.at[0], 1), second.plus)
    settle(2)
    b1 = net.send(rows_half(r1.at[2], 0), rows_half(sb.at[1], 0), second.minus)
    settle(3)
    yield
    a0.wait_recv()
    add_into(sa.at[0], rows_half(r1.at[1], 0))
    b2 = net.send(sa.at[0], rows_half(sb.at[0], 0), second.plus)
    a1.wait_recv()
    add_into(sa.at[1], rows_half(r1.at[2], 1))
    b3 = net.send(sa.at[1], rows_half(sb.at[1], 1), second.minus)
    yield
    for copy in (b0, b1, b2, b3):
        copy.wait_recv()
    add_into(r1.at[3], sb.at[0], sb.at[1], out=out)


def rs2d_bufs(shape, dtype=bf16):
    rows, cols = shape
    half = (rows // 2, cols)
    return [
        pltpu.VMEM((4, 4) + shape, dtype),
        pltpu.VMEM((4, 4) + shape, dtype),
        pltpu.VMEM((2, 4) + half, dtype),
        pltpu.VMEM((2, 4) + shape, dtype),
        pltpu.VMEM((4,) + shape, dtype),
        pltpu.VMEM((2,) + half, dtype),
        pltpu.VMEM((2,) + shape, dtype),
    ]


def sems(count, local):
    return [
        pltpu.SemaphoreType.DMA((count,)),
        pltpu.SemaphoreType.DMA((count,)),
        pltpu.SemaphoreType.DMA((local,)),
    ]


ANY = pl.BlockSpec(memory_space=pl.ANY)
VM = pl.BlockSpec(memory_space=pltpu.VMEM)


def kernel_call(body, name, cid, ins, in_specs, outs, out_specs, scratch, nbytes=1 << 20):
    return pl.pallas_call(
        body,
        out_shape=[jax.ShapeDtypeStruct(s, d) for s, d in outs],
        in_specs=in_specs,
        out_specs=out_specs,
        scratch_shapes=scratch,
        compiler_params=pltpu.CompilerParams(
            collective_id=cid, has_side_effects=True, vmem_limit_bytes=56 << 20
        ),
        cost_estimate=pl.CostEstimate(flops=0, bytes_accessed=nbytes, transcendentals=0),
        name=name,
    )(*ins)


def block_of(x, y, core):
    return (y % 2) * 8 + x * 2 + core


def col_at(d):
    return pl.ds(pl.multiple_of(d * 128, 128), 128)


def row_at(start, size):
    return pl.ds(pl.multiple_of(start, size), size)


def at_query(ref, x, y, core):
    return ref.at[row_at(block_of(x, y, core) * 128, 128), row_at((y // 2) * 256, 256)]


def at_keyval(ref, x, y, core):
    return ref.at[row_at(block_of(x, y, core) * 128 + (y // 2) * 64, 64), :]


def at_out(ref, x, y, core):
    return ref.at[row_at((y // 2) * 256, 256), col_at(block_of(x, y, core))]


def at_up(ref, x, y, core):
    return ref.at[row_at(block_of(x, y, core) * 128, 128), row_at((y // 2) * 1024, 1024)]


def at_down(ref, x, y, core):
    return ref.at[row_at((y // 2) * 1024, 1024), col_at(block_of(x, y, core))]


def at_small(ref, x, y, core):
    return ref.at[y // 2, block_of(x, y, core)]


def gather(net, place, at, own, whole, order):
    x, y = place.ring("x"), place.ring("y")
    if order == "xy":
        return ag2d(net, place, own, lambda a, b: at(whole, a, b, place.core), x, y)
    return ag2d(net, place, own, lambda a, b: at(whole, b, a, place.core), y, x)


def scatter(net, place, at, part, order, bufs, out):
    x, y = place.ring("x"), place.ring("y")
    if order == "xy":
        return rs2d(net, place, lambda a, b, c: at(part, a, b, c), x, y, bufs, out)
    return rs2d(net, place, lambda a, b, c: at(part, b, a, c), y, x, bufs, out)


def plane_peers(place):
    x, y = place.ring("x"), place.ring("y")
    return [place.sibling(), x.plus, x.minus, y.plus, y.minus]


def gather_first(query_w, keyval_w, out_w, small, g_query, g_keyval, g_out, g_small, *sem):
    place = Place()
    greet(plane_peers(place))
    net = Net(*sem)
    net.run(
        gather(net, place, at_query, query_w, g_query, "xy"),
        gather(net, place, at_out, out_w, g_out, "yx"),
        gather(net, place, at_keyval, keyval_w, g_keyval, "xy"),
        gather(net, place, at_small, small, g_small, "yx"),
    )


def spread(values):
    center = values - jnp.mean(values, axis=-1, keepdims=True)
    return center, lax.rsqrt(jnp.mean(center * center, axis=-1, keepdims=True) + EPS)


def attn_out(part, tok, vecs, up_w, down_w, g_up, g_down, normed, middle, ra, rb, mine, *sem):
    place = Place()
    z = place.ring("z")
    greet(plane_peers(place) + [z.plus, z.minus])
    net = Net(*sem)

    def rows():
        def done(own, one, two):
            def some(at):
                mid = (
                    tok[at, :].astype(f32)
                    + own[at, :].astype(f32)
                    + one[at, :].astype(f32)
                    + two[at, :].astype(f32)
                    + vecs[0:1, :]
                )
                middle[at, :] = mid
                center, inv = spread(mid)
                mine[at, :] = (center * inv * vecs[1:2, :] + vecs[2:3, :]).astype(bf16)

            over_rows(96, 16, some)

        yield from rs_ring(net, z, lambda i: part.at[i], lambda i: ra.at[i], lambda i: rb.at[i], done)
        keep = net.local(mine, normed.at[z.p])
        yield from ag_ring(net, z, lambda i: normed.at[i], mine)
        keep.wait()

    net.run(
        rows(),
        gather(net, place, at_up, up_w, g_up, "xy"),
        gather(net, place, at_down, down_w, g_down, "yx"),
    )


def mlp_back(
    part_out, part_norm, middle, cot, vecs, part_up, part_down,
    out_rows, grad_mid, grad_all, sums, up_grad, down_grad,
    ra, rb, rc, rd, mine, *rest,
):
    place = Place()
    z = place.ring("z")
    greet(plane_peers(place) + [z.plus, z.minus])
    ups, downs, sem = rest[:7], rest[7:14], rest[14:]
    net = Net(*sem)

    def back():
        def done(own, one, two):
            sums[...] = jnp.zeros_like(sums)

            def some(at):
                grad = own[at, :].astype(f32) + one[at, :].astype(f32) + two[at, :].astype(f32)
                center, inv = spread(middle[at, :])
                norm = center * inv
                flow = grad * vecs[1:2, :]
                top = cot[at, :].astype(f32)
                mid = top + inv * (
                    flow
                    - jnp.mean(flow, axis=-1, keepdims=True)
                    - norm * jnp.mean(flow * norm, axis=-1, keepdims=True)
                )
                grad_mid[at, :] = mid
                low = mid.astype(bf16)
                mine[at, :] = low
                sums[0:1, :] += jnp.sum(grad * norm, axis=0, keepdims=True)
                sums[1:2, :] += jnp.sum(grad, axis=0, keepdims=True)
                sums[2:3, :] += jnp.sum(low.astype(f32), axis=0, keepdims=True)
                sums[3:4, :] += jnp.sum(top, axis=0, keepdims=True)

            over_rows(96, 16, some)

        yield from rs_ring(
            net, z, lambda i: part_norm.at[i], lambda i: ra.at[i], lambda i: rb.at[i], done
        )
        keep = net.local(mine, grad_all.at[z.p])
        yield from ag_ring(net, z, lambda i: grad_all.at[i], mine)
        keep.wait()

    def fore():
        def done(own, one, two):
            def some(at):
                out_rows[at, :] = (
                    middle[at, :]
                    + own[at, :].astype(f32)
                    + one[at, :].astype(f32)
                    + two[at, :].astype(f32)
                    + vecs[0:1, :]
                ).astype(bf16)

            over_rows(96, 16, some)

        yield
        yield from rs_ring(
            net, z, lambda i: part_out.at[i], lambda i: rc.at[i], lambda i: rd.at[i], done
        )

    net.run(
        back(),
        scatter(net, place, at_up, part_up, "yx", ups, up_grad),
        scatter(net, place, at_down, part_down, "xy", downs, down_grad),
        fore(),
    )


def device_of_block(place, block):
    d = block // 2
    return ((d // 8) * 8 + ((d // 2) % 4) * 2 + d % 2, (block % 2) * 4 + place.z)


def attn_back(pieces, part, kv_grad, total, ra, rb, rk, stage, rz, *sem):
    place = Place()
    z = place.ring("z")
    peers = [place.dev(z=(place.z + k) % 4) for k in (1, 2, 3)]
    block = ((place.y % 2) * 8 + place.x * 2 + place.core) * 2 + place.y // 2
    earlier = [device_of_block(place, (block + 32 - k) % 32) for k in (1, 2, 3, 4)]
    later = [device_of_block(place, (block + k) % 32) for k in (1, 2, 3, 4)]
    greet(peers + earlier + later)
    net = Net(*sem)

    def kv():
        sent = [net.send(pieces.at[4 - k], rk.at[k - 1], earlier[k - 1]) for k in (1, 2, 3, 4)]
        yield
        for copy in sent:
            copy.wait_recv()
        for i in range(4):
            at = pl.ds(i * 96, 96)
            add_into(
                pieces.at[4, at], *[rk.at[k, at] for k in range(4)], out=stage.at[i]
            )
        out = [net.send(stage.at[(place.z + k) % 4], rz.at[k - 1], peers[k - 1]) for k in (1, 2, 3)]
        yield
        for copy in out:
            copy.wait_recv()
        add_into(stage.at[place.z], *[rz.at[k] for k in range(3)], out=kv_grad.at[place.z])
        home = kv_grad.at[place.z]
        out = [net.send(home, home, peer) for peer in peers]
        yield
        for copy in out:
            copy.wait_recv()

    def done(own, one, two):
        add_into(own, one, two, out=total)

    net.run(
        kv(),
        rs_ring(net, z, lambda i: part.at[i], lambda i: ra.at[i], lambda i: rb.at[i], done),
    )


def finish(
    out_rows, in_rows, part_query, part_keyval, part_out, part_small,
    output, input_grad, query_grad, keyval_grad, out_grad, small_grad,
    small_own, small_in, kv_own, *rest,
):
    place = Place()
    x, y, z = place.ring("x"), place.ring("y"), place.ring("z")
    partner = place.dev(y=y.across)
    across = place.dev(z=z.across)
    greet(plane_peers(place) + [z.plus, z.minus, partner, across])
    hi = place.y // 2
    queries, keyvals, outs, smalls, sem = (
        rest[:7], rest[7:14], rest[14:21], rest[21:28], rest[28:],
    )
    net = Net(*sem)

    def y_first(own, whole):
        keep = net.local(own, whole.at[hi, z.p])
        swap = net.send(own, whole.at[hi, z.p], partner)
        net.todo.append(ag_ring(net, z, lambda i: whole.at[hi, i], own))
        yield
        swap.wait_recv()
        net.todo.append(ag_ring(net, z, lambda i: whole.at[1 - hi, i], whole.at[1 - hi, z.p]))
        yield
        keep.wait()

    def z_first(own, whole):
        keep = net.local(own, whole.at[hi, z.p])
        swaps = [net.send(own, whole.at[hi, z.p], partner)]

        def have(i):
            ref = whole.at[hi, i]
            swaps.append(net.send(ref, ref, partner))

        yield from ag_ring(net, z, lambda i: whole.at[hi, i], own, have)
        yield
        keep.wait()
        for swap in swaps:
            swap.wait_recv()

    def keyval():
        yield from scatter(net, place, at_keyval, part_keyval, "yx", keyvals, kv_own)
        home = keyval_grad.at[pl.ds(pl.multiple_of(hi * 64, 64), 64), :]
        keep = net.local(kv_own, home)
        swap = net.send(kv_own, home, partner)
        yield
        keep.wait()
        swap.wait_recv()

    def small():
        yield from scatter(net, place, at_small, part_small, "xy", smalls, small_own)
        sent = [
            net.send(small_own, small_in.at[0], z.plus),
            net.send(small_own, small_in.at[1], z.minus),
            net.send(small_own, small_in.at[2], across),
        ]
        yield
        for copy in sent:
            copy.wait_recv()
        total = small_own[...]
        whole = total + small_in[0] + small_in[1] + small_in[2]
        row = lax.broadcasted_iota(jnp.int32, (16, 128), 0)
        small_grad[...] = jnp.where(row < 6, whole, total)

    net.run(
        z_first(in_rows, input_grad),
        small(),
        keyval(),
        y_first(out_rows, output),
        scatter(net, place, at_query, part_query, "xy", queries, query_grad),
        scatter(net, place, at_out, part_out, "yx", outs, out_grad),
    )


def matmul(left, right):
    return jnp.dot(left, right, preferred_element_type=f32)


def contract_rows(left, right):
    return lax.dot_general(left, right, (((0,), (0,)), ((), ())), preferred_element_type=f32)


def contract_cols(left, right):
    return lax.dot_general(left, right, (((1,), (1,)), ((), ())), preferred_element_type=f32)


def gelu_tanh(upward):
    inner = 0.7978845608028654 * (upward + 0.044715 * upward * upward * upward)
    return 0.5 * upward * (1.0 + jnp.tanh(inner))


def from_behind(value, axis, steps):
    count = lax.axis_size(axis)
    return lax.ppermute(value, axis, [(source, source + steps) for source in range(count - steps)])


def heads_to_rows(matrix, heads, rows):
    return matrix.reshape(rows, heads, HD).transpose(1, 0, 2).reshape(heads * rows, HD)


def rows_to_heads(matrix, heads, rows):
    return matrix.reshape(heads, rows, HD).transpose(1, 0, 2).reshape(rows, heads * HD)


def body(
    tokens, cotangent, segments, attn_norm_gain, attn_norm_bias, query_weight, query_bias,
    kv_weight, value_bias, out_weight, out_bias, mlp_norm_gain, mlp_norm_bias, up_weight,
    up_bias, down_weight, down_bias,
):
    dp = lax.axis_index("dp")
    tensor = lax.axis_index("tensor")
    hi, z = tensor // 4, tensor % 4
    scale = 1.0 / math.sqrt(HD)
    half, heads = 384, 4

    rest = jnp.concatenate([query_bias.reshape(-1), up_bias.reshape(-1), value_bias.reshape(-1)])
    small = jnp.stack(
        [attn_norm_gain, attn_norm_bias, out_bias, mlp_norm_gain, mlp_norm_bias, down_bias,
         jnp.pad(rest, (0, 40))]
    )
    small = jnp.pad(small, ((0, 9), (0, 0))).astype(bf16).astype(f32)
    keyval_own = lax.dynamic_slice_in_dim(kv_weight, hi * 64, 64).astype(bf16)
    query_w, keyval_w, out_w, small_all = kernel_call(
        gather_first, "gather_first", 0,
        [query_weight.astype(bf16), keyval_own, out_weight.astype(bf16), small],
        [ANY] * 4,
        [((2048, 512), bf16), ((2048, 256), bf16), ((512, 2048), bf16), ((2, 16, 16, 128), f32)],
        [ANY] * 4,
        sems(160, 8),
    )
    vectors = small_all[0, :, :6].transpose(1, 0, 2).reshape(6, 2048)
    gain_one, shift_one, out_b, gain_two, shift_two, down_b = (vectors[i] for i in range(6))
    others = small_all[:, :, 6]
    query_b = others[:, :, :16].reshape(2, 16, 2, 8).transpose(0, 2, 1, 3).reshape(512)
    up_b = others[:, :, 16:80].reshape(2, 16, 8, 8).transpose(0, 2, 1, 3).reshape(2048)
    value_b = others[0, :, 80:88].reshape(128)

    center, inv = spread(tokens.astype(f32))
    normed_all = (center * inv * gain_one + shift_one).astype(bf16)
    normed_one = lax.dynamic_slice_in_dim(normed_all, hi * half, half)
    keyval = (
        matmul(normed_all, keyval_w) + jnp.concatenate([jnp.zeros((HD,), f32), value_b])
    ).astype(bf16)
    query = (matmul(normed_one, query_w) + query_b).astype(bf16)
    window = jnp.concatenate([from_behind(keyval, "dp", 2), from_behind(keyval, "dp", 1), keyval])
    window = lax.dynamic_slice_in_dim(window, hi * half, 5 * half)
    keys, values = window[:, :HD], window[:, HD:]
    start = dp * 768 + hi * half
    key_seg = lax.dynamic_slice_in_dim(
        jnp.concatenate([jnp.full((4 * half,), -1, jnp.int32), segments]), start, 5 * half
    )
    query_seg = lax.dynamic_slice_in_dim(segments, start, half)
    allowed = (query_seg[:, None] == key_seg[None, :]) & (
        jnp.arange(5 * half)[None, :] <= 4 * half + jnp.arange(half)[:, None]
    )
    allowed = jnp.tile(allowed, (heads, 1))
    query_rows = heads_to_rows(query, heads, half)
    scores = jnp.where(allowed, contract_cols(query_rows, keys) * scale, NEG)
    top = jnp.max(scores, axis=-1, keepdims=True)
    log_total = top + jnp.log(jnp.sum(jnp.exp(scores - top), axis=-1, keepdims=True))
    probs = jnp.exp(scores - log_total).astype(bf16)
    attended = rows_to_heads(matmul(probs, values).astype(bf16), heads, half)
    attn_part = matmul(attended, out_w).astype(bf16).reshape(4, 96, 2048)

    mine = hi * half + z * 96
    tok_rows = lax.dynamic_slice_in_dim(tokens, mine, 96)
    cot_rows = lax.dynamic_slice_in_dim(cotangent, mine, 96)
    up_w, down_w, normed_two, middle = kernel_call(
        attn_out, "attn_out", 1,
        [attn_part, tok_rows, jnp.stack([out_b, gain_two, shift_two]), up_weight.astype(bf16),
         down_weight.astype(bf16)],
        [VM, VM, VM, ANY, ANY],
        [((2048, 2048), bf16), ((2048, 2048), bf16), ((4, 96, 2048), bf16), ((96, 2048), f32)],
        [ANY, ANY, ANY, VM],
        [pltpu.VMEM((2, 48, 2048), bf16), pltpu.VMEM((2, 96, 2048), bf16), pltpu.VMEM((96, 2048), bf16)]
        + sems(96, 8),
    )
    normed_two = normed_two.reshape(half, 2048)

    cot = lax.dynamic_slice_in_dim(cotangent, hi * half, half)
    hidden, gelu_back = jax.vjp(gelu_tanh, matmul(normed_two, up_w) + up_b)
    hidden = hidden.astype(bf16)
    mlp_part = matmul(hidden, down_w).astype(bf16).reshape(4, 96, 2048)
    down_part = contract_rows(hidden, cot).astype(bf16)
    grad_up = gelu_back(contract_cols(cot, down_w))[0].astype(bf16)
    up_bias_sum = jnp.sum(grad_up.astype(f32), axis=0)
    up_part = contract_rows(normed_two, grad_up).astype(bf16)
    norm_part = contract_cols(grad_up, up_w).astype(bf16).reshape(4, 96, 2048)
    out_rows, grad_middle, grad_attn, sums, up_grad, down_grad = kernel_call(
        mlp_back, "mlp_back", 2,
        [mlp_part, norm_part, middle, cot_rows, jnp.stack([down_b, gain_two]), up_part, down_part],
        [VM, VM, VM, VM, VM, ANY, ANY],
        [((96, 2048), bf16), ((96, 2048), f32), ((4, 96, 2048), bf16), ((8, 2048), f32),
         ((128, 1024), f32), ((1024, 128), f32)],
        [VM, VM, ANY, VM, VM, VM],
        [pltpu.VMEM((2, 48, 2048), bf16), pltpu.VMEM((2, 96, 2048), bf16)] * 2
        + [pltpu.VMEM((96, 2048), bf16)]
        + rs2d_bufs((128, 1024)) + rs2d_bufs((1024, 128)) + sems(128, 40),
    )
    grad_attn = grad_attn.reshape(half, 2048)

    out_part = contract_rows(attended, grad_attn).astype(bf16)
    grad_rows = heads_to_rows(contract_cols(grad_attn, out_w).astype(bf16), heads, half)
    probs_again = jnp.exp(
        jnp.where(allowed, contract_cols(query_rows, keys) * scale, NEG) - log_total
    )
    grad_probs = contract_cols(grad_rows, values)
    delta = jnp.sum(probs_again * grad_probs, axis=-1, keepdims=True)
    grad_scores = (probs_again * (grad_probs - delta)).astype(bf16)
    grad_query = rows_to_heads((matmul(grad_scores, keys) * scale).astype(bf16), heads, half)
    grad_keys = contract_rows(grad_scores, query_rows) * scale
    grad_values = contract_rows(probs_again.astype(bf16), grad_rows)
    pieces = jnp.concatenate([grad_keys, grad_values], 1).astype(bf16).reshape(5, half, 256)
    norm_part = contract_cols(grad_query, query_w).astype(bf16).reshape(4, 96, 2048)
    kv_grad, total = kernel_call(
        attn_back, "attn_back", 3,
        [pieces, norm_part], [VM, VM],
        [((4, 96, 256), bf16), ((96, 2048), f32)], [VM, VM],
        [pltpu.VMEM((2, 48, 2048), bf16), pltpu.VMEM((2, 96, 2048), bf16),
         pltpu.VMEM((4, half, 256), bf16), pltpu.VMEM((4, 96, 256), bf16),
         pltpu.VMEM((3, 96, 256), bf16)] + sems(24, 4),
    )
    kv_rows = lax.dynamic_index_in_dim(kv_grad, z, 0, keepdims=False)
    kv_grad = kv_grad.reshape(half, 256)
    query_bias_sum = jnp.sum(grad_query.astype(f32), axis=0)
    query_part = contract_rows(normed_one, grad_query).astype(bf16)
    keyval_part = contract_rows(normed_one, kv_grad).astype(bf16)
    value_bias_sum = jnp.sum(kv_grad[:, HD:].astype(f32), axis=0)
    grad_norm = total + contract_cols(kv_rows, keyval_w)
    center, inv = spread(tok_rows.astype(f32))
    norm = center * inv
    flow = grad_norm * gain_one
    in_rows = grad_middle + inv * (
        flow
        - jnp.mean(flow, axis=-1, keepdims=True)
        - norm * jnp.mean(flow * norm, axis=-1, keepdims=True)
    )
    gain_sum = jnp.sum(grad_norm * norm, axis=0)
    shift_sum = jnp.sum(grad_norm, axis=0)
    six = jnp.stack([gain_sum, shift_sum, sums[2], sums[0], sums[1], sums[3]])
    six = jnp.broadcast_to(six.reshape(6, 16, 128).transpose(1, 0, 2)[None], (2, 16, 6, 128))
    last = jnp.concatenate(
        [
            query_bias_sum.reshape(2, 2, 16, 8).transpose(0, 2, 1, 3).reshape(2, 16, 16),
            up_bias_sum.reshape(2, 8, 16, 8).transpose(0, 2, 1, 3).reshape(2, 16, 64),
            jnp.broadcast_to(value_bias_sum.reshape(16, 8)[None], (2, 16, 8)),
            jnp.zeros((2, 16, 40), f32),
        ],
        axis=-1,
    )
    small_part = jnp.concatenate([six, last[:, :, None], jnp.zeros((2, 16, 9, 128), f32)], 2)
    output, input_grad, query_grad, keyval_grad, out_grad, small_grad = kernel_call(
        finish, "finish", 4,
        [out_rows, in_rows.astype(bf16), query_part, keyval_part, out_part, small_part],
        [ANY] * 6,
        [((2, 4, 96, 2048), bf16), ((2, 4, 96, 2048), bf16), ((128, 256), f32), ((128, 256), f32),
         ((256, 128), f32), ((16, 128), f32)],
        [ANY, ANY, VM, VM, VM, VM],
        [pltpu.VMEM((16, 128), f32), pltpu.VMEM((3, 16, 128), f32), pltpu.VMEM((64, 256), f32)]
        + rs2d_bufs((128, 256)) + rs2d_bufs((64, 256)) + rs2d_bufs((256, 128))
        + rs2d_bufs((16, 128), f32) + sems(224, 72),
    )
    return (
        output.reshape(768, 2048),
        input_grad.reshape(768, 2048).astype(f32),
        small_grad[0],
        small_grad[1],
        query_grad,
        small_grad[6, :16].reshape(2, 8),
        keyval_grad,
        small_grad[6, 80:88],
        out_grad,
        small_grad[2],
        small_grad[3],
        small_grad[4],
        up_grad,
        small_grad[6, 16:80].reshape(8, 8),
        down_grad,
        small_grad[5],
    )


def solution(mesh):
    return jax.shard_map(
        body,
        mesh=mesh,
        in_specs=(
            P("dp", None), P("dp", None), P(), P("dp"), P("dp"), P("dp", "tensor"),
            P("tensor", "dp"), P("dp", None), P("dp"), P("tensor", "dp"), P("dp"), P("dp"),
            P("dp"), P("dp", "tensor"), P("tensor", "dp"), P("tensor", "dp"), P("dp"),
        ),
        out_specs=(
            P("dp", None), P("dp", None), P("dp"), P("dp"), P("dp", "tensor"),
            P("tensor", "dp"), P("dp", None), P("dp"), P("tensor", "dp"), P("dp"), P("dp"),
            P("dp"), P("dp", "tensor"), P("tensor", "dp"), P("tensor", "dp"), P("dp"),
        ),
        check_vma=False,
    )
```

```python
import functools
import math

import jax
import jax.numpy as jnp
from jax import lax
from jax.experimental import pallas as pl
from jax.experimental.pallas import tpu as pltpu
from jax.sharding import PartitionSpec as P

HD = 128
EPS = 1e-05
NEG = -1e30
MESH = pl.DeviceIdType.MESH
bf16 = jnp.bfloat16
f32 = jnp.float32


class Place:
    def __init__(self):
        dp = lax.axis_index("dp")
        tensor = lax.axis_index("tensor")
        self.core = dp % 2
        self.x = (dp // 2) % 4
        self.y = (tensor // 4) * 2 + dp // 8
        self.z = tensor % 4

    def dev(self, x=None, y=None, z=None, core=None):
        x = self.x if x is None else x
        y = self.y if y is None else y
        z = self.z if z is None else z
        core = self.core if core is None else core
        return ((y % 2) * 8 + x * 2 + core, (y // 2) * 4 + z)

    def sibling(self):
        return self.dev(core=1 - self.core)

    def ring(self, axis):
        return Ring(self, axis)


class Ring:
    def __init__(self, place, axis):
        self.p = getattr(place, axis)
        self.plus = place.dev(**{axis: (self.p + 1) % 4})
        self.minus = place.dev(**{axis: (self.p + 3) % 4})
        self.after = (self.p + 1) % 4
        self.before = (self.p + 3) % 4
        self.across = (self.p + 2) % 4
        self.others = [place.dev(**{axis: self.across}), self.plus, self.minus]
        self.sources = [self.across, self.before, self.after]


class Net:
    def __init__(self, ssem, rsem, lsem):
        self.ssem, self.rsem, self.lsem = ssem, rsem, lsem
        self.n = 0
        self.m = 0
        self.sent = []
        self.group = 0
        self.todo = {}

    def send(self, src, dst, dev):
        i = self.n
        self.n += 1
        copy = pltpu.make_async_remote_copy(
            src_ref=src,
            dst_ref=dst,
            send_sem=self.ssem.at[i],
            recv_sem=self.rsem.at[i],
            device_id=dev,
            device_id_type=MESH,
        )
        copy.start()
        self.sent.append(copy)
        return copy

    def local(self, src, dst):
        i = self.m
        self.m += 1
        copy = pltpu.make_async_copy(src, dst, self.lsem.at[i])
        copy.start()
        return copy

    def spawn(self, gen):
        place = self.todo.setdefault(self.group, [])
        place.append(gen)
        self.step(gen, place)

    def begin(self, gen, group=0):
        state = [False]

        def whole():
            yield from gen
            state[0] = True

        self.group = group
        self.spawn(whole())
        return state

    def step(self, gen, place):
        try:
            next(gen)
        except StopIteration:
            place.remove(gen)

    def pump(self, *groups):
        for group in groups:
            self.group = group
            place = self.todo.setdefault(group, [])
            for gen in list(place):
                self.step(gen, place)

    def until(self, *states):
        for group, state in states:
            while not state[0]:
                self.pump(group)

    def run(self, *gens):
        for gen in gens:
            self.spawn(gen)
        while any(self.todo.values()):
            self.pump(*self.todo)
        for copy in self.sent:
            copy.wait_send()


def greet(devices):
    barrier = pltpu.get_barrier_semaphore()
    for device in devices:
        pl.semaphore_signal(barrier, inc=1, device_id=device, device_id_type=MESH)
    pl.semaphore_wait(barrier, len(devices))


def rows_half(ref, which):
    n = ref.shape[-2] // 2
    if len(ref.shape) == 2:
        return ref.at[pl.ds(which * n, n), :]
    return ref.at[:, pl.ds(which * n, n), :]


def lane_step(shape):
    return max(16, min(shape[0], 32768 // shape[1]))


def over_rows(rows, step, fn):
    def one(i, carry):
        fn(pl.ds(pl.multiple_of(i * step, step), step))
        return carry

    lax.fori_loop(0, rows // step, one, 0)


def add_into(dst, *srcs, out=None):
    out = dst if out is None else out
    rows, step = dst.shape[0], lane_step(dst.shape)
    if rows % step:
        step = 16 if rows % 16 == 0 else rows

    def one(at):
        total = dst[at, :].astype(f32)
        for src in srcs:
            total = total + src[at, :].astype(f32)
        out[at, :] = total.astype(out.dtype)

    over_rows(rows, step, one)


def ag_ring(net, ring, slot, own, have=None, half=rows_half):
    have = have or (lambda pos: None)
    c0 = net.send(own, slot(ring.p), ring.plus)
    c1 = net.send(own, slot(ring.p), ring.minus)
    yield
    c0.wait_recv()
    one = half(slot(ring.before), 0)
    c2 = net.send(one, one, ring.plus)
    have(ring.before)
    c1.wait_recv()
    two = half(slot(ring.after), 1)
    c3 = net.send(two, two, ring.minus)
    have(ring.after)
    yield
    c2.wait_recv()
    c3.wait_recv()
    have(ring.across)


def ag2d(net, place, own, slot, first, second):
    sib = place.sibling()
    pairs = []

    def give(a, b, src=None):
        ref = slot(a, b)
        pairs.append(net.send(ref if src is None else src, ref, sib))

    def column(a, src):
        return ag_ring(net, second, lambda b: slot(a, b), src, lambda b: give(a, b))

    def main():
        keep = net.local(own, slot(first.p, second.p))
        c0 = net.send(own, slot(first.p, second.p), first.plus)
        c1 = net.send(own, slot(first.p, second.p), first.minus)
        yield
        net.spawn(column(first.p, own))
        give(first.p, second.p, own)
        c0.wait_recv()
        one = rows_half(slot(first.before, second.p), 0)
        c2 = net.send(one, one, first.plus)
        net.spawn(column(first.before, slot(first.before, second.p)))
        c1.wait_recv()
        two = rows_half(slot(first.after, second.p), 1)
        c3 = net.send(two, two, first.minus)
        net.spawn(column(first.after, slot(first.after, second.p)))
        give(first.before, second.p)
        give(first.after, second.p)
        yield
        c2.wait_recv()
        c3.wait_recv()
        net.spawn(column(first.across, slot(first.across, second.p)))
        give(first.across, second.p)
        keep.wait()
        while len(pairs) < 16:
            yield
        for pair in pairs:
            pair.wait_recv()

    return main()


def ag2d_direct(net, place, own, slot, first, second):
    sib = place.sibling()
    pairs = []

    def give(a, b, src=None):
        ref = slot(a, b)
        pairs.append(net.send(ref if src is None else src, ref, sib))

    def column(a, src):
        return [net.send(src, slot(a, second.p), dev) for dev in second.others]

    keep = net.local(own, slot(first.p, second.p))
    rows = [net.send(own, slot(first.p, second.p), dev) for dev in first.others]
    columns = [(first.p, column(first.p, own))]
    give(first.p, second.p, own)
    yield
    for a, copy in zip(first.sources, rows):
        copy.wait_recv()
        columns.append((a, column(a, slot(a, second.p))))
        give(a, second.p)
    yield
    for a, copies in columns:
        for b, copy in zip(second.sources, copies):
            copy.wait_recv()
            give(a, b)
    yield
    keep.wait()
    for pair in pairs:
        pair.wait_recv()


def rs_ring(net, ring, src, ra, rb, done):
    across, after, before = src(ring.across), src(ring.after), src(ring.before)
    a0 = net.send(rows_half(across, 0), ra(0), ring.plus)
    a1 = net.send(rows_half(across, 1), ra(1), ring.minus)
    b0 = net.send(rows_half(after, 1), rows_half(rb(0), 1), ring.plus)
    b1 = net.send(rows_half(before, 0), rows_half(rb(1), 0), ring.minus)
    yield
    a0.wait_recv()
    add_into(ra(0), rows_half(after, 0))
    b2 = net.send(ra(0), rows_half(rb(0), 0), ring.plus)
    a1.wait_recv()
    add_into(ra(1), rows_half(before, 1))
    b3 = net.send(ra(1), rows_half(rb(1), 1), ring.minus)
    yield
    for copy in (b0, b1, b2, b3):
        copy.wait_recv()
    done(src(ring.p), rb(0), rb(1))


def rs2d(net, place, part, first, second, bufs, out):
    r0, rv, ra, rb, r1, sa, sb = bufs
    sib = place.sibling()
    firsts = (first.across, first.after, first.before, first.p)
    seconds = (second.across, second.after, second.before, second.p)
    come, keep = {}, {}
    for i, a in enumerate(firsts):
        for j, b in enumerate(seconds):
            come[i, j] = net.send(part(a, b, 1 - place.core), rv.at[i, j], sib)
            keep[i, j] = net.local(part(a, b, place.core), r0.at[i, j])

    def pair(i, j):
        come[i, j].wait_recv()
        keep[i, j].wait()
        add_into(r0.at[i, j], rv.at[i, j])

    yield
    halves, wholes = {}, {}
    for j in range(4):
        pair(0, j)
        halves[0, j] = net.send(rows_half(r0.at[0, j], 0), ra.at[0, j], first.plus)
        halves[1, j] = net.send(rows_half(r0.at[0, j], 1), ra.at[1, j], first.minus)
    yield
    for j in range(4):
        pair(1, j)
        wholes[0, j] = net.send(rows_half(r0.at[1, j], 1), rows_half(rb.at[0, j], 1), first.plus)
        pair(2, j)
        wholes[1, j] = net.send(rows_half(r0.at[2, j], 0), rows_half(rb.at[1, j], 0), first.minus)
    yield
    for j in range(4):
        halves[0, j].wait_recv()
        add_into(ra.at[0, j], rows_half(r0.at[1, j], 0))
        wholes[2, j] = net.send(ra.at[0, j], rows_half(rb.at[0, j], 0), first.plus)
        halves[1, j].wait_recv()
        add_into(ra.at[1, j], rows_half(r0.at[2, j], 1))
        wholes[3, j] = net.send(ra.at[1, j], rows_half(rb.at[1, j], 1), first.minus)
        pair(3, j)
    yield

    def settle(j):
        for k in range(4):
            wholes[k, j].wait_recv()
        add_into(r0.at[3, j], rb.at[0, j], rb.at[1, j], out=r1.at[j])

    settle(0)
    a0 = net.send(rows_half(r1.at[0], 0), sa.at[0], second.plus)
    a1 = net.send(rows_half(r1.at[0], 1), sa.at[1], second.minus)
    settle(1)
    b0 = net.send(rows_half(r1.at[1], 1), rows_half(sb.at[0], 1), second.plus)
    settle(2)
    b1 = net.send(rows_half(r1.at[2], 0), rows_half(sb.at[1], 0), second.minus)
    settle(3)
    yield
    a0.wait_recv()
    add_into(sa.at[0], rows_half(r1.at[1], 0))
    b2 = net.send(sa.at[0], rows_half(sb.at[0], 0), second.plus)
    a1.wait_recv()
    add_into(sa.at[1], rows_half(r1.at[2], 1))
    b3 = net.send(sa.at[1], rows_half(sb.at[1], 1), second.minus)
    yield
    for copy in (b0, b1, b2, b3):
        copy.wait_recv()
    add_into(r1.at[3], sb.at[0], sb.at[1], out=out)


def rs2d_bufs(shape, dtype=bf16):
    rows, cols = shape
    half = (rows // 2, cols)
    return [
        pltpu.VMEM((4, 4) + shape, dtype),
        pltpu.VMEM((4, 4) + shape, dtype),
        pltpu.VMEM((2, 4) + half, dtype),
        pltpu.VMEM((2, 4) + shape, dtype),
        pltpu.VMEM((4,) + shape, dtype),
        pltpu.VMEM((2,) + half, dtype),
        pltpu.VMEM((2,) + shape, dtype),
    ]


def sems(count, local):
    return [
        pltpu.SemaphoreType.DMA((count,)),
        pltpu.SemaphoreType.DMA((count,)),
        pltpu.SemaphoreType.DMA((local,)),
    ]


ANY = pl.BlockSpec(memory_space=pl.ANY)
VM = pl.BlockSpec(memory_space=pltpu.VMEM)


def kernel_call(body, name, cid, ins, in_specs, outs, out_specs, scratch, nbytes=1 << 20):
    return pl.pallas_call(
        body,
        out_shape=[jax.ShapeDtypeStruct(s, d) for s, d in outs],
        in_specs=in_specs,
        out_specs=out_specs,
        scratch_shapes=scratch,
        compiler_params=pltpu.CompilerParams(
            collective_id=cid, has_side_effects=True, vmem_limit_bytes=56 << 20
        ),
        cost_estimate=pl.CostEstimate(flops=0, bytes_accessed=nbytes, transcendentals=0),
        name=name,
    )(*ins)


def block_of(x, y, core):
    return (y % 2) * 8 + x * 2 + core


def col_at(d):
    return pl.ds(pl.multiple_of(d * 128, 128), 128)


def row_at(start, size):
    return pl.ds(pl.multiple_of(start, size), size)


def at_query(ref, x, y, core):
    return ref.at[row_at(block_of(x, y, core) * 128, 128), row_at((y // 2) * 256, 256)]


def at_keyval(ref, x, y, core):
    return ref.at[row_at(block_of(x, y, core) * 128 + (y // 2) * 64, 64), :]


def at_out(ref, x, y, core):
    return ref.at[row_at((y // 2) * 256, 256), col_at(block_of(x, y, core))]


def at_up(ref, x, y, core):
    return ref.at[row_at(block_of(x, y, core) * 128, 128), row_at((y // 2) * 1024, 1024)]


def at_down(ref, x, y, core):
    return ref.at[row_at((y // 2) * 1024, 1024), col_at(block_of(x, y, core))]


def at_small(ref, x, y, core):
    return ref.at[y // 2, block_of(x, y, core)]


def gather(net, place, at, own, whole, order, how=ag2d):
    x, y = place.ring("x"), place.ring("y")
    if order == "xy":
        return how(net, place, own, lambda a, b: at(whole, a, b, place.core), x, y)
    return how(net, place, own, lambda a, b: at(whole, b, a, place.core), y, x)


def scatter(net, place, at, part, order, bufs, out):
    x, y = place.ring("x"), place.ring("y")
    if order == "xy":
        return rs2d(net, place, lambda a, b, c: at(part, a, b, c), x, y, bufs, out)
    return rs2d(net, place, lambda a, b, c: at(part, b, a, c), y, x, bufs, out)


def plane_peers(place):
    x, y = place.ring("x"), place.ring("y")
    return [place.sibling(), x.plus, x.minus, y.plus, y.minus]


def spread(values):
    center = values - jnp.mean(values, axis=-1, keepdims=True)
    return center, lax.rsqrt(jnp.mean(center * center, axis=-1, keepdims=True) + EPS)


def cast_into(dst, src):
    step = lane_step(dst.shape)
    step = step if dst.shape[0] % step == 0 else 16

    def one(at):
        dst[at, :] = src[at, :].astype(dst.dtype)

    over_rows(dst.shape[0], step, one)


def front(
    tokens, key_seg, query_seg, small_own, query_w, keyval_w, out_w, up_w, down_w,
    o_query_w, o_keyval_w, o_out_w, g_up, g_down, vecs, o_normed, o_query, o_window, o_lse,
    o_attended, normed_two, middle,
    g_query, g_keyval, g_out, g_small, tok, normed, query, window, take, lse, attended, bias,
    f_query, f_keyval, f_out, f_up, f_down, b_query, b_keyval, b_out, b_up, b_down,
    unit, scores, weights, mixed, part, ra, rb, mine, *sem,
):
    place = Place()
    z = place.ring("z")
    hi = place.y // 2
    block = ((place.y % 2) * 8 + place.x * 2 + place.core) * 2 + hi
    earlier = [device_of_block(place, (block + 32 - k) % 32) for k in (1, 2, 3, 4)]
    later = [device_of_block(place, (block + k) % 32) for k in (1, 2, 3, 4)]
    net = Net(*sem)
    half_rows = pl.ds(pl.multiple_of(hi * 64, 64), 64)
    loads = [
        net.local(keyval_w.at[half_rows, :], f_keyval),
        net.local(query_w, f_query),
        net.local(out_w, f_out),
        net.local(tokens.at[pl.ds(pl.multiple_of(hi * 384, 384), 384), :], tok),
        net.local(up_w, f_up),
        net.local(down_w, f_down),
    ]
    x, y = place.ring("x"), place.ring("y")
    greet([place.sibling()] + x.others + y.others + z.others + earlier + later)
    s_small = net.begin(gather(net, place, at_small, small_own, g_small, "yx", ag2d_direct), 1)
    loads[0].wait()
    cast_into(b_keyval, f_keyval)
    s_keyval = net.begin(gather(net, place, at_keyval, b_keyval, g_keyval, "xy", ag2d_direct), 1)
    loads[3].wait()

    def norm_some(at):
        center, inv = spread(tok[at, :].astype(f32))
        unit[at, :] = center * inv

    over_rows(96, 16, lambda at: norm_some(pl.ds(pl.multiple_of(at.start + place.z * 96, 16), 16)))
    net.pump(1)
    loads[1].wait()
    cast_into(b_query, f_query)
    loads[2].wait()
    cast_into(b_out, f_out)
    loads[4].wait()
    cast_into(b_up, f_up)
    loads[5].wait()
    cast_into(b_down, f_down)
    s_up = net.begin(gather(net, place, at_up, b_up, g_up, "xy"), 3)
    s_down = net.begin(gather(net, place, at_down, b_down, g_down, "yx"), 3)
    net.pump(1)
    net.until((1, s_small), (1, s_keyval))

    for d in range(16):
        vecs[0:6, d * 128 : (d + 1) * 128] = g_small[0, d, 0:6, :]
    lane = lax.broadcasted_iota(jnp.int32, (8, 128), 1)

    def collect(which, rows):
        total = jnp.zeros((8, 128), f32)
        for d in range(16):
            piece = jnp.where(lane < 8, g_small[which, d, rows : rows + 8, :], 0.0)
            total = total + (pltpu.roll(piece, d * 8, 1) if d else piece)
        return total

    biases = []
    for which in range(2):
        ups = collect(which, 8)
        for r in range(8):
            at = which * 1024 + r * 128
            vecs[6:7, at : at + 128] = ups[r : r + 1, :]
        biases.append(collect(which, 0))
    query_b = [biases[0][6:7], biases[0][7:8], biases[1][6:7], biases[1][7:8]]
    value_b = jnp.zeros((8, 128), f32)
    for d in range(16):
        piece = jnp.where((lane >= 8) & (lane < 16), g_small[0, d, 0:8, :], 0.0)
        shift = (d * 8 + 120) % 128
        value_b = value_b + (pltpu.roll(piece, shift, 1) if shift else piece)
    value_b = value_b[6:7]

    def apply_some(at):
        normed[at, :] = (unit[at, :] * vecs[0:1, :] + vecs[1:2, :]).astype(bf16)

    over_rows(96, 16, lambda at: apply_some(pl.ds(pl.multiple_of(at.start + place.z * 96, 16), 16)))
    quarter = pl.ds(pl.multiple_of(place.z * 96, 96), 96)
    kv = jnp.dot(normed[quarter, :], g_keyval[...], preferred_element_type=f32)
    window[4, place.z] = (kv + jnp.concatenate([jnp.zeros((1, 128), f32), value_b], 1)).astype(bf16)

    def keys_values():
        own = window.at[4, place.z]
        sent = [net.send(own, window.at[4 - k, place.z], later[k - 1]) for k in (1, 2, 3, 4)]
        yield
        for copy in sent:
            copy.wait_recv()
        mine = window.at[:, place.z]
        sent = [net.send(mine, mine, dev) for dev in z.others]
        yield
        for copy in sent:
            copy.wait_recv()

    s_window = net.begin(keys_values(), 1)
    s_query = net.begin(gather(net, place, at_query, b_query, g_query, "xy", ag2d_direct), 2)
    s_out = net.begin(gather(net, place, at_out, b_out, g_out, "yx", ag2d_direct), 2)
    over_rows(192, 16, norm_some)
    net.pump(1)
    over_rows(192, 16, lambda at: norm_some(pl.ds(pl.multiple_of(at.start + 192, 16), 16)))
    net.pump(2)
    net.pump(3)
    over_rows(384, 16, apply_some)
    row = lax.broadcasted_iota(jnp.int32, (96, 1632), 0)
    column = lax.broadcasted_iota(jnp.int32, (96, 1632), 1)
    for i in range(4):
        same = query_seg[i * 96 : (i + 1) * 96, :] == key_seg[i : i + 1, :]
        bias[i] = jnp.where(same & (column <= row + 1536), 0.0, NEG)
    net.until((1, s_window))
    net.until((2, s_query))
    for i in range(4):
        rows = jnp.dot(normed[i * 96 : (i + 1) * 96, :], g_query[...], preferred_element_type=f32)
        for h in range(4):
            query[i, h * 96 : (h + 1) * 96, :] = (
                rows[:, h * 128 : (h + 1) * 128] + query_b[h]
            ).astype(bf16)
    net.until((1, s_window), (2, s_out))
    keeps = [
        net.local(*pair)
        for pair in (
            (g_query, o_query_w), (g_keyval, o_keyval_w), (g_out, o_out_w), (normed, o_normed),
            (query, o_query), (window, o_window),
        )
    ]
    for j in range(5):
        for i in range(4):
            take[pl.ds((j * 4 + i) * 96, 96), :] = window[j, i]
    scale = 1.0 / math.sqrt(HD)

    def attend(i):
        reach = pl.ds(pl.multiple_of(i * 96, 32), 1632)
        scores[...] = lax.dot_general(
            query[i], take[reach, 0:128], (((1,), (1,)), ((), ())), preferred_element_type=f32
        )

        def soften(c, carry):
            at = pl.ds(pl.multiple_of(c * 16, 16), 16)
            mask = pl.ds(pl.multiple_of((c % 6) * 16, 16), 16)
            some = scores[at, :] * scale + bias[i, mask, :]
            top = jnp.max(some, axis=-1, keepdims=True)
            some = jnp.exp(some - top)
            total = jnp.sum(some, axis=-1, keepdims=True)
            weights[at, :] = (some * (1.0 / total)).astype(bf16)
            lse[i, at, :] = jnp.broadcast_to(top + jnp.log(total), (16, 128))
            return carry

        lax.fori_loop(0, 24, soften, 0, unroll=4)
        mixed[...] = jnp.dot(
            weights[...], take[reach, 128:256], preferred_element_type=f32
        ).astype(bf16)
        for h in range(4):
            attended[i, :, h * 128 : (h + 1) * 128] = mixed[h * 96 : (h + 1) * 96, :]
        for n in range(4):
            columns = slice(n * 512, (n + 1) * 512)
            part[i, :, columns] = jnp.dot(
                attended[i], g_out[:, columns], preferred_element_type=f32
            ).astype(bf16)

    attend(z.across)
    a0 = net.send(rows_half(part.at[z.across], 0), ra.at[0], z.plus)
    a1 = net.send(rows_half(part.at[z.across], 1), ra.at[1], z.minus)
    attend(z.after)
    after = part.at[z.after]
    b0 = net.send(rows_half(after, 1), rows_half(rb.at[0], 1), z.plus)
    a0.wait_recv()
    add_into(ra.at[0], rows_half(after, 0))
    b1 = net.send(ra.at[0], rows_half(rb.at[0], 0), z.plus)
    net.pump(3)
    attend(z.before)
    before = part.at[z.before]
    b2 = net.send(rows_half(before, 0), rows_half(rb.at[1], 0), z.minus)
    a1.wait_recv()
    add_into(ra.at[1], rows_half(before, 1))
    b3 = net.send(ra.at[1], rows_half(rb.at[1], 1), z.minus)
    attend(z.p)
    keeps += [net.local(attended, o_attended), net.local(lse, o_lse)]
    for copy in (b0, b1, b2, b3):
        copy.wait_recv()

    def residual(at):
        mid = (
            tok[pl.ds(pl.multiple_of(place.z * 96 + at.start, 16), 16), :].astype(f32)
            + part[place.z, at, :].astype(f32)
            + rb[0, at, :].astype(f32)
            + rb[1, at, :].astype(f32)
            + vecs[2:3, :]
        )
        middle[at, :] = mid
        center, inv = spread(mid)
        mine[at, :] = (center * inv * vecs[3:4, :] + vecs[4:5, :]).astype(bf16)

    over_rows(96, 16, residual)
    keeps.append(net.local(mine, normed_two.at[z.p]))
    s_normed = net.begin(ag_ring(net, z, lambda i: normed_two.at[i], mine), 1)
    net.run()
    for keep in keeps:
        keep.wait()


def mlp_back(
    part_out, part_norm, middle, cot, vecs, part_up, part_down,
    out_rows, grad_mid, grad_all, sums, up_grad, down_grad,
    ra, rb, rc, rd, mine, *rest,
):
    place = Place()
    z = place.ring("z")
    greet(plane_peers(place) + [z.plus, z.minus])
    ups, downs, sem = rest[:7], rest[7:14], rest[14:]
    net = Net(*sem)

    def back():
        def done(own, one, two):
            sums[...] = jnp.zeros_like(sums)

            def some(at):
                grad = own[at, :].astype(f32) + one[at, :].astype(f32) + two[at, :].astype(f32)
                center, inv = spread(middle[at, :])
                norm = center * inv
                flow = grad * vecs[1:2, :]
                top = cot[at, :].astype(f32)
                mid = top + inv * (
                    flow
                    - jnp.mean(flow, axis=-1, keepdims=True)
                    - norm * jnp.mean(flow * norm, axis=-1, keepdims=True)
                )
                grad_mid[at, :] = mid
                low = mid.astype(bf16)
                mine[at, :] = low
                sums[0:1, :] += jnp.sum(grad * norm, axis=0, keepdims=True)
                sums[1:2, :] += jnp.sum(grad, axis=0, keepdims=True)
                sums[2:3, :] += jnp.sum(low.astype(f32), axis=0, keepdims=True)
                sums[3:4, :] += jnp.sum(top, axis=0, keepdims=True)

            over_rows(96, 16, some)

        yield from rs_ring(
            net, z, lambda i: part_norm.at[i], lambda i: ra.at[i], lambda i: rb.at[i], done
        )
        keep = net.local(mine, grad_all.at[z.p])
        yield from ag_ring(net, z, lambda i: grad_all.at[i], mine)
        keep.wait()

    def fore():
        def done(own, one, two):
            def some(at):
                out_rows[at, :] = (
                    middle[at, :]
                    + own[at, :].astype(f32)
                    + one[at, :].astype(f32)
                    + two[at, :].astype(f32)
                    + vecs[0:1, :]
                ).astype(bf16)

            over_rows(96, 16, some)

        yield
        yield from rs_ring(
            net, z, lambda i: part_out.at[i], lambda i: rc.at[i], lambda i: rd.at[i], done
        )

    net.run(
        back(),
        scatter(net, place, at_up, part_up, "yx", ups, up_grad),
        scatter(net, place, at_down, part_down, "xy", downs, down_grad),
        fore(),
    )


def device_of_block(place, block):
    d = block // 2
    return ((d // 8) * 8 + ((d // 2) % 4) * 2 + d % 2, (block % 2) * 4 + place.z)


def lanes_half(ref, which):
    n = ref.shape[-1] // 2
    return ref.at[:, pl.ds(which * n, n)]


def tail(
    grad_all, attended_all, query_all, window_all, lse_all, normed_all, query_w, keyval_w, out_w,
    tokens, out_rows, low, grad_mid, vecs, sums, up_sum,
    output, input_grad, query_grad, keyval_grad, out_grad, small_grad,
    grad, attended, query, window, lse, normed, w_query, w_keyval, w_out, tok,
    part_out, part_query, part_keyval, flow, scores, change, probs, slopes, d_keys, d_values,
    grad_query, part, ra, rb, pieces, rk, stage, rz, kv_grad, mine, six, tiles, part_small,
    small_own, small_in, kv_own, *rest,
):
    place = Place()
    x, y, z = place.ring("x"), place.ring("y"), place.ring("z")
    hi = place.y // 2
    partner = y.others[0]
    block = ((place.y % 2) * 8 + place.x * 2 + place.core) * 2 + hi
    earlier = [device_of_block(place, (block + 32 - k) % 32) for k in (1, 2, 3, 4)]
    later = [device_of_block(place, (block + k) % 32) for k in (1, 2, 3, 4)]
    queries, keyvals, outs, smalls, sem = (
        rest[:7], rest[7:14], rest[14:21], rest[21:28], rest[28:],
    )
    net = Net(*sem)
    token_rows = pl.ds(pl.multiple_of(hi * 384 + place.z * 96, 96), 96)
    loads = {
        name: net.local(*pair)
        for name, pair in dict(
            grad=(grad_all, grad), attended=(attended_all, attended), out=(out_w, w_out),
            query=(query_all, query), window=(window_all, window), lse=(lse_all, lse),
            query_w=(query_w, w_query), normed=(normed_all, normed), keyval=(keyval_w, w_keyval),
            tok=(tokens.at[token_rows, :], tok),
        ).items()
    }
    greet([place.sibling()] + x.others + y.others + z.others + earlier + later)

    def y_first(own, slot, half):
        keep = net.local(own, slot(hi, z.p))
        swap = net.send(own, slot(hi, z.p), partner)
        net.spawn(ag_ring(net, z, lambda i: slot(hi, i), own, half=half))
        yield
        swap.wait_recv()
        net.spawn(ag_ring(net, z, lambda i: slot(1 - hi, i), slot(1 - hi, z.p), half=half))
        keep.wait()

    def z_first(own, slot, half):
        keep = net.local(own, slot(hi, z.p))
        swaps = [net.send(own, slot(hi, z.p), partner)]

        def have(i):
            swaps.append(net.send(slot(hi, i), slot(hi, i), partner))

        yield from ag_ring(net, z, lambda i: slot(hi, i), own, have, half)
        yield
        keep.wait()
        for swap in swaps:
            swap.wait_recv()

    loads["grad"].wait()
    loads["attended"].wait()
    for n in range(4):
        columns = slice(n * 512, (n + 1) * 512)
        part_out[:, columns] = contract_rows(attended[...], grad[:, columns]).astype(bf16)
    net.begin(scatter(net, place, at_out, part_out, "yx", outs, out_grad), 2)
    net.begin(y_first(out_rows, lambda a, b: output.at[a, b], rows_half), 4)
    loads["out"].wait()
    whole = contract_cols(grad[...], w_out[...]).astype(bf16)
    for i in range(4):
        for h in range(4):
            flow[i, h * 96 : (h + 1) * 96, :] = whole[
                i * 96 : (i + 1) * 96, h * 128 : (h + 1) * 128
            ]
    d_keys[...] = jnp.zeros_like(d_keys)
    d_values[...] = jnp.zeros_like(d_values)
    for name in ("query", "window", "lse", "query_w"):
        loads[name].wait()
    scale = 1.0 / math.sqrt(HD)
    lane = lax.broadcasted_iota(jnp.int32, (384, 128), 1)
    last = 1536 + lax.broadcasted_iota(jnp.int32, (32, 384), 1) % 96
    key = lax.broadcasted_iota(jnp.int32, (32, 384), 0)

    def attend(i):
        reach = pl.ds(pl.multiple_of(i * 96, 32), 1632)
        rows = pl.ds(pl.multiple_of(i * 96, 32), 96)
        for h in range(4):
            at = pl.ds(h * 96, 96)
            product = flow[i, at, :].astype(f32) * attended[
                rows, h * 128 : (h + 1) * 128
            ].astype(f32)
            lse[i, at, :] = jnp.where(
                lane[:96] == 0, lse[i, at, :], jnp.sum(product, axis=-1, keepdims=True)
            )
        across = jnp.transpose(lse[i])
        total, delta = across[0:1, :], across[1:2, :]
        first = low[pl.ds(i, 1), :]
        scores[...] = contract_cols(window[reach, 0:128], query[i])
        change[...] = contract_cols(window[reach, 128:256], flow[i])

        def soften(c, carry):
            at = pl.ds(pl.multiple_of(c * 32, 32), 32)
            where = key + c * 32
            some = jnp.where(
                (where >= first) & (where <= last), scores[at, :] * scale - total, NEG
            )
            some = jnp.exp(some)
            probs[at, :] = some.astype(bf16)
            slopes[at, :] = (some * (change[at, :] - delta)).astype(bf16)
            return carry

        lax.fori_loop(0, 51, soften, 0, unroll=3)
        d_values[reach, :] += matmul(probs[...], flow[i])
        d_keys[reach, :] += matmul(slopes[...], query[i])
        turned = jnp.transpose(contract_rows(window[reach, 0:128], slopes[...])) * scale
        for h in range(4):
            grad_query[rows, h * 128 : (h + 1) * 128] = turned[h * 96 : (h + 1) * 96].astype(bf16)
        for n in range(4):
            columns = slice(n * 512, (n + 1) * 512)
            part[i, :, columns] = contract_cols(grad_query[rows, :], w_query[columns, :]).astype(bf16)

    attend(z.across)
    a0 = net.send(rows_half(part.at[z.across], 0), ra.at[0], z.plus)
    a1 = net.send(rows_half(part.at[z.across], 1), ra.at[1], z.minus)
    net.pump(2)
    attend(z.after)
    after = part.at[z.after]
    b0 = net.send(rows_half(after, 1), rows_half(rb.at[0], 1), z.plus)
    a0.wait_recv()
    add_into(ra.at[0], rows_half(after, 0))
    b1 = net.send(ra.at[0], rows_half(rb.at[0], 0), z.plus)
    net.pump(2, 4)
    attend(z.before)
    before = part.at[z.before]
    b2 = net.send(rows_half(before, 0), rows_half(rb.at[1], 0), z.minus)
    a1.wait_recv()
    add_into(ra.at[1], rows_half(before, 1))
    b3 = net.send(ra.at[1], rows_half(rb.at[1], 1), z.minus)
    net.pump(2, 4)
    attend(z.p)
    for j in range(5):
        at = slice(j * 384, (j + 1) * 384)
        pieces[j, :, 0:128] = (d_keys[at, :] * scale).astype(bf16)
        pieces[j, :, 128:256] = d_values[at, :].astype(bf16)

    def keys_values():
        sent = [net.send(pieces.at[4 - k], rk.at[k - 1], earlier[k - 1]) for k in (1, 2, 3, 4)]
        yield
        for copy in sent:
            copy.wait_recv()
        for i in range(4):
            at = pl.ds(i * 96, 96)
            add_into(pieces.at[4, at], *[rk.at[k, at] for k in range(4)], out=stage.at[i])
        sent = [
            net.send(stage.at[pos], rz.at[k], dev)
            for k, (pos, dev) in enumerate(zip((z.across, z.after, z.before), z.others))
        ]
        yield
        for copy in sent:
            copy.wait_recv()
        home = kv_grad.at[pl.ds(pl.multiple_of(place.z * 96, 96), 96), :]
        add_into(stage.at[place.z], *[rz.at[k] for k in range(3)], out=home)
        sent = [net.send(home, home, dev) for dev in z.others]
        state_rows[0] = True
        yield
        for copy in sent:
            copy.wait_recv()

    state_rows = [False]
    s_kv = net.begin(keys_values(), 1)
    loads["normed"].wait()
    for n in range(4):
        rows = slice(n * 512, (n + 1) * 512)
        part_query[rows, :] = contract_rows(normed[:, rows], grad_query[...]).astype(bf16)
    net.begin(scatter(net, place, at_query, part_query, "xy", queries, query_grad), 3)
    net.pump(2, 4)
    loads["keyval"].wait()
    loads["tok"].wait()
    net.until((1, state_rows))
    for copy in (b0, b1, b2, b3):
        copy.wait_recv()
    six[...] = jnp.zeros_like(six)

    def norm_back(at):
        grad_norm = (
            part[place.z, at, :].astype(f32)
            + rb[0, at, :].astype(f32)
            + rb[1, at, :].astype(f32)
            + contract_cols(
                kv_grad[pl.ds(pl.multiple_of(place.z * 96 + at.start, 16), at.size), :],
                w_keyval[...],
            )
        )
        center, inv = spread(tok[at, :].astype(f32))
        norm = center * inv
        down = grad_norm * vecs[0:1, :]
        mine[at, :] = (
            grad_mid[at, :]
            + inv
            * (
                down
                - jnp.mean(down, axis=-1, keepdims=True)
                - norm * jnp.mean(down * norm, axis=-1, keepdims=True)
            )
        ).astype(bf16)
        six[0:1, :] += jnp.sum(grad_norm * norm, axis=0, keepdims=True)
        six[1:2, :] += jnp.sum(grad_norm, axis=0, keepdims=True)

    for i in range(2):
        norm_back(pl.ds(i * 48, 48))
    top, bottom = pl.ds(0, 48), pl.ds(48, 48)
    net.begin(y_first(mine.at[top], lambda a, b: input_grad.at[a, b, top], lanes_half), 5)
    net.begin(z_first(mine.at[bottom], lambda a, b: input_grad.at[a, b, bottom], lanes_half), 5)
    net.until((1, s_kv))
    for n in range(4):
        rows = slice(n * 512, (n + 1) * 512)
        part_keyval[rows, :] = contract_rows(normed[:, rows], kv_grad[...]).astype(bf16)

    def keyval():
        yield from scatter(net, place, at_keyval, part_keyval, "yx", keyvals, kv_own)
        home = keyval_grad.at[pl.ds(pl.multiple_of(hi * 64, 64), 64), :]
        keep = net.local(kv_own, home)
        swap = net.send(kv_own, home, partner)
        yield
        keep.wait()
        swap.wait_recv()

    net.begin(keyval(), 3)
    six[2:3, :] = sums[2:3, :]
    six[3:4, :] = sums[0:1, :]
    six[4:5, :] = sums[1:2, :]
    six[5:6, :] = sums[3:4, :]
    bias_sum = jnp.sum(grad_query[...].astype(f32), axis=0, keepdims=True)
    value_sum = jnp.sum(kv_grad[:, 128:256].astype(f32), axis=0, keepdims=True)
    tiles[...] = jnp.zeros_like(tiles)
    for which in range(2):
        for h in range(2):
            at = (which * 2 + h) * 128
            tiles[which, 6 + h : 7 + h, :] = bias_sum[:, at : at + 128]
        for r in range(8):
            at = which * 1024 + r * 128
            tiles[which, 8 + r : 9 + r, :] = up_sum[0:1, at : at + 128]
    tiles[2, 6:7, :] = value_sum
    lane = lax.broadcasted_iota(jnp.int32, (16, 128), 1)

    def turn(tile, shift):
        shift = shift % 128
        return pltpu.roll(tile, shift, 1) if shift else tile

    for d in range(16):
        values = jnp.where((lane >= 8) & (lane < 16), turn(tiles[2], 136 - d * 8), 0.0)
        for which in range(2):
            piece = jnp.where(lane < 8, turn(tiles[which], 128 - d * 8), values)
            part_small[which, d, 6:16, :] = piece[6:16]
            part_small[which, d, 0:6, :] = six[0:6, d * 128 : (d + 1) * 128]

    def small():
        yield from scatter(net, place, at_small, part_small, "xy", smalls, small_own)
        sent = [net.send(small_own, small_in.at[k], dev) for k, dev in enumerate(z.others)]
        yield
        for copy in sent:
            copy.wait_recv()
        total = small_own[...]
        whole = total + small_in[0] + small_in[1] + small_in[2]
        row = lax.broadcasted_iota(jnp.int32, (16, 128), 0)
        small_grad[...] = jnp.where(row < 6, whole, total)

    net.begin(small(), 3)
    net.run()


def matmul(left, right):
    return jnp.dot(left, right, preferred_element_type=f32)


def contract_rows(left, right):
    return lax.dot_general(left, right, (((0,), (0,)), ((), ())), preferred_element_type=f32)


def contract_cols(left, right):
    return lax.dot_general(left, right, (((1,), (1,)), ((), ())), preferred_element_type=f32)


def gelu_tanh(upward):
    inner = 0.7978845608028654 * (upward + 0.044715 * upward * upward * upward)
    return 0.5 * upward * (1.0 + jnp.tanh(inner))


def body(
    tokens, cotangent, segments, attn_norm_gain, attn_norm_bias, query_weight, query_bias,
    kv_weight, value_bias, out_weight, out_bias, mlp_norm_gain, mlp_norm_bias, up_weight,
    up_bias, down_weight, down_bias,
):
    dp = lax.axis_index("dp")
    tensor = lax.axis_index("tensor")
    hi, z = tensor // 4, tensor % 4
    half, heads = 384, 4

    shorts = jnp.concatenate(
        [jnp.concatenate([query_bias, jnp.stack([value_bias, value_bias])], 1),
         jnp.concatenate([up_bias, up_bias], 1)]
    )
    small = jnp.concatenate(
        [jnp.stack([attn_norm_gain, attn_norm_bias, out_bias, mlp_norm_gain, mlp_norm_bias, down_bias]),
         jnp.pad(shorts, ((0, 0), (0, 112)))]
    ).astype(bf16).astype(f32)
    start = dp * 768 + hi * half
    key_seg = lax.dynamic_slice_in_dim(
        jnp.concatenate([jnp.full((4 * half,), -1, jnp.int32), segments]), start, 5 * half
    )
    query_seg = key_seg[4 * half :]
    mine = hi * half + z * 96
    tok_rows = lax.dynamic_slice_in_dim(tokens, mine, 96)
    cot_rows = lax.dynamic_slice_in_dim(cotangent, mine, 96)
    (
        query_w, keyval_w, out_w, up_w, down_w, vectors, normed_one, query_rows, window, lse,
        attended, normed_two, middle,
    ) = kernel_call(
        front, "front", 0,
        [tokens, jnp.stack([key_seg[i * 96 : i * 96 + 1632] for i in range(4)]),
         query_seg[:, None], small, query_weight, kv_weight, out_weight, up_weight, down_weight],
        [ANY, VM, VM, VM, ANY, ANY, ANY, ANY, ANY],
        [((2048, 512), bf16), ((2048, 256), bf16), ((512, 2048), bf16), ((2048, 2048), bf16),
         ((2048, 2048), bf16), ((8, 2048), f32), ((384, 2048), bf16), ((4, 384, 128), bf16),
         ((5, 4, 96, 256), bf16), ((4, 384, 128), f32), ((4, 96, 512), bf16),
         ((4, 96, 2048), bf16), ((96, 2048), f32)],
        [ANY] * 5 + [VM] + [ANY] * 6 + [VM],
        [pltpu.VMEM((2048, 512), bf16), pltpu.VMEM((2048, 256), bf16), pltpu.VMEM((512, 2048), bf16),
         pltpu.VMEM((2, 16, 16, 128), f32), pltpu.VMEM((384, 2048), bf16),
         pltpu.VMEM((384, 2048), bf16), pltpu.VMEM((4, 384, 128), bf16),
         pltpu.VMEM((5, 4, 96, 256), bf16), pltpu.VMEM((1920, 256), bf16),
         pltpu.VMEM((4, 384, 128), f32), pltpu.VMEM((4, 96, 512), bf16),
         pltpu.VMEM((4, 96, 1632), f32),
         pltpu.VMEM((128, 256), f32), pltpu.VMEM((64, 256), f32), pltpu.VMEM((256, 128), f32),
         pltpu.VMEM((128, 1024), f32), pltpu.VMEM((1024, 128), f32),
         pltpu.VMEM((128, 256), bf16), pltpu.VMEM((64, 256), bf16), pltpu.VMEM((256, 128), bf16),
         pltpu.VMEM((128, 1024), bf16), pltpu.VMEM((1024, 128), bf16),
         pltpu.VMEM((384, 2048), f32), pltpu.VMEM((384, 1632), f32), pltpu.VMEM((384, 1632), bf16),
         pltpu.VMEM((384, 128), bf16), pltpu.VMEM((4, 96, 2048), bf16),
         pltpu.VMEM((2, 48, 2048), bf16), pltpu.VMEM((2, 96, 2048), bf16), pltpu.VMEM((96, 2048), bf16)]
        + sems(256, 32),
    )
    normed_two = normed_two.reshape(half, 2048)
    gain_two, down_b, up_b = vectors[3], vectors[5], vectors[6]

    cot = lax.dynamic_slice_in_dim(cotangent, hi * half, half)
    hidden, gelu_back = jax.vjp(gelu_tanh, matmul(normed_two, up_w) + up_b)
    hidden = hidden.astype(bf16)
    mlp_part = matmul(hidden, down_w).astype(bf16).reshape(4, 96, 2048)
    down_part = contract_rows(hidden, cot).astype(bf16)
    grad_up = gelu_back(contract_cols(cot, down_w))[0].astype(bf16)
    up_bias_sum = jnp.sum(grad_up.astype(f32), axis=0)
    up_part = contract_rows(normed_two, grad_up).astype(bf16)
    norm_part = contract_cols(grad_up, up_w).astype(bf16).reshape(4, 96, 2048)
    out_rows, grad_middle, grad_attn, sums, up_grad, down_grad = kernel_call(
        mlp_back, "mlp_back", 2,
        [mlp_part, norm_part, middle, cot_rows, jnp.stack([down_b, gain_two]), up_part, down_part],
        [VM, VM, VM, VM, VM, ANY, ANY],
        [((96, 2048), bf16), ((96, 2048), f32), ((4, 96, 2048), bf16), ((8, 2048), f32),
         ((128, 1024), f32), ((1024, 128), f32)],
        [VM, VM, ANY, VM, VM, VM],
        [pltpu.VMEM((2, 48, 2048), bf16), pltpu.VMEM((2, 96, 2048), bf16)] * 2
        + [pltpu.VMEM((96, 2048), bf16)]
        + rs2d_bufs((128, 1024)) + rs2d_bufs((1024, 128)) + sems(128, 40),
    )
    lows = jnp.sum(key_seg[None, :] < query_seg[:, None], axis=1, dtype=jnp.int32)
    lows = jnp.tile(lows.reshape(4, 96) - 96 * jnp.arange(4)[:, None], (1, heads))
    V = pltpu.VMEM
    output, input_grad, query_grad, keyval_grad, out_grad, small_grad = kernel_call(
        tail, "tail", 3,
        [grad_attn.reshape(half, 2048), attended.reshape(half, 512), query_rows,
         window.reshape(5 * half, 256), lse, normed_one, query_w, keyval_w, out_w, tokens, out_rows,
         lows, grad_middle, vectors, sums, up_bias_sum[None]],
        [ANY] * 11 + [VM] * 5,
        [((2, 4, 96, 2048), bf16), ((2, 4, 96, 2048), bf16), ((128, 256), f32), ((128, 256), f32),
         ((256, 128), f32), ((16, 128), f32)],
        [ANY, ANY, VM, VM, VM, VM],
        [V((384, 2048), bf16), V((384, 512), bf16), V((4, 384, 128), bf16), V((1920, 256), bf16),
         V((4, 384, 128), f32), V((384, 2048), bf16), V((2048, 512), bf16), V((2048, 256), bf16),
         V((512, 2048), bf16), V((96, 2048), bf16),
         V((512, 2048), bf16), V((2048, 512), bf16), V((2048, 256), bf16), V((4, 384, 128), bf16),
         V((1632, 384), f32), V((1632, 384), f32), V((1632, 384), bf16), V((1632, 384), bf16),
         V((1920, 128), f32), V((1920, 128), f32), V((384, 512), bf16), V((4, 96, 2048), bf16),
         V((2, 48, 2048), bf16), V((2, 96, 2048), bf16), V((5, 384, 256), bf16),
         V((4, 384, 256), bf16), V((4, 96, 256), bf16), V((3, 96, 256), bf16), V((384, 256), bf16),
         V((96, 2048), bf16), V((8, 2048), f32), V((3, 16, 128), f32), V((2, 16, 16, 128), f32),
         V((16, 128), f32), V((3, 16, 128), f32), V((64, 256), f32)]
        + rs2d_bufs((128, 256)) + rs2d_bufs((64, 256)) + rs2d_bufs((256, 128))
        + rs2d_bufs((16, 128), f32) + sems(256, 96),
    )
    return (
        output.reshape(768, 2048),
        input_grad.reshape(768, 2048).astype(f32),
        small_grad[0],
        small_grad[1],
        query_grad,
        small_grad[6:8, :8],
        keyval_grad,
        small_grad[6, 8:16],
        out_grad,
        small_grad[2],
        small_grad[3],
        small_grad[4],
        up_grad,
        small_grad[8:16, :8],
        down_grad,
        small_grad[5],
    )


def solution(mesh):
    return jax.shard_map(
        body,
        mesh=mesh,
        in_specs=(
            P("dp", None), P("dp", None), P(), P("dp"), P("dp"), P("dp", "tensor"),
            P("tensor", "dp"), P("dp", None), P("dp"), P("tensor", "dp"), P("dp"), P("dp"),
            P("dp"), P("dp", "tensor"), P("tensor", "dp"), P("tensor", "dp"), P("dp"),
        ),
        out_specs=(
            P("dp", None), P("dp", None), P("dp"), P("dp"), P("dp", "tensor"),
            P("tensor", "dp"), P("dp", None), P("dp"), P("tensor", "dp"), P("dp"), P("dp"),
            P("dp"), P("dp", "tensor"), P("tensor", "dp"), P("tensor", "dp"), P("dp"),
        ),
        check_vma=False,
    )
```

```python
import functools
import math

import jax
import jax.numpy as jnp
from jax import lax
from jax.experimental import pallas as pl
from jax.experimental.pallas import tpu as pltpu
from jax.sharding import PartitionSpec as P

HD = 128
EPS = 1e-05
NEG = -1e30
MESH = pl.DeviceIdType.MESH
bf16 = jnp.bfloat16
f32 = jnp.float32


class Place:
    def __init__(self):
        dp = lax.axis_index("dp")
        tensor = lax.axis_index("tensor")
        self.core = dp % 2
        self.x = (dp // 2) % 4
        self.y = (tensor // 4) * 2 + dp // 8
        self.z = tensor % 4

    def dev(self, x=None, y=None, z=None, core=None):
        x = self.x if x is None else x
        y = self.y if y is None else y
        z = self.z if z is None else z
        core = self.core if core is None else core
        return ((y % 2) * 8 + x * 2 + core, (y // 2) * 4 + z)

    def sibling(self):
        return self.dev(core=1 - self.core)

    def ring(self, axis):
        return Ring(self, axis)


class Ring:
    def __init__(self, place, axis):
        self.p = getattr(place, axis)
        self.plus = place.dev(**{axis: (self.p + 1) % 4})
        self.minus = place.dev(**{axis: (self.p + 3) % 4})
        self.after = (self.p + 1) % 4
        self.before = (self.p + 3) % 4
        self.across = (self.p + 2) % 4
        self.others = [place.dev(**{axis: self.across}), self.plus, self.minus]
        self.sources = [self.across, self.before, self.after]


class Net:
    def __init__(self, ssem, rsem, lsem):
        self.ssem, self.rsem, self.lsem = ssem, rsem, lsem
        self.n = 0
        self.m = 0
        self.sent = []
        self.group = 0
        self.todo = {}

    def send(self, src, dst, dev):
        i = self.n
        self.n += 1
        copy = pltpu.make_async_remote_copy(
            src_ref=src,
            dst_ref=dst,
            send_sem=self.ssem.at[i],
            recv_sem=self.rsem.at[i],
            device_id=dev,
            device_id_type=MESH,
        )
        copy.start()
        self.sent.append(copy)
        return copy

    def local(self, src, dst):
        i = self.m
        self.m += 1
        copy = pltpu.make_async_copy(src, dst, self.lsem.at[i])
        copy.start()
        return copy

    def spawn(self, gen):
        place = self.todo.setdefault(self.group, [])
        place.append(gen)
        self.step(gen, place)

    def begin(self, gen, group=0):
        state = [False]

        def whole():
            yield from gen
            state[0] = True

        self.group = group
        self.spawn(whole())
        return state

    def step(self, gen, place):
        try:
            next(gen)
        except StopIteration:
            place.remove(gen)

    def pump(self, *groups):
        for group in groups:
            self.group = group
            place = self.todo.setdefault(group, [])
            for gen in list(place):
                self.step(gen, place)

    def until(self, *states):
        for group, state in states:
            while not state[0]:
                self.pump(group)

    def run(self, *gens):
        for gen in gens:
            self.spawn(gen)
        while any(self.todo.values()):
            self.pump(*self.todo)
        for copy in self.sent:
            copy.wait_send()


def greet(devices):
    barrier = pltpu.get_barrier_semaphore()
    for device in devices:
        pl.semaphore_signal(barrier, inc=1, device_id=device, device_id_type=MESH)
    pl.semaphore_wait(barrier, len(devices))


def rows_half(ref, which):
    n = ref.shape[-2] // 2
    if len(ref.shape) == 2:
        return ref.at[pl.ds(which * n, n), :]
    return ref.at[:, pl.ds(which * n, n), :]


def lane_step(shape):
    return max(16, min(shape[0], 32768 // shape[1]))


def over_rows(rows, step, fn):
    def one(i, carry):
        fn(pl.ds(pl.multiple_of(i * step, step), step))
        return carry

    lax.fori_loop(0, rows // step, one, 0)


def add_into(dst, *srcs, out=None):
    out = dst if out is None else out
    rows, step = dst.shape[0], lane_step(dst.shape)
    if rows % step:
        step = 16 if rows % 16 == 0 else rows

    def one(at):
        total = dst[at, :].astype(f32)
        for src in srcs:
            total = total + src[at, :].astype(f32)
        out[at, :] = total.astype(out.dtype)

    over_rows(rows, step, one)


def ag_ring(net, ring, slot, own, have=None, half=rows_half):
    have = have or (lambda pos: None)
    c0 = net.send(own, slot(ring.p), ring.plus)
    c1 = net.send(own, slot(ring.p), ring.minus)
    yield
    c0.wait_recv()
    one = half(slot(ring.before), 0)
    c2 = net.send(one, one, ring.plus)
    have(ring.before)
    c1.wait_recv()
    two = half(slot(ring.after), 1)
    c3 = net.send(two, two, ring.minus)
    have(ring.after)
    yield
    c2.wait_recv()
    c3.wait_recv()
    have(ring.across)


def ag2d(net, place, own, slot, first, second):
    sib = place.sibling()
    pairs = []

    def give(a, b, src=None):
        ref = slot(a, b)
        pairs.append(net.send(ref if src is None else src, ref, sib))

    def column(a, src):
        return ag_ring(net, second, lambda b: slot(a, b), src, lambda b: give(a, b))

    def main():
        keep = net.local(own, slot(first.p, second.p))
        c0 = net.send(own, slot(first.p, second.p), first.plus)
        c1 = net.send(own, slot(first.p, second.p), first.minus)
        yield
        net.spawn(column(first.p, own))
        give(first.p, second.p, own)
        c0.wait_recv()
        one = rows_half(slot(first.before, second.p), 0)
        c2 = net.send(one, one, first.plus)
        net.spawn(column(first.before, slot(first.before, second.p)))
        c1.wait_recv()
        two = rows_half(slot(first.after, second.p), 1)
        c3 = net.send(two, two, first.minus)
        net.spawn(column(first.after, slot(first.after, second.p)))
        give(first.before, second.p)
        give(first.after, second.p)
        yield
        c2.wait_recv()
        c3.wait_recv()
        net.spawn(column(first.across, slot(first.across, second.p)))
        give(first.across, second.p)
        keep.wait()
        while len(pairs) < 16:
            yield
        for pair in pairs:
            pair.wait_recv()

    return main()


def ag2d_direct(net, place, own, slot, first, second):
    sib = place.sibling()
    pairs = []

    def give(a, b, src=None):
        ref = slot(a, b)
        pairs.append(net.send(ref if src is None else src, ref, sib))

    def column(a, src):
        return [net.send(src, slot(a, second.p), dev) for dev in second.others]

    keep = net.local(own, slot(first.p, second.p))
    rows = [net.send(own, slot(first.p, second.p), dev) for dev in first.others]
    columns = [(first.p, column(first.p, own))]
    give(first.p, second.p, own)
    yield
    for a, copy in zip(first.sources, rows):
        copy.wait_recv()
        columns.append((a, column(a, slot(a, second.p))))
        give(a, second.p)
    yield
    for a, copies in columns:
        for b, copy in zip(second.sources, copies):
            copy.wait_recv()
            give(a, b)
    yield
    keep.wait()
    for pair in pairs:
        pair.wait_recv()


def rs_ring(net, ring, src, ra, rb, done):
    across, after, before = src(ring.across), src(ring.after), src(ring.before)
    a0 = net.send(rows_half(across, 0), ra(0), ring.plus)
    a1 = net.send(rows_half(across, 1), ra(1), ring.minus)
    b0 = net.send(rows_half(after, 1), rows_half(rb(0), 1), ring.plus)
    b1 = net.send(rows_half(before, 0), rows_half(rb(1), 0), ring.minus)
    yield
    a0.wait_recv()
    add_into(ra(0), rows_half(after, 0))
    b2 = net.send(ra(0), rows_half(rb(0), 0), ring.plus)
    a1.wait_recv()
    add_into(ra(1), rows_half(before, 1))
    b3 = net.send(ra(1), rows_half(rb(1), 1), ring.minus)
    yield
    for copy in (b0, b1, b2, b3):
        copy.wait_recv()
    done(src(ring.p), rb(0), rb(1))


def rs2d_direct(net, place, part, order, bufs, out):
    rv, ra, rb = bufs
    first, second = (place.ring(axis) for axis in order)
    own = part.at[place.core]

    def along(a):
        return own.at[:, a] if order == "xy" else own.at[a]

    def one(a, b):
        return own.at[b, a] if order == "xy" else own.at[a, b]

    pair = net.send(part.at[1 - place.core], rv, place.sibling())
    yield
    pair.wait_recv()

    def add_pair(i, carry):
        add_into(own.at[i // 4, i % 4], rv.at[i // 4, i % 4])
        return carry

    lax.fori_loop(0, 16, add_pair, 0)
    sent = [
        net.send(along(pos), ra.at[k], dev)
        for k, (pos, dev) in enumerate(zip((first.across, first.after, first.before), first.others))
    ]
    yield
    for copy in sent:
        copy.wait_recv()
    for b in range(4):
        add_into(one(first.p, b), ra.at[0, b], ra.at[1, b], ra.at[2, b])
    sent = [
        net.send(one(first.p, pos), rb.at[k], dev)
        for k, (pos, dev) in enumerate(
            zip((second.across, second.after, second.before), second.others)
        )
    ]
    yield
    for copy in sent:
        copy.wait_recv()
    add_into(one(first.p, second.p), rb.at[0], rb.at[1], rb.at[2], out=out)


def direct_bufs(shape, dtype=bf16):
    return [
        pltpu.VMEM((4, 4) + shape, dtype),
        pltpu.VMEM((3, 4) + shape, dtype),
        pltpu.VMEM((3,) + shape, dtype),
    ]


def rs2d_sum(net, r0, first, second, bufs, out):
    ra, rb, r1, sa, sb = bufs
    firsts = (first.across, first.after, first.before, first.p)
    seconds = (second.across, second.after, second.before, second.p)

    def term(i, j):
        return r0(firsts[i], seconds[j])

    halves, wholes = {}, {}
    for j in range(4):
        halves[0, j] = net.send(rows_half(term(0, j), 0), ra.at[0, j], first.plus)
        halves[1, j] = net.send(rows_half(term(0, j), 1), ra.at[1, j], first.minus)
    for j in range(4):
        wholes[0, j] = net.send(rows_half(term(1, j), 1), rows_half(rb.at[0, j], 1), first.plus)
        wholes[1, j] = net.send(rows_half(term(2, j), 0), rows_half(rb.at[1, j], 0), first.minus)
    yield
    for j in range(4):
        halves[0, j].wait_recv()
        add_into(ra.at[0, j], rows_half(term(1, j), 0))
        wholes[2, j] = net.send(ra.at[0, j], rows_half(rb.at[0, j], 0), first.plus)
        halves[1, j].wait_recv()
        add_into(ra.at[1, j], rows_half(term(2, j), 1))
        wholes[3, j] = net.send(ra.at[1, j], rows_half(rb.at[1, j], 1), first.minus)
        if j == 1:
            yield
    yield

    def settle(j):
        for k in range(4):
            wholes[k, j].wait_recv()
        add_into(term(3, j), rb.at[0, j], rb.at[1, j], out=r1.at[j])

    settle(0)
    a0 = net.send(rows_half(r1.at[0], 0), sa.at[0], second.plus)
    a1 = net.send(rows_half(r1.at[0], 1), sa.at[1], second.minus)
    settle(1)
    b0 = net.send(rows_half(r1.at[1], 1), rows_half(sb.at[0], 1), second.plus)
    yield
    settle(2)
    b1 = net.send(rows_half(r1.at[2], 0), rows_half(sb.at[1], 0), second.minus)
    settle(3)
    yield
    a0.wait_recv()
    add_into(sa.at[0], rows_half(r1.at[1], 0))
    b2 = net.send(sa.at[0], rows_half(sb.at[0], 0), second.plus)
    a1.wait_recv()
    add_into(sa.at[1], rows_half(r1.at[2], 1))
    b3 = net.send(sa.at[1], rows_half(sb.at[1], 1), second.minus)
    yield
    for copy in (b0, b1, b2, b3):
        copy.wait_recv()
    add_into(r1.at[3], sb.at[0], sb.at[1], out=out)


def ring_bufs(shape, dtype=bf16):
    rows, cols = shape
    half = (rows // 2, cols)
    return [
        pltpu.VMEM((2, 4) + half, dtype),
        pltpu.VMEM((2, 4) + shape, dtype),
        pltpu.VMEM((4,) + shape, dtype),
        pltpu.VMEM((2,) + half, dtype),
        pltpu.VMEM((2,) + shape, dtype),
    ]


def sems(count, local):
    return [
        pltpu.SemaphoreType.DMA((count,)),
        pltpu.SemaphoreType.DMA((count,)),
        pltpu.SemaphoreType.DMA((local,)),
    ]


ANY = pl.BlockSpec(memory_space=pl.ANY)
VM = pl.BlockSpec(memory_space=pltpu.VMEM)


def kernel_call(body, name, cid, ins, in_specs, outs, out_specs, scratch, nbytes=1 << 20):
    return pl.pallas_call(
        body,
        out_shape=[jax.ShapeDtypeStruct(s, d) for s, d in outs],
        in_specs=in_specs,
        out_specs=out_specs,
        scratch_shapes=scratch,
        compiler_params=pltpu.CompilerParams(
            collective_id=cid, has_side_effects=True, vmem_limit_bytes=58 << 20
        ),
        cost_estimate=pl.CostEstimate(flops=0, bytes_accessed=nbytes, transcendentals=0),
        name=name,
    )(*ins)


def block_of(x, y, core):
    return (y % 2) * 8 + x * 2 + core


def col_at(d):
    return pl.ds(pl.multiple_of(d * 128, 128), 128)


def row_at(start, size):
    return pl.ds(pl.multiple_of(start, size), size)


def at_query(ref, x, y, core):
    return ref.at[row_at(block_of(x, y, core) * 128, 128), row_at((y // 2) * 256, 256)]


def at_keyval(ref, x, y, core):
    return ref.at[row_at(block_of(x, y, core) * 128 + (y // 2) * 64, 64), :]


def at_out(ref, x, y, core):
    return ref.at[row_at((y // 2) * 256, 256), col_at(block_of(x, y, core))]


def at_up(ref, x, y, core):
    return ref.at[row_at(block_of(x, y, core) * 128, 128), row_at((y // 2) * 1024, 1024)]


def at_down(ref, x, y, core):
    return ref.at[row_at((y // 2) * 1024, 1024), col_at(block_of(x, y, core))]


def at_small(ref, x, y, core):
    return ref.at[y // 2, block_of(x, y, core)]


def gather(net, place, at, own, whole, order, how=ag2d):
    x, y = place.ring("x"), place.ring("y")
    if order == "xy":
        return how(net, place, own, lambda a, b: at(whole, a, b, place.core), x, y)
    return how(net, place, own, lambda a, b: at(whole, b, a, place.core), y, x)


def plane_peers(place):
    x, y = place.ring("x"), place.ring("y")
    return [place.sibling(), x.plus, x.minus, y.plus, y.minus]


def spread(values):
    center = values - jnp.mean(values, axis=-1, keepdims=True)
    return center, lax.rsqrt(jnp.mean(center * center, axis=-1, keepdims=True) + EPS)


def cast_into(dst, src):
    step = lane_step(dst.shape)
    step = step if dst.shape[0] % step == 0 else 16

    def one(at):
        dst[at, :] = src[at, :].astype(dst.dtype)

    over_rows(dst.shape[0], step, one)


def front(
    tokens, key_seg, query_seg, v0, v1, v2, v3, v4, v5, query_bias, value_bias, up_bias,
    query_w, keyval_w, out_w, up_w, down_w,
    o_query_w, o_keyval_w, o_out_w, g_up, g_down, vecs, o_normed, o_query, o_window, o_lse,
    o_attended, normed_two, middle,
    g_query, g_keyval, g_out, g_small, tok, normed, query, window, take, lse, attended, bias,
    f_query, f_keyval, f_out, f_up, f_down, b_query, b_keyval, b_out, b_up, b_down,
    unit, scores, weights, mixed, part, ra, rb, mine, rows6, short_q, short_v, short_u, small_own,
    *sem,
):
    place = Place()
    z = place.ring("z")
    hi = place.y // 2
    block = ((place.y % 2) * 8 + place.x * 2 + place.core) * 2 + hi
    earlier = [device_of_block(place, (block + 32 - k) % 32) for k in (1, 2, 3, 4)]
    later = [device_of_block(place, (block + k) % 32) for k in (1, 2, 3, 4)]
    net = Net(*sem)
    half_rows = pl.ds(pl.multiple_of(hi * 64, 64), 64)
    shorts = [net.local(v, rows6.at[i]) for i, v in enumerate((v0, v1, v2, v3, v4, v5))]
    shorts += [net.local(query_bias, short_q), net.local(value_bias, short_v), net.local(up_bias, short_u)]
    loads = [
        net.local(keyval_w.at[half_rows, :], f_keyval),
        net.local(query_w, f_query),
        net.local(out_w, f_out),
        net.local(tokens.at[pl.ds(pl.multiple_of(hi * 384, 384), 384), :], tok),
        net.local(up_w, f_up),
        net.local(down_w, f_down),
    ]
    x, y = place.ring("x"), place.ring("y")
    greet([place.sibling()] + x.others + y.others + z.others + earlier + later)
    for short in shorts:
        short.wait()

    def rounded(values):
        return values.astype(bf16).astype(f32)

    small_own[...] = jnp.zeros_like(small_own)
    for i in range(6):
        small_own[i : i + 1, :] = rounded(rows6[i])
    small_own[6:8, 0:8] = rounded(short_q[...])
    small_own[8:16, 0:8] = rounded(short_u[...])
    small_own[16:17, 0:8] = rounded(short_v[...])
    s_small = net.begin(gather(net, place, at_small, small_own, g_small, "yx", ag2d_direct), 1)
    loads[0].wait()
    cast_into(b_keyval, f_keyval)
    s_keyval = net.begin(gather(net, place, at_keyval, b_keyval, g_keyval, "xy", ag2d_direct), 1)
    loads[3].wait()

    def norm_some(at):
        center, inv = spread(tok[at, :].astype(f32))
        unit[at, :] = center * inv

    over_rows(96, 16, lambda at: norm_some(pl.ds(pl.multiple_of(at.start + place.z * 96, 16), 16)))
    net.pump(1)
    loads[1].wait()
    cast_into(b_query, f_query)
    loads[2].wait()
    cast_into(b_out, f_out)
    loads[4].wait()
    cast_into(b_up, f_up)
    loads[5].wait()
    cast_into(b_down, f_down)
    s_up = net.begin(gather(net, place, at_up, b_up, g_up, "xy"), 3)
    s_down = net.begin(gather(net, place, at_down, b_down, g_down, "yx"), 3)
    net.pump(1)
    net.until((1, s_small), (1, s_keyval))

    for d in range(16):
        vecs[0:6, d * 128 : (d + 1) * 128] = g_small[0, d, 0:6, :]
    lane = lax.broadcasted_iota(jnp.int32, (8, 128), 1)

    def collect(which, rows):
        total = jnp.zeros((8, 128), f32)
        for d in range(16):
            piece = jnp.where(lane < 8, g_small[which, d, rows : rows + 8, :], 0.0)
            total = total + (pltpu.roll(piece, d * 8, 1) if d else piece)
        return total

    biases = []
    for which in range(2):
        ups = collect(which, 8)
        for r in range(8):
            at = which * 1024 + r * 128
            vecs[6:7, at : at + 128] = ups[r : r + 1, :]
        biases.append(collect(which, 0))
    query_b = [biases[0][6:7], biases[0][7:8], biases[1][6:7], biases[1][7:8]]
    value_b = collect(0, 16)[0:1]

    def apply_some(at):
        normed[at, :] = (unit[at, :] * vecs[0:1, :] + vecs[1:2, :]).astype(bf16)

    over_rows(96, 16, lambda at: apply_some(pl.ds(pl.multiple_of(at.start + place.z * 96, 16), 16)))
    quarter = pl.ds(pl.multiple_of(place.z * 96, 96), 96)
    kv = jnp.dot(normed[quarter, :], g_keyval[...], preferred_element_type=f32)
    window[4, place.z] = (kv + jnp.concatenate([jnp.zeros((1, 128), f32), value_b], 1)).astype(bf16)

    def keys_values():
        own = window.at[4, place.z]
        sent = [net.send(own, window.at[4 - k, place.z], later[k - 1]) for k in (1, 2, 3, 4)]
        yield
        for copy in sent:
            copy.wait_recv()
        mine = window.at[:, place.z]
        sent = [net.send(mine, mine, dev) for dev in z.others]
        yield
        for copy in sent:
            copy.wait_recv()

    s_window = net.begin(keys_values(), 1)
    s_query = net.begin(gather(net, place, at_query, b_query, g_query, "xy", ag2d_direct), 2)
    s_out = net.begin(gather(net, place, at_out, b_out, g_out, "yx", ag2d_direct), 2)
    over_rows(192, 16, norm_some)
    net.pump(1)
    over_rows(192, 16, lambda at: norm_some(pl.ds(pl.multiple_of(at.start + 192, 16), 16)))
    net.pump(2)
    net.pump(3)
    over_rows(384, 16, apply_some)
    row = lax.broadcasted_iota(jnp.int32, (96, 1632), 0)
    column = lax.broadcasted_iota(jnp.int32, (96, 1632), 1)
    for i in range(4):
        same = query_seg[i * 96 : (i + 1) * 96, :] == key_seg[i : i + 1, :]
        bias[i] = jnp.where(same & (column <= row + 1536), 0.0, NEG)
    net.until((1, s_window))
    net.until((2, s_query))
    for i in range(4):
        rows = jnp.dot(normed[i * 96 : (i + 1) * 96, :], g_query[...], preferred_element_type=f32)
        for h in range(4):
            query[i, h * 96 : (h + 1) * 96, :] = (
                rows[:, h * 128 : (h + 1) * 128] + query_b[h]
            ).astype(bf16)
    net.until((1, s_window), (2, s_out))
    keeps = [
        net.local(*pair)
        for pair in (
            (g_query, o_query_w), (g_keyval, o_keyval_w), (g_out, o_out_w), (normed, o_normed),
            (query, o_query), (window, o_window),
        )
    ]
    for j in range(5):
        for i in range(4):
            take[pl.ds((j * 4 + i) * 96, 96), :] = window[j, i]
    scale = 1.0 / math.sqrt(HD)

    def attend(i):
        reach = pl.ds(pl.multiple_of(i * 96, 32), 1632)
        scores[...] = lax.dot_general(
            query[i], take[reach, 0:128], (((1,), (1,)), ((), ())), preferred_element_type=f32
        )

        def soften(c, carry):
            at = pl.ds(pl.multiple_of(c * 16, 16), 16)
            mask = pl.ds(pl.multiple_of((c % 6) * 16, 16), 16)
            some = scores[at, :] * scale + bias[i, mask, :]
            top = jnp.max(some, axis=-1, keepdims=True)
            some = jnp.exp(some - top)
            total = jnp.sum(some, axis=-1, keepdims=True)
            weights[at, :] = (some * (1.0 / total)).astype(bf16)
            lse[i, at, :] = jnp.broadcast_to(top + jnp.log(total), (16, 128))
            return carry

        lax.fori_loop(0, 24, soften, 0, unroll=4)
        mixed[...] = jnp.dot(
            weights[...], take[reach, 128:256], preferred_element_type=f32
        ).astype(bf16)
        for h in range(4):
            attended[i, :, h * 128 : (h + 1) * 128] = mixed[h * 96 : (h + 1) * 96, :]
        for n in range(4):
            columns = slice(n * 512, (n + 1) * 512)
            part[i, :, columns] = jnp.dot(
                attended[i], g_out[:, columns], preferred_element_type=f32
            ).astype(bf16)

    attend(z.across)
    a0 = net.send(rows_half(part.at[z.across], 0), ra.at[0], z.plus)
    a1 = net.send(rows_half(part.at[z.across], 1), ra.at[1], z.minus)
    attend(z.after)
    after = part.at[z.after]
    b0 = net.send(rows_half(after, 1), rows_half(rb.at[0], 1), z.plus)
    a0.wait_recv()
    add_into(ra.at[0], rows_half(after, 0))
    b1 = net.send(ra.at[0], rows_half(rb.at[0], 0), z.plus)
    net.pump(3)
    attend(z.before)
    before = part.at[z.before]
    b2 = net.send(rows_half(before, 0), rows_half(rb.at[1], 0), z.minus)
    a1.wait_recv()
    add_into(ra.at[1], rows_half(before, 1))
    b3 = net.send(ra.at[1], rows_half(rb.at[1], 1), z.minus)
    attend(z.p)
    keeps += [net.local(attended, o_attended), net.local(lse, o_lse)]
    for copy in (b0, b1, b2, b3):
        copy.wait_recv()

    def residual(at):
        mid = (
            tok[pl.ds(pl.multiple_of(place.z * 96 + at.start, 16), 16), :].astype(f32)
            + part[place.z, at, :].astype(f32)
            + rb[0, at, :].astype(f32)
            + rb[1, at, :].astype(f32)
            + vecs[2:3, :]
        )
        middle[at, :] = mid
        center, inv = spread(mid)
        mine[at, :] = (center * inv * vecs[3:4, :] + vecs[4:5, :]).astype(bf16)

    over_rows(96, 16, residual)
    keeps.append(net.local(mine, normed_two.at[z.p]))
    s_normed = net.begin(ag_ring(net, z, lambda i: normed_two.at[i], mine), 1)
    net.run()
    for keep in keeps:
        keep.wait()


def mid(
    normed_all, cotangent, up_w, down_w, vecs, middle,
    out_rows, grad_mid, grad_all, sums, up_sum, o_up, o_down,
    w_up, w_down, normed, cot, normed_pair, cot_pair, normed_sib, cot_sib, hidden, slope,
    part_norm, part_out, ra, rb, rc, rd, mine, up_terms, down_terms, up_later, down_later, up_grad, down_grad, up_more, down_more,
    *rest,
):
    place = Place()
    x, y, z = place.ring("x"), place.ring("y"), place.ring("z")
    hi = place.y // 2
    sib = place.sibling()
    ups, downs, ups_later, downs_later, sem = rest[:5], rest[5:10], rest[10:15], rest[15:20], rest[20:]
    net = Net(*sem)
    load_normed = net.local(normed_all, normed)
    load_cot = net.local(cotangent.at[pl.ds(pl.multiple_of(hi * 384, 384), 384), :], cot)
    load_up, load_down = [], []
    for c in range(4):
        at = pl.ds(c * 512, 512)
        load_up.append(net.local(up_w.at[:, at], w_up.at[:, at]))
        load_down.append(net.local(down_w.at[at, :], w_down.at[at, :]))
    greet([sib, x.plus, x.minus, y.plus, y.minus, z.plus, z.minus])

    def split(full, pair, other):
        for m in range(8):
            at = pl.ds(m * 128, 128)
            pair[0:384, at] = full[:, col_at(2 * m + place.core)]
            other[:, at] = full[:, col_at(2 * m + 1 - place.core)]
        return net.send(other, pair.at[pl.ds(384, 384), :], sib)

    load_normed.wait()
    swaps = [split(normed, normed_pair, normed_sib)]
    load_cot.wait()
    swaps.append(split(cot, cot_pair, cot_sib))
    for c in range(4):
        at = pl.ds(c * 512, 512)
        load_up[c].wait()
        load_down[c].wait()

        def some(r, carry):
            rows = pl.ds(pl.multiple_of(r * 192, 64), 192)
            upward = matmul(normed[rows, :], w_up[:, at]) + vecs[6:7, at]
            flow = contract_cols(cot[rows, :], w_down[at, :])
            square = upward * upward
            curve = jnp.tanh(0.7978845608028654 * upward * (1.0 + 0.044715 * square))
            hidden[rows, at] = (0.5 * upward * (1.0 + curve)).astype(bf16)
            steep = 0.5 * (1.0 + curve) + 0.5 * upward * (1.0 - curve * curve) * (
                0.7978845608028654 * (1.0 + 3.0 * 0.044715 * square)
            )
            slope[rows, at] = (flow * steep).astype(bf16)
            return carry

        lax.fori_loop(0, 2, some, 0)
        up_sum[0:1, at] = jnp.sum(slope[0:384, at].astype(f32), axis=0, keepdims=True)
        for pair in (hidden, slope):
            swaps.append(net.send(pair.at[pl.ds(0, 384), at], pair.at[pl.ds(384, 384), at], sib))

    for c in range(4):
        at = slice(c * 512, (c + 1) * 512)
        total = contract_cols(slope[0:384, :], w_up[at, :])
        for i in range(4):
            part_norm[i, :, at] = total[i * 96 : (i + 1) * 96].astype(bf16)

    def back():
        def done(own, one, two):
            sums[...] = jnp.zeros_like(sums)

            def some(at):
                grad = own[at, :].astype(f32) + one[at, :].astype(f32) + two[at, :].astype(f32)
                center, inv = spread(middle[at, :])
                norm = center * inv
                flow = grad * vecs[3:4, :]
                top = cot[pl.ds(pl.multiple_of(place.z * 96 + at.start, 16), 16), :].astype(f32)
                low = top + inv * (
                    flow
                    - jnp.mean(flow, axis=-1, keepdims=True)
                    - norm * jnp.mean(flow * norm, axis=-1, keepdims=True)
                )
                grad_mid[at, :] = low
                low = low.astype(bf16)
                mine[at, :] = low
                sums[0:1, :] += jnp.sum(grad * norm, axis=0, keepdims=True)
                sums[1:2, :] += jnp.sum(grad, axis=0, keepdims=True)
                sums[2:3, :] += jnp.sum(low.astype(f32), axis=0, keepdims=True)
                sums[3:4, :] += jnp.sum(top, axis=0, keepdims=True)

            over_rows(96, 16, some)

        yield from rs_ring(
            net, z, lambda i: part_norm.at[i], lambda i: ra.at[i], lambda i: rb.at[i], done
        )
        keep = net.local(mine, grad_all.at[z.p])
        yield from ag_ring(net, z, lambda i: grad_all.at[i], mine)
        keep.wait()

    def fore():
        def done(own, one, two):
            def some(at):
                out_rows[at, :] = (
                    middle[at, :]
                    + own[at, :].astype(f32)
                    + one[at, :].astype(f32)
                    + two[at, :].astype(f32)
                    + vecs[5:6, :]
                ).astype(bf16)

            over_rows(96, 16, some)

        yield from rs_ring(
            net, z, lambda i: part_out.at[i], lambda i: rc.at[i], lambda i: rd.at[i], done
        )

    net.begin(back(), 1)
    for copy in swaps:
        copy.wait_recv()

    def up_terms_of(k, carry):
        rows = pl.ds(pl.multiple_of((k % 2) * 512, 512), 512)
        columns = pl.ds(pl.multiple_of((k // 2) * 1024, 1024), 1024)
        total = contract_rows(normed_pair[:, rows], slope[:, columns])
        for i in range(4):
            up_terms[k, i] = total[i * 128 : (i + 1) * 128, 0:512].astype(bf16)
            up_later[k, i] = total[i * 128 : (i + 1) * 128, 512:1024].astype(bf16)
        return carry

    lax.fori_loop(0, 4, up_terms_of, 0)
    net.begin(rs2d_sum(net, lambda a, b: up_terms.at[a, b], y, x, ups, up_grad), 2)
    net.begin(rs2d_sum(net, lambda a, b: up_later.at[a, b], y, x, ups_later, up_more), 5)
    net.pump(1)

    def down_terms_of(k, carry):
        rows = pl.ds(pl.multiple_of((k // 2) * 1024, 1024), 1024)
        columns = pl.ds(pl.multiple_of((k % 2) * 512, 512), 512)
        total = contract_rows(hidden[:, rows], cot_pair[:, columns])
        for i in range(4):
            down_terms[i, k] = total[0:512, i * 128 : (i + 1) * 128].astype(bf16)
            down_later[i, k] = total[512:1024, i * 128 : (i + 1) * 128].astype(bf16)
        return carry

    lax.fori_loop(0, 4, down_terms_of, 0)
    net.begin(rs2d_sum(net, lambda a, b: down_terms.at[a, b], x, y, downs, down_grad), 4)
    net.begin(rs2d_sum(net, lambda a, b: down_later.at[a, b], x, y, downs_later, down_more), 6)
    net.pump(1)
    net.pump(2)
    for c in range(4):
        at = slice(c * 512, (c + 1) * 512)
        total = matmul(hidden[0:384, :], w_down[:, at])
        for i in range(4):
            part_out[i, :, at] = total[i * 96 : (i + 1) * 96].astype(bf16)
    net.pump(2)
    net.pump(4)
    net.pump(1)
    net.begin(fore(), 3)
    net.pump(5)
    net.pump(6)
    while any(net.todo.values()):
        for group in (2, 4, 1, 3, 5, 6):
            net.pump(group)
    net.run()
    keeps = [
        net.local(up_grad, o_up.at[:, pl.ds(0, 512)]),
        net.local(up_more, o_up.at[:, pl.ds(512, 512)]),
        net.local(down_grad, o_down.at[pl.ds(0, 512), :]),
        net.local(down_more, o_down.at[pl.ds(512, 512), :]),
    ]
    for keep in keeps:
        keep.wait()


def device_of_block(place, block):
    d = block // 2
    return ((d // 8) * 8 + ((d // 2) % 4) * 2 + d % 2, (block % 2) * 4 + place.z)


def lanes_half(ref, which):
    n = ref.shape[-1] // 2
    return ref.at[:, pl.ds(which * n, n)]


def tail(
    grad_all, attended_all, query_all, window_all, lse_all, normed_all, query_w, keyval_w, out_w,
    tokens, out_rows, low, grad_mid, vecs, sums, up_sum,
    output, input_grad, query_grad, keyval_grad, out_grad, small_grad,
    grad, attended, query, window, lse, normed, w_query, w_keyval, w_out, tok,
    part_out, part_query, part_keyval, flow, scores, change, probs, slopes, d_keys, d_values,
    grad_query, part, ra, rb, pieces, rk, stage, rz, kv_rows, mine, six, tiles, part_small,
    small_own, small_in, kv_own, kv_in, kv_sum, query_own, out_own, keyval_sum, small_sum, *rest,
):
    place = Place()
    x, y, z = place.ring("x"), place.ring("y"), place.ring("z")
    hi = place.y // 2
    partner = y.others[0]
    block = ((place.y % 2) * 8 + place.x * 2 + place.core) * 2 + hi
    earlier = [device_of_block(place, (block + 32 - k) % 32) for k in (1, 2, 3, 4)]
    later = [device_of_block(place, (block + k) % 32) for k in (1, 2, 3, 4)]
    queries, keyvals, outs, smalls, sem = rest[:3], rest[3:6], rest[6:9], rest[9:12], rest[12:]
    net = Net(*sem)
    token_rows = pl.ds(pl.multiple_of(hi * 384 + place.z * 96, 96), 96)
    loads = {
        name: net.local(*pair)
        for name, pair in dict(
            grad=(grad_all, grad), attended=(attended_all, attended), out=(out_w, w_out),
            query=(query_all, query), window=(window_all, window), lse=(lse_all, lse),
            query_w=(query_w, w_query), normed=(normed_all, normed), keyval=(keyval_w, w_keyval),
            tok=(tokens.at[token_rows, :], tok),
        ).items()
    }
    greet([place.sibling()] + x.others + y.others + z.others + earlier + later)

    def y_first(own, slot, half):
        keep = net.local(own, slot(hi, z.p))
        swap = net.send(own, slot(hi, z.p), partner)
        net.spawn(ag_ring(net, z, lambda i: slot(hi, i), own, half=half))
        yield
        swap.wait_recv()
        net.spawn(ag_ring(net, z, lambda i: slot(1 - hi, i), slot(1 - hi, z.p), half=half))
        keep.wait()

    def z_first(own, slot, half):
        keep = net.local(own, slot(hi, z.p))
        swaps = [net.send(own, slot(hi, z.p), partner)]

        def have(i):
            swaps.append(net.send(slot(hi, i), slot(hi, i), partner))

        yield from ag_ring(net, z, lambda i: slot(hi, i), own, have, half)
        yield
        keep.wait()
        for swap in swaps:
            swap.wait_recv()

    net.pump(5, 1)
    net.begin(y_first(out_rows, lambda a, b: output.at[a, b], rows_half), 4)
    loads["grad"].wait()
    loads["attended"].wait()
    for n in range(4):
        total = contract_rows(attended[...], grad[:, n * 512 : (n + 1) * 512]).astype(bf16)
        for i in range(4):
            for which in range(2):
                part_out[i % 2, which * 2 + n // 2, (n % 2) * 2 + i // 2] = total[
                    which * 256 : (which + 1) * 256, i * 128 : (i + 1) * 128
                ]
    net.begin(rs2d_direct(net, place, part_out, "xy", outs, out_own), 2)
    loads["out"].wait()
    whole = contract_cols(grad[...], w_out[...]).astype(bf16)
    for i in range(4):
        for h in range(4):
            flow[i, h * 96 : (h + 1) * 96, :] = whole[
                i * 96 : (i + 1) * 96, h * 128 : (h + 1) * 128
            ]
    d_keys[...] = jnp.zeros_like(d_keys)
    d_values[...] = jnp.zeros_like(d_values)
    for name in ("query", "window", "lse", "query_w"):
        loads[name].wait()
    scale = 1.0 / math.sqrt(HD)
    lane = lax.broadcasted_iota(jnp.int32, (384, 128), 1)
    last = 1536 + lax.broadcasted_iota(jnp.int32, (32, 384), 1) % 96
    key = lax.broadcasted_iota(jnp.int32, (32, 384), 0)

    def attend(i):
        reach = pl.ds(pl.multiple_of(i * 96, 32), 1632)
        rows = pl.ds(pl.multiple_of(i * 96, 32), 96)
        for h in range(4):
            at = pl.ds(h * 96, 96)
            product = flow[i, at, :].astype(f32) * attended[
                rows, h * 128 : (h + 1) * 128
            ].astype(f32)
            lse[i, at, :] = jnp.where(
                lane[:96] == 0, lse[i, at, :], jnp.sum(product, axis=-1, keepdims=True)
            )
        across = jnp.transpose(lse[i])
        total, delta = across[0:1, :], across[1:2, :]
        first = low[pl.ds(i, 1), :]
        scores[...] = contract_cols(window[reach, 0:128], query[i])
        change[...] = contract_cols(window[reach, 128:256], flow[i])

        def soften(c, carry):
            at = pl.ds(pl.multiple_of(c * 32, 32), 32)
            where = key + c * 32
            some = jnp.where(
                (where >= first) & (where <= last), scores[at, :] * scale - total, NEG
            )
            some = jnp.exp(some)
            probs[at, :] = some.astype(bf16)
            slopes[at, :] = (some * (change[at, :] - delta)).astype(bf16)
            return carry

        lax.fori_loop(0, 51, soften, 0, unroll=3)
        d_values[reach, :] += matmul(probs[...], flow[i])
        d_keys[reach, :] += matmul(slopes[...], query[i])
        turned = jnp.transpose(contract_rows(window[reach, 0:128], slopes[...])) * scale
        for h in range(4):
            grad_query[rows, h * 128 : (h + 1) * 128] = turned[h * 96 : (h + 1) * 96].astype(bf16)
        for n in range(4):
            columns = slice(n * 512, (n + 1) * 512)
            part[i, :, columns] = contract_cols(grad_query[rows, :], w_query[columns, :]).astype(bf16)

    attend(z.across)
    a0 = net.send(rows_half(part.at[z.across], 0), ra.at[0], z.plus)
    a1 = net.send(rows_half(part.at[z.across], 1), ra.at[1], z.minus)
    net.pump(2)
    attend(z.after)
    after = part.at[z.after]
    b0 = net.send(rows_half(after, 1), rows_half(rb.at[0], 1), z.plus)
    net.pump(4)
    attend(z.before)
    before = part.at[z.before]
    b2 = net.send(rows_half(before, 0), rows_half(rb.at[1], 0), z.minus)
    a0.wait_recv()
    add_into(ra.at[0], rows_half(after, 0))
    b1 = net.send(ra.at[0], rows_half(rb.at[0], 0), z.plus)
    a1.wait_recv()
    add_into(ra.at[1], rows_half(before, 1))
    b3 = net.send(ra.at[1], rows_half(rb.at[1], 1), z.minus)
    attend(z.p)
    for j in range(5):
        at = slice(j * 384, (j + 1) * 384)
        pieces[j, :, 0:128] = (d_keys[at, :] * scale).astype(bf16)
        pieces[j, :, 128:256] = d_values[at, :].astype(bf16)

    def keys_values():
        sent = [net.send(pieces.at[4 - k], rk.at[k - 1], earlier[k - 1]) for k in (1, 2, 3, 4)]
        yield
        for copy in sent:
            copy.wait_recv()
        for i in range(4):
            at = pl.ds(i * 96, 96)
            add_into(pieces.at[4, at], *[rk.at[k, at] for k in range(4)], out=stage.at[i])
        sent = [
            net.send(stage.at[pos], rz.at[k], dev)
            for k, (pos, dev) in enumerate(zip((z.across, z.after, z.before), z.others))
        ]
        yield
        for copy in sent:
            copy.wait_recv()
        add_into(stage.at[place.z], *[rz.at[k] for k in range(3)], out=kv_rows)

    s_kv = net.begin(keys_values(), 1)
    loads["normed"].wait()
    for n in range(4):
        total = contract_rows(normed[:, n * 512 : (n + 1) * 512], grad_query[...]).astype(bf16)
        for i in range(4):
            for which in range(2):
                part_query[i % 2, which * 2 + n // 2, (n % 2) * 2 + i // 2] = total[
                    i * 128 : (i + 1) * 128, which * 256 : (which + 1) * 256
                ]
    net.begin(rs2d_direct(net, place, part_query, "xy", queries, query_own), 3)
    net.pump(2)
    net.pump(4)
    net.pump(1)
    net.pump(3)
    loads["keyval"].wait()
    loads["tok"].wait()
    net.until((1, s_kv))
    quarter = pl.ds(pl.multiple_of(place.z * 96, 96), 96)
    for n in range(4):
        total = contract_rows(normed[quarter, n * 512 : (n + 1) * 512], kv_rows[...]).astype(bf16)
        for i in range(4):
            for which in range(2):
                part_keyval[i % 2, which * 2 + n // 2, (n % 2) * 2 + i // 2] = total[
                    i * 128 + which * 64 : i * 128 + (which + 1) * 64, :
                ]

    def keyval():
        yield from rs2d_direct(net, place, part_keyval, "xy", keyvals, kv_own)
        sent = [net.send(kv_own, kv_in.at[k], dev) for k, dev in enumerate(z.others)]
        yield
        for copy in sent:
            copy.wait_recv()
        add_into(kv_own, kv_in.at[0], kv_in.at[1], kv_in.at[2], out=kv_sum)
        home = keyval_sum.at[pl.ds(pl.multiple_of(hi * 64, 64), 64), :]
        keep = net.local(kv_sum, home)
        swap = net.send(kv_sum, home, partner)
        yield
        keep.wait()
        swap.wait_recv()

    net.begin(keyval(), 7)
    for copy in (b0, b1, b2, b3):
        copy.wait_recv()
    six[...] = jnp.zeros_like(six)

    def norm_back(at):
        grad_norm = (
            part[place.z, at, :].astype(f32)
            + rb[0, at, :].astype(f32)
            + rb[1, at, :].astype(f32)
            + contract_cols(kv_rows[at, :], w_keyval[...])
        )
        center, inv = spread(tok[at, :].astype(f32))
        norm = center * inv
        down = grad_norm * vecs[0:1, :]
        mine[at, :] = (
            grad_mid[at, :]
            + inv
            * (
                down
                - jnp.mean(down, axis=-1, keepdims=True)
                - norm * jnp.mean(down * norm, axis=-1, keepdims=True)
            )
        ).astype(bf16)
        six[0:1, :] += jnp.sum(grad_norm * norm, axis=0, keepdims=True)
        six[1:2, :] += jnp.sum(grad_norm, axis=0, keepdims=True)

    for i in range(2):
        norm_back(pl.ds(i * 48, 48))
    top, bottom = pl.ds(0, 48), pl.ds(48, 48)
    net.begin(y_first(mine.at[top], lambda a, b: input_grad.at[a, b, top], lanes_half), 5)
    net.begin(z_first(mine.at[bottom], lambda a, b: input_grad.at[a, b, bottom], lanes_half), 5)
    six[2:3, :] = sums[2:3, :]
    six[3:4, :] = sums[0:1, :]
    six[4:5, :] = sums[1:2, :]
    six[5:6, :] = sums[3:4, :]
    bias_sum = jnp.sum(grad_query[...].astype(f32), axis=0, keepdims=True)
    value_sum = jnp.sum(kv_rows[:, 128:256].astype(f32), axis=0, keepdims=True)
    tiles[...] = jnp.zeros_like(tiles)
    for which in range(2):
        for h in range(2):
            at = (which * 2 + h) * 128
            tiles[which, 6 + h : 7 + h, :] = bias_sum[:, at : at + 128]
        for r in range(8):
            at = which * 1024 + r * 128
            tiles[which, 8 + r : 9 + r, :] = up_sum[0:1, at : at + 128]
    tiles[2, 6:7, :] = value_sum
    lane = lax.broadcasted_iota(jnp.int32, (16, 128), 1)

    def turn(tile, shift):
        shift = shift % 128
        return pltpu.roll(tile, shift, 1) if shift else tile

    for d in range(16):
        values = jnp.where((lane >= 8) & (lane < 16), turn(tiles[2], 136 - d * 8), 0.0)
        for which in range(2):
            piece = jnp.where(lane < 8, turn(tiles[which], 128 - d * 8), values)
            home = (d % 2, which * 2 + d // 8, (d // 2) % 4)
            part_small[home + (slice(6, 16),)] = piece[6:16]
            part_small[home + (slice(0, 6),)] = six[0:6, d * 128 : (d + 1) * 128]

    def small():
        yield from rs2d_direct(net, place, part_small, "xy", smalls, small_own)
        sent = [net.send(small_own, small_in.at[k], dev) for k, dev in enumerate(z.others)]
        yield
        for copy in sent:
            copy.wait_recv()
        total = small_own[...]
        whole = total + small_in[0] + small_in[1] + small_in[2]
        row = lax.broadcasted_iota(jnp.int32, (16, 128), 0)
        total = jnp.where((row < 6) | ((row == 6) & (lane >= 8)), whole, total)
        small_sum[0:16, :] = total
        small_sum[16:24, :] = turn(total[0:8], 120)

    net.begin(small(), 7)
    net.run()
    keeps = [
        net.local(*pair)
        for pair in (
            (query_own, query_grad), (out_own, out_grad), (keyval_sum, keyval_grad),
            (small_sum, small_grad),
        )
    ]
    for keep in keeps:
        keep.wait()


def leave_kernel(
    output, input_grad, small, query, keyval, out, up, down,
    o_output, o_input, o_gain_one, o_shift_one, o_query, o_query_b, o_keyval, o_value_b, o_out,
    o_out_b, o_gain_two, o_shift_two, o_up, o_up_b, o_down, o_down_b,
):
    o_output[...] = output[...]
    o_input[...] = input_grad[...].astype(f32)

    @pl.when(pl.program_id(0) == 0)
    def _():
        rows = (o_gain_one, o_shift_one, o_out_b, o_gain_two, o_shift_two, o_down_b)
        for i, row in enumerate(rows):
            row[...] = small[i]
        o_query_b[...] = small[6:8, 0:8]
        o_value_b[...] = small[22, 0:8]
        o_up_b[...] = small[8:16, 0:8]
        o_query[...] = query[...]
        o_keyval[...] = keyval[...]
        o_out[...] = out[...]
        o_up[...] = up[...]
        o_down[...] = down[...]


def leave(output, input_grad, *rest):
    rows = pl.BlockSpec((128, 2048), lambda i: (i, 0))

    def fixed(shape):
        return pl.BlockSpec(shape, lambda i: (0,) * len(shape))

    shapes = [(128,), (128,), (128, 256), (2, 8), (128, 256), (8,), (256, 128), (128,), (128,),
              (128,), (128, 1024), (8, 8), (1024, 128), (128,)]
    return pl.pallas_call(
        leave_kernel,
        grid=(6,),
        out_shape=[jax.ShapeDtypeStruct((768, 2048), bf16), jax.ShapeDtypeStruct((768, 2048), f32)]
        + [jax.ShapeDtypeStruct(shape, f32) for shape in shapes],
        in_specs=[rows, rows] + [fixed(array.shape) for array in rest],
        out_specs=[rows, rows] + [fixed(shape) for shape in shapes],
        compiler_params=pltpu.CompilerParams(vmem_limit_bytes=60 << 20),
        cost_estimate=pl.CostEstimate(flops=0, bytes_accessed=16 << 20, transcendentals=0),
        name="leave",
    )(output, input_grad, *rest)


def matmul(left, right):
    return jnp.dot(left, right, preferred_element_type=f32)


def contract_rows(left, right):
    return lax.dot_general(left, right, (((0,), (0,)), ((), ())), preferred_element_type=f32)


def contract_cols(left, right):
    return lax.dot_general(left, right, (((1,), (1,)), ((), ())), preferred_element_type=f32)


def body(
    tokens, cotangent, segments, attn_norm_gain, attn_norm_bias, query_weight, query_bias,
    kv_weight, value_bias, out_weight, out_bias, mlp_norm_gain, mlp_norm_bias, up_weight,
    up_bias, down_weight, down_bias,
):
    dp = lax.axis_index("dp")
    tensor = lax.axis_index("tensor")
    hi, z = tensor // 4, tensor % 4
    half, heads = 384, 4

    start = dp * 768 + hi * half
    key_seg = lax.dynamic_slice_in_dim(
        jnp.concatenate([jnp.full((4 * half,), -1, jnp.int32), segments]), start, 5 * half
    )
    query_seg = key_seg[4 * half :]
    (
        query_w, keyval_w, out_w, up_w, down_w, vectors, normed_one, query_rows, window, lse,
        attended, normed_two, middle,
    ) = kernel_call(
        front, "front", 0,
        [tokens, jnp.stack([key_seg[i * 96 : i * 96 + 1632] for i in range(4)]),
         query_seg[:, None], attn_norm_gain[None], attn_norm_bias[None], out_bias[None],
         mlp_norm_gain[None], mlp_norm_bias[None], down_bias[None], query_bias, value_bias[None],
         up_bias, query_weight, kv_weight, out_weight, up_weight, down_weight],
        [ANY, VM, VM] + [ANY] * 14,
        [((2048, 512), bf16), ((2048, 256), bf16), ((512, 2048), bf16), ((2048, 2048), bf16),
         ((2048, 2048), bf16), ((8, 2048), f32), ((384, 2048), bf16), ((4, 384, 128), bf16),
         ((5, 4, 96, 256), bf16), ((4, 384, 128), f32), ((4, 96, 512), bf16),
         ((4, 96, 2048), bf16), ((96, 2048), f32)],
        [ANY] * 5 + [VM] + [ANY] * 6 + [VM],
        [pltpu.VMEM((2048, 512), bf16), pltpu.VMEM((2048, 256), bf16), pltpu.VMEM((512, 2048), bf16),
         pltpu.VMEM((2, 16, 24, 128), f32), pltpu.VMEM((384, 2048), bf16),
         pltpu.VMEM((384, 2048), bf16), pltpu.VMEM((4, 384, 128), bf16),
         pltpu.VMEM((5, 4, 96, 256), bf16), pltpu.VMEM((1920, 256), bf16),
         pltpu.VMEM((4, 384, 128), f32), pltpu.VMEM((4, 96, 512), bf16),
         pltpu.VMEM((4, 96, 1632), f32),
         pltpu.VMEM((128, 256), f32), pltpu.VMEM((64, 256), f32), pltpu.VMEM((256, 128), f32),
         pltpu.VMEM((128, 1024), f32), pltpu.VMEM((1024, 128), f32),
         pltpu.VMEM((128, 256), bf16), pltpu.VMEM((64, 256), bf16), pltpu.VMEM((256, 128), bf16),
         pltpu.VMEM((128, 1024), bf16), pltpu.VMEM((1024, 128), bf16),
         pltpu.VMEM((384, 2048), f32), pltpu.VMEM((384, 1632), f32), pltpu.VMEM((384, 1632), bf16),
         pltpu.VMEM((384, 128), bf16), pltpu.VMEM((4, 96, 2048), bf16),
         pltpu.VMEM((2, 48, 2048), bf16), pltpu.VMEM((2, 96, 2048), bf16), pltpu.VMEM((96, 2048), bf16),
         pltpu.VMEM((6, 1, 128), f32), pltpu.VMEM((2, 8), f32), pltpu.VMEM((1, 8), f32),
         pltpu.VMEM((8, 8), f32), pltpu.VMEM((24, 128), f32)]
        + sems(256, 40),
    )
    V = pltpu.VMEM
    (
        out_rows, grad_middle, grad_attn, sums, up_bias_sum, up_grad, down_grad,
    ) = kernel_call(
        mid, "mid", 2,
        [normed_two.reshape(half, 2048), cotangent, up_w, down_w, vectors, middle],
        [ANY, ANY, ANY, ANY, VM, VM],
        [((96, 2048), bf16), ((96, 2048), f32), ((4, 96, 2048), bf16), ((8, 2048), f32),
         ((1, 2048), f32), ((128, 1024), f32), ((1024, 128), f32)],
        [VM, VM, ANY, VM, VM, ANY, ANY],
        [V((2048, 2048), bf16), V((2048, 2048), bf16), V((384, 2048), bf16), V((384, 2048), bf16),
         V((768, 1024), bf16), V((768, 1024), bf16), V((384, 1024), bf16), V((384, 1024), bf16),
         V((768, 2048), bf16), V((768, 2048), bf16), V((4, 96, 2048), bf16),
         V((4, 96, 2048), bf16)]
        + [V((2, 48, 2048), bf16), V((2, 96, 2048), bf16)] * 2
        + [V((96, 2048), bf16)] + [V((4, 4, 128, 512), bf16), V((4, 4, 512, 128), bf16)] * 2
        + [V((128, 512), f32), V((512, 128), f32)] * 2
        + (ring_bufs((128, 512)) + ring_bufs((512, 128))) * 2 + sems(192, 16),
    )

    lows = jnp.sum(key_seg[None, :] < query_seg[:, None], axis=1, dtype=jnp.int32)
    lows = jnp.tile(lows.reshape(4, 96) - 96 * jnp.arange(4)[:, None], (1, heads))
    output, input_grad, query_grad, keyval_grad, out_grad, small_grad = kernel_call(
        tail, "tail", 3,
        [grad_attn.reshape(half, 2048), attended.reshape(half, 512), query_rows,
         window.reshape(5 * half, 256), lse, normed_one, query_w, keyval_w, out_w, tokens, out_rows,
         lows, grad_middle, vectors, sums, up_bias_sum],
        [ANY] * 11 + [VM] * 5,
        [((2, 4, 96, 2048), bf16), ((2, 4, 96, 2048), bf16), ((128, 256), f32), ((128, 256), f32),
         ((256, 128), f32), ((24, 128), f32)],
        [ANY] * 6,
        [V((384, 2048), bf16), V((384, 512), bf16), V((4, 384, 128), bf16), V((1920, 256), bf16),
         V((4, 384, 128), f32), V((384, 2048), bf16), V((2048, 512), bf16), V((2048, 256), bf16),
         V((512, 2048), bf16), V((96, 2048), bf16),
         V((2, 4, 4, 256, 128), bf16), V((2, 4, 4, 128, 256), bf16), V((2, 4, 4, 64, 256), bf16),
         V((4, 384, 128), bf16),
         V((1632, 384), f32), V((1632, 384), f32), V((1632, 384), bf16), V((1632, 384), bf16),
         V((1920, 128), f32), V((1920, 128), f32), V((384, 512), bf16), V((4, 96, 2048), bf16),
         V((2, 48, 2048), bf16), V((2, 96, 2048), bf16), V((5, 384, 256), bf16),
         V((4, 384, 256), bf16), V((4, 96, 256), bf16), V((3, 96, 256), bf16), V((96, 256), bf16),
         V((96, 2048), bf16), V((8, 2048), f32), V((3, 16, 128), f32), V((2, 4, 4, 16, 128), f32),
         V((16, 128), f32), V((3, 16, 128), f32), V((64, 256), f32),
         V((3, 64, 256), f32), V((64, 256), f32), V((128, 256), f32), V((256, 128), f32),
         V((128, 256), f32), V((24, 128), f32)]
        + direct_bufs((128, 256)) + direct_bufs((64, 256)) + direct_bufs((256, 128))
        + direct_bufs((16, 128), f32) + sems(128, 24),
    )
    return leave(
        output.reshape(768, 2048), input_grad.reshape(768, 2048), small_grad, query_grad,
        keyval_grad, out_grad, up_grad, down_grad,
    )


def solution(mesh):
    return jax.shard_map(
        body,
        mesh=mesh,
        in_specs=(
            P("dp", None), P("dp", None), P(), P("dp"), P("dp"), P("dp", "tensor"),
            P("tensor", "dp"), P("dp", None), P("dp"), P("tensor", "dp"), P("dp"), P("dp"),
            P("dp"), P("dp", "tensor"), P("tensor", "dp"), P("tensor", "dp"), P("dp"),
        ),
        out_specs=(
            P("dp", None), P("dp", None), P("dp"), P("dp"), P("dp", "tensor"),
            P("tensor", "dp"), P("dp", None), P("dp"), P("tensor", "dp"), P("dp"), P("dp"),
            P("dp"), P("dp", "tensor"), P("tensor", "dp"), P("tensor", "dp"), P("dp"),
        ),
        check_vma=False,
    )
```

```python
import functools
import math

import jax
import jax.numpy as jnp
from jax import lax
from jax.experimental import pallas as pl
from jax.experimental.pallas import tpu as pltpu
from jax.sharding import PartitionSpec as P

HD = 128
EPS = 1e-05
NEG = -1e30
MESH = pl.DeviceIdType.MESH
bf16 = jnp.bfloat16
f32 = jnp.float32


class Place:
    def __init__(self):
        dp = lax.axis_index("dp")
        tensor = lax.axis_index("tensor")
        self.core = dp % 2
        self.x = (dp // 2) % 4
        self.y = (tensor // 4) * 2 + dp // 8
        self.z = tensor % 4

    def dev(self, x=None, y=None, z=None, core=None):
        x = self.x if x is None else x
        y = self.y if y is None else y
        z = self.z if z is None else z
        core = self.core if core is None else core
        return ((y % 2) * 8 + x * 2 + core, (y // 2) * 4 + z)

    def sibling(self):
        return self.dev(core=1 - self.core)

    def ring(self, axis):
        return Ring(self, axis)


class Ring:
    def __init__(self, place, axis):
        self.p = getattr(place, axis)
        self.plus = place.dev(**{axis: (self.p + 1) % 4})
        self.minus = place.dev(**{axis: (self.p + 3) % 4})
        self.after = (self.p + 1) % 4
        self.before = (self.p + 3) % 4
        self.across = (self.p + 2) % 4
        self.others = [place.dev(**{axis: self.across}), self.plus, self.minus]
        self.sources = [self.across, self.before, self.after]


class Net:
    def __init__(self, ssem, rsem, lsem):
        self.ssem, self.rsem, self.lsem = ssem, rsem, lsem
        self.n = 0
        self.m = 0
        self.sent = []
        self.group = 0
        self.todo = {}

    def send(self, src, dst, dev):
        i = self.n
        self.n += 1
        copy = pltpu.make_async_remote_copy(
            src_ref=src,
            dst_ref=dst,
            send_sem=self.ssem.at[i],
            recv_sem=self.rsem.at[i],
            device_id=dev,
            device_id_type=MESH,
        )
        copy.start()
        self.sent.append(copy)
        return copy

    def local(self, src, dst):
        i = self.m
        self.m += 1
        copy = pltpu.make_async_copy(src, dst, self.lsem.at[i])
        copy.start()
        return copy

    def spawn(self, gen):
        place = self.todo.setdefault(self.group, [])
        place.append(gen)
        self.step(gen, place)

    def begin(self, gen, group=0):
        state = [False]

        def whole():
            yield from gen
            state[0] = True

        self.group = group
        self.spawn(whole())
        return state

    def step(self, gen, place):
        try:
            next(gen)
        except StopIteration:
            place.remove(gen)

    def pump(self, *groups):
        for group in groups:
            self.group = group
            place = self.todo.setdefault(group, [])
            for gen in list(place):
                self.step(gen, place)

    def until(self, *states):
        for group, state in states:
            while not state[0]:
                self.pump(group)

    def run(self, *gens):
        for gen in gens:
            self.spawn(gen)
        while any(self.todo.values()):
            self.pump(*self.todo)
        for copy in self.sent:
            copy.wait_send()


def greet(devices):
    barrier = pltpu.get_barrier_semaphore()
    for device in devices:
        pl.semaphore_signal(barrier, inc=1, device_id=device, device_id_type=MESH)
    pl.semaphore_wait(barrier, len(devices))


def rows_half(ref, which):
    n = ref.shape[-2] // 2
    if len(ref.shape) == 2:
        return ref.at[pl.ds(which * n, n), :]
    return ref.at[:, pl.ds(which * n, n), :]


def lane_step(shape):
    return max(16, min(shape[0], 32768 // shape[1]))


def over_rows(rows, step, fn):
    def one(i, carry):
        fn(pl.ds(pl.multiple_of(i * step, step), step))
        return carry

    lax.fori_loop(0, rows // step, one, 0)


def add_into(dst, *srcs, out=None):
    out = dst if out is None else out
    rows, step = dst.shape[0], lane_step(dst.shape)
    if rows % step:
        step = 16 if rows % 16 == 0 else rows

    def one(at):
        total = dst[at, :].astype(f32)
        for src in srcs:
            total = total + src[at, :].astype(f32)
        out[at, :] = total.astype(out.dtype)

    over_rows(rows, step, one)


def ag_ring(net, ring, slot, own, have=None, half=rows_half):
    have = have or (lambda pos: None)
    c0 = net.send(own, slot(ring.p), ring.plus)
    c1 = net.send(own, slot(ring.p), ring.minus)
    yield
    c0.wait_recv()
    one = half(slot(ring.before), 0)
    c2 = net.send(one, one, ring.plus)
    have(ring.before)
    c1.wait_recv()
    two = half(slot(ring.after), 1)
    c3 = net.send(two, two, ring.minus)
    have(ring.after)
    yield
    c2.wait_recv()
    c3.wait_recv()
    have(ring.across)


def ag2d(net, place, own, slot, first, second):
    sib = place.sibling()
    pairs = []

    def give(a, b, src=None):
        ref = slot(a, b)
        pairs.append(net.send(ref if src is None else src, ref, sib))

    def column(a, src):
        return ag_ring(net, second, lambda b: slot(a, b), src, lambda b: give(a, b))

    def main():
        keep = net.local(own, slot(first.p, second.p))
        c0 = net.send(own, slot(first.p, second.p), first.plus)
        c1 = net.send(own, slot(first.p, second.p), first.minus)
        yield
        net.spawn(column(first.p, own))
        give(first.p, second.p, own)
        c0.wait_recv()
        one = rows_half(slot(first.before, second.p), 0)
        c2 = net.send(one, one, first.plus)
        net.spawn(column(first.before, slot(first.before, second.p)))
        c1.wait_recv()
        two = rows_half(slot(first.after, second.p), 1)
        c3 = net.send(two, two, first.minus)
        net.spawn(column(first.after, slot(first.after, second.p)))
        give(first.before, second.p)
        give(first.after, second.p)
        yield
        c2.wait_recv()
        c3.wait_recv()
        net.spawn(column(first.across, slot(first.across, second.p)))
        give(first.across, second.p)
        keep.wait()
        while len(pairs) < 16:
            yield
        for pair in pairs:
            pair.wait_recv()

    return main()


def ag2d_direct(net, place, own, slot, first, second):
    sib = place.sibling()
    pairs = []

    def give(a, b, src=None):
        ref = slot(a, b)
        pairs.append(net.send(ref if src is None else src, ref, sib))

    def column(a, src):
        return [net.send(src, slot(a, second.p), dev) for dev in second.others]

    keep = net.local(own, slot(first.p, second.p))
    rows = [net.send(own, slot(first.p, second.p), dev) for dev in first.others]
    columns = [(first.p, column(first.p, own))]
    give(first.p, second.p, own)
    yield
    for a, copy in zip(first.sources, rows):
        copy.wait_recv()
        columns.append((a, column(a, slot(a, second.p))))
        give(a, second.p)
    yield
    for a, copies in columns:
        for b, copy in zip(second.sources, copies):
            copy.wait_recv()
            give(a, b)
    yield
    keep.wait()
    for pair in pairs:
        pair.wait_recv()


def rs_ring(net, ring, src, ra, rb, done):
    across, after, before = src(ring.across), src(ring.after), src(ring.before)
    a0 = net.send(rows_half(across, 0), ra(0), ring.plus)
    a1 = net.send(rows_half(across, 1), ra(1), ring.minus)
    b0 = net.send(rows_half(after, 1), rows_half(rb(0), 1), ring.plus)
    b1 = net.send(rows_half(before, 0), rows_half(rb(1), 0), ring.minus)
    yield
    a0.wait_recv()
    add_into(ra(0), rows_half(after, 0))
    b2 = net.send(ra(0), rows_half(rb(0), 0), ring.plus)
    a1.wait_recv()
    add_into(ra(1), rows_half(before, 1))
    b3 = net.send(ra(1), rows_half(rb(1), 1), ring.minus)
    yield
    for copy in (b0, b1, b2, b3):
        copy.wait_recv()
    done(src(ring.p), rb(0), rb(1))


def rs2d_direct(net, place, part, order, bufs, out):
    rv, ra, rb = bufs
    first, second = (place.ring(axis) for axis in order)
    own = part.at[place.core]

    def along(a):
        return own.at[:, a] if order == "xy" else own.at[a]

    def one(a, b):
        return own.at[b, a] if order == "xy" else own.at[a, b]

    pair = net.send(part.at[1 - place.core], rv, place.sibling())
    yield
    pair.wait_recv()

    def add_pair(i, carry):
        add_into(own.at[i // 4, i % 4], rv.at[i // 4, i % 4])
        return carry

    lax.fori_loop(0, 16, add_pair, 0)
    sent = [
        net.send(along(pos), ra.at[k], dev)
        for k, (pos, dev) in enumerate(zip((first.across, first.after, first.before), first.others))
    ]
    yield
    for copy in sent:
        copy.wait_recv()
    for b in range(4):
        add_into(one(first.p, b), ra.at[0, b], ra.at[1, b], ra.at[2, b])
    sent = [
        net.send(one(first.p, pos), rb.at[k], dev)
        for k, (pos, dev) in enumerate(
            zip((second.across, second.after, second.before), second.others)
        )
    ]
    yield
    for copy in sent:
        copy.wait_recv()
    add_into(one(first.p, second.p), rb.at[0], rb.at[1], rb.at[2], out=out)


def direct_bufs(shape, dtype=bf16):
    return [
        pltpu.VMEM((4, 4) + shape, dtype),
        pltpu.VMEM((3, 4) + shape, dtype),
        pltpu.VMEM((3,) + shape, dtype),
    ]


def rs2d_sum(net, r0, first, second, bufs, out):
    ra, rb, r1, sa, sb = bufs
    firsts = (first.across, first.after, first.before, first.p)
    seconds = (second.across, second.after, second.before, second.p)

    def term(i, j):
        return r0(firsts[i], seconds[j])

    halves, wholes = {}, {}
    for j in range(4):
        halves[0, j] = net.send(rows_half(term(0, j), 0), ra.at[0, j], first.plus)
        halves[1, j] = net.send(rows_half(term(0, j), 1), ra.at[1, j], first.minus)
    yield
    for j in range(4):
        wholes[0, j] = net.send(rows_half(term(1, j), 1), rows_half(rb.at[0, j], 1), first.plus)
        wholes[1, j] = net.send(rows_half(term(2, j), 0), rows_half(rb.at[1, j], 0), first.minus)
    yield
    for j in range(4):
        halves[0, j].wait_recv()
        add_into(ra.at[0, j], rows_half(term(1, j), 0))
        wholes[2, j] = net.send(ra.at[0, j], rows_half(rb.at[0, j], 0), first.plus)
        halves[1, j].wait_recv()
        add_into(ra.at[1, j], rows_half(term(2, j), 1))
        wholes[3, j] = net.send(ra.at[1, j], rows_half(rb.at[1, j], 1), first.minus)
        if j == 1:
            yield
    yield

    def settle(j):
        for k in range(4):
            wholes[k, j].wait_recv()
        add_into(term(3, j), rb.at[0, j], rb.at[1, j], out=r1.at[j])

    settle(0)
    a0 = net.send(rows_half(r1.at[0], 0), sa.at[0], second.plus)
    a1 = net.send(rows_half(r1.at[0], 1), sa.at[1], second.minus)
    settle(1)
    b0 = net.send(rows_half(r1.at[1], 1), rows_half(sb.at[0], 1), second.plus)
    yield
    settle(2)
    b1 = net.send(rows_half(r1.at[2], 0), rows_half(sb.at[1], 0), second.minus)
    settle(3)
    yield
    a0.wait_recv()
    add_into(sa.at[0], rows_half(r1.at[1], 0))
    b2 = net.send(sa.at[0], rows_half(sb.at[0], 0), second.plus)
    a1.wait_recv()
    add_into(sa.at[1], rows_half(r1.at[2], 1))
    b3 = net.send(sa.at[1], rows_half(sb.at[1], 1), second.minus)
    yield
    for copy in (b0, b1, b2, b3):
        copy.wait_recv()
    add_into(r1.at[3], sb.at[0], sb.at[1], out=out)


def ring_bufs(shape, dtype=bf16):
    rows, cols = shape
    half = (rows // 2, cols)
    return [
        pltpu.VMEM((2, 4) + half, dtype),
        pltpu.VMEM((2, 4) + shape, dtype),
        pltpu.VMEM((4,) + shape, dtype),
        pltpu.VMEM((2,) + half, dtype),
        pltpu.VMEM((2,) + shape, dtype),
    ]


def sems(count, local):
    return [
        pltpu.SemaphoreType.DMA((count,)),
        pltpu.SemaphoreType.DMA((count,)),
        pltpu.SemaphoreType.DMA((local,)),
    ]


ANY = pl.BlockSpec(memory_space=pl.ANY)
VM = pl.BlockSpec(memory_space=pltpu.VMEM)


def kernel_call(body, name, cid, ins, in_specs, outs, out_specs, scratch, nbytes=1 << 20):
    return pl.pallas_call(
        body,
        out_shape=[jax.ShapeDtypeStruct(s, d) for s, d in outs],
        in_specs=in_specs,
        out_specs=out_specs,
        scratch_shapes=scratch,
        compiler_params=pltpu.CompilerParams(
            collective_id=cid, has_side_effects=True, vmem_limit_bytes=58 << 20
        ),
        cost_estimate=pl.CostEstimate(flops=0, bytes_accessed=nbytes, transcendentals=0),
        name=name,
    )(*ins)


def block_of(x, y, core):
    return (y % 2) * 8 + x * 2 + core


def col_at(d):
    return pl.ds(pl.multiple_of(d * 128, 128), 128)


def row_at(start, size):
    return pl.ds(pl.multiple_of(start, size), size)


def at_query(ref, x, y, core):
    return ref.at[row_at(block_of(x, y, core) * 128, 128), row_at((y // 2) * 256, 256)]


def at_keyval(ref, x, y, core):
    return ref.at[row_at(block_of(x, y, core) * 128 + (y // 2) * 64, 64), :]


def at_out(ref, x, y, core):
    return ref.at[row_at((y // 2) * 256, 256), col_at(block_of(x, y, core))]


def at_up(ref, x, y, core):
    return ref.at[row_at(block_of(x, y, core) * 128, 128), row_at((y // 2) * 1024, 1024)]


def at_down(ref, x, y, core):
    return ref.at[row_at((y // 2) * 1024, 1024), col_at(block_of(x, y, core))]


def at_small(ref, x, y, core):
    return ref.at[y // 2, block_of(x, y, core)]


def gather(net, place, at, own, whole, order, how=ag2d):
    x, y = place.ring("x"), place.ring("y")
    if order == "xy":
        return how(net, place, own, lambda a, b: at(whole, a, b, place.core), x, y)
    return how(net, place, own, lambda a, b: at(whole, b, a, place.core), y, x)


def plane_peers(place):
    x, y = place.ring("x"), place.ring("y")
    return [place.sibling(), x.plus, x.minus, y.plus, y.minus]


def spread(values):
    center = values - jnp.mean(values, axis=-1, keepdims=True)
    return center, lax.rsqrt(jnp.mean(center * center, axis=-1, keepdims=True) + EPS)


def cast_into(dst, src):
    step = lane_step(dst.shape)
    step = step if dst.shape[0] % step == 0 else 16

    def one(at):
        dst[at, :] = src[at, :].astype(dst.dtype)

    over_rows(dst.shape[0], step, one)


def front(
    tokens, key_seg, query_seg, v0, v1, v2, v3, v4, v5, query_bias, value_bias, up_bias,
    query_w, keyval_w, out_w, up_w, down_w,
    o_query_w, o_keyval_w, o_out_w, g_up, g_down, vecs, o_normed, o_query, o_window, o_lse,
    o_attended, normed_two, middle,
    g_query, g_keyval, g_out, g_small, tok, normed, query, window, take, lse, attended, bias,
    f_query, f_keyval, f_out, f_up, f_down, b_query, b_keyval, b_out, b_up, b_down,
    unit, scores, weights, mixed, part, ra, rb, mine, rows6, short_q, short_v, short_u, small_own,
    *sem,
):
    place = Place()
    z = place.ring("z")
    hi = place.y // 2
    block = ((place.y % 2) * 8 + place.x * 2 + place.core) * 2 + hi
    earlier = [device_of_block(place, (block + 32 - k) % 32) for k in (1, 2, 3, 4)]
    later = [device_of_block(place, (block + k) % 32) for k in (1, 2, 3, 4)]
    net = Net(*sem)
    half_rows = pl.ds(pl.multiple_of(hi * 64, 64), 64)
    shorts = [net.local(v, rows6.at[i]) for i, v in enumerate((v0, v1, v2, v3, v4, v5))]
    shorts += [net.local(query_bias, short_q), net.local(value_bias, short_v), net.local(up_bias, short_u)]
    loads = [
        net.local(keyval_w.at[half_rows, :], f_keyval),
        net.local(query_w, f_query),
        net.local(out_w, f_out),
        net.local(tokens.at[pl.ds(pl.multiple_of(hi * 384, 384), 384), :], tok),
        net.local(up_w, f_up),
        net.local(down_w, f_down),
    ]
    x, y = place.ring("x"), place.ring("y")
    greet([place.sibling()] + x.others + y.others + z.others + earlier + later)
    for short in shorts:
        short.wait()

    def rounded(values):
        return values.astype(bf16).astype(f32)

    small_own[...] = jnp.zeros_like(small_own)
    for i in range(6):
        small_own[i : i + 1, :] = rounded(rows6[i])
    small_own[6:8, 0:8] = rounded(short_q[...])
    small_own[8:16, 0:8] = rounded(short_u[...])
    small_own[16:17, 0:8] = rounded(short_v[...])
    s_small = net.begin(gather(net, place, at_small, small_own, g_small, "yx", ag2d_direct), 1)
    loads[0].wait()
    cast_into(b_keyval, f_keyval)
    s_keyval = net.begin(gather(net, place, at_keyval, b_keyval, g_keyval, "xy", ag2d_direct), 1)
    loads[3].wait()

    def norm_some(at):
        center, inv = spread(tok[at, :].astype(f32))
        unit[at, :] = center * inv

    over_rows(192, 16, norm_some)
    net.pump(1)
    loads[1].wait()
    cast_into(b_query, f_query)
    s_query = net.begin(gather(net, place, at_query, b_query, g_query, "xy", ag2d_direct), 2)
    loads[2].wait()
    cast_into(b_out, f_out)
    s_out = net.begin(gather(net, place, at_out, b_out, g_out, "yx", ag2d_direct), 2)
    loads[4].wait()
    cast_into(b_up, f_up)
    loads[5].wait()
    cast_into(b_down, f_down)
    net.begin(gather(net, place, at_up, b_up, g_up, "xy"), 3)
    net.begin(gather(net, place, at_down, b_down, g_down, "yx"), 3)
    over_rows(192, 16, lambda at: norm_some(pl.ds(pl.multiple_of(at.start + 192, 16), 16)))
    net.pump(1)
    net.until((1, s_small), (1, s_keyval))

    for d in range(16):
        vecs[0:6, d * 128 : (d + 1) * 128] = g_small[0, d, 0:6, :]
    lane = lax.broadcasted_iota(jnp.int32, (8, 128), 1)

    def collect(which, rows):
        total = jnp.zeros((8, 128), f32)
        for d in range(16):
            piece = jnp.where(lane < 8, g_small[which, d, rows : rows + 8, :], 0.0)
            total = total + (pltpu.roll(piece, d * 8, 1) if d else piece)
        return total

    biases = []
    for which in range(2):
        ups = collect(which, 8)
        for r in range(8):
            at = which * 1024 + r * 128
            vecs[6:7, at : at + 128] = ups[r : r + 1, :]
        biases.append(collect(which, 0))
    query_b = [biases[0][6:7], biases[0][7:8], biases[1][6:7], biases[1][7:8]]
    value_b = collect(0, 16)[0:1]

    def apply_some(at):
        normed[at, :] = (unit[at, :] * vecs[0:1, :] + vecs[1:2, :]).astype(bf16)

    over_rows(384, 16, apply_some)
    kv = jnp.dot(normed[...], g_keyval[...], preferred_element_type=f32)
    kv = (kv + jnp.concatenate([jnp.zeros((1, 128), f32), value_b], 1)).astype(bf16)
    for i in range(4):
        window[4, i] = kv[i * 96 : (i + 1) * 96]

    def keys_values():
        own = window.at[4, place.z]
        sent = [net.send(own, window.at[4 - k, place.z], later[k - 1]) for k in (1, 2, 3, 4)]
        yield
        for copy in sent:
            copy.wait_recv()
        mine = window.at[pl.ds(0, 4), place.z]
        sent = [net.send(mine, mine, dev) for dev in z.others]
        yield
        for copy in sent:
            copy.wait_recv()

    s_window = net.begin(keys_values(), 1)
    net.pump(2)
    row = lax.broadcasted_iota(jnp.int32, (96, 1632), 0)
    column = lax.broadcasted_iota(jnp.int32, (96, 1632), 1)
    for i in range(4):
        same = query_seg[i * 96 : (i + 1) * 96, :] == key_seg[i : i + 1, :]
        bias[i] = jnp.where(same & (column <= row + 1536), 0.0, NEG)
    net.pump(1)
    net.pump(3)
    net.pump(2)
    net.until((2, s_query))
    for i in range(4):
        rows = jnp.dot(normed[i * 96 : (i + 1) * 96, :], g_query[...], preferred_element_type=f32)
        for h in range(4):
            query[i, h * 96 : (h + 1) * 96, :] = (
                rows[:, h * 128 : (h + 1) * 128] + query_b[h]
            ).astype(bf16)
    net.until((1, s_window), (2, s_out))
    keeps = [
        net.local(*pair)
        for pair in (
            (g_query, o_query_w), (g_keyval, o_keyval_w), (g_out, o_out_w), (normed, o_normed),
            (query, o_query), (window, o_window),
        )
    ]
    for j in range(5):
        for i in range(4):
            take[pl.ds((j * 4 + i) * 96, 96), :] = window[j, i]
    scale = 1.0 / math.sqrt(HD)

    def attend(i):
        reach = pl.ds(pl.multiple_of(i * 96, 32), 1632)
        scores[...] = lax.dot_general(
            query[i], take[reach, 0:128], (((1,), (1,)), ((), ())), preferred_element_type=f32
        )

        def soften(c, carry):
            at = pl.ds(pl.multiple_of(c * 16, 16), 16)
            mask = pl.ds(pl.multiple_of((c % 6) * 16, 16), 16)
            some = scores[at, :] * scale + bias[i, mask, :]
            top = jnp.max(some, axis=-1, keepdims=True)
            some = jnp.exp(some - top)
            total = jnp.sum(some, axis=-1, keepdims=True)
            weights[at, :] = (some * (1.0 / total)).astype(bf16)
            lse[i, at, :] = jnp.broadcast_to(top + jnp.log(total), (16, 128))
            return carry

        lax.fori_loop(0, 24, soften, 0, unroll=4)
        mixed[...] = jnp.dot(
            weights[...], take[reach, 128:256], preferred_element_type=f32
        ).astype(bf16)
        for h in range(4):
            attended[i, :, h * 128 : (h + 1) * 128] = mixed[h * 96 : (h + 1) * 96, :]
        for n in range(4):
            columns = slice(n * 512, (n + 1) * 512)
            part[i, :, columns] = jnp.dot(
                attended[i], g_out[:, columns], preferred_element_type=f32
            ).astype(bf16)

    attend(z.across)
    a0 = net.send(rows_half(part.at[z.across], 0), ra.at[0], z.plus)
    a1 = net.send(rows_half(part.at[z.across], 1), ra.at[1], z.minus)
    attend(z.after)
    after = part.at[z.after]
    b0 = net.send(rows_half(after, 1), rows_half(rb.at[0], 1), z.plus)
    attend(z.before)
    before = part.at[z.before]
    b2 = net.send(rows_half(before, 0), rows_half(rb.at[1], 0), z.minus)
    a0.wait_recv()
    add_into(ra.at[0], rows_half(after, 0))
    b1 = net.send(ra.at[0], rows_half(rb.at[0], 0), z.plus)
    a1.wait_recv()
    add_into(ra.at[1], rows_half(before, 1))
    b3 = net.send(ra.at[1], rows_half(rb.at[1], 1), z.minus)
    net.pump(3)
    attend(z.p)
    keeps += [net.local(attended, o_attended), net.local(lse, o_lse)]

    def residual(at):
        mid = (
            tok[pl.ds(pl.multiple_of(place.z * 96 + at.start, 16), 16), :].astype(f32)
            + part[place.z, at, :].astype(f32)
            + rb[0, at, :].astype(f32)
            + rb[1, at, :].astype(f32)
            + vecs[2:3, :]
        )
        middle[at, :] = mid
        center, inv = spread(mid)
        mine[at, :] = (center * inv * vecs[3:4, :] + vecs[4:5, :]).astype(bf16)

    for which, copies in ((0, (b1, b2)), (1, (b0, b3))):
        for copy in copies:
            copy.wait_recv()
        at = pl.ds(which * 48, 48)
        over_rows(48, 16, lambda r: residual(pl.ds(pl.multiple_of(r.start + which * 48, 16), 16)))
        keeps.append(net.local(mine.at[at], normed_two.at[z.p, at]))
        net.begin(
            ag_ring(net, z, lambda i, at=at: normed_two.at[i, at], mine.at[at], half=lanes_half), 1
        )
    net.pump(3)
    net.pump(1)
    while any(net.todo[group] for group in (1, 3)):
        net.pump(3, 1)
    net.run()
    for keep in keeps:
        keep.wait()


def mid(
    normed_all, cotangent, up_w, down_w, vecs, middle,
    out_rows, grad_mid, grad_all, sums, up_sum, o_up, o_down,
    w_up, w_down, normed, cot, normed_pair, cot_pair, normed_sib, cot_sib, hidden, slope,
    part_norm, part_out, ra, rb, rc, rd, mine, up_terms, down_terms, up_later, down_later, up_grad, down_grad, up_more, down_more,
    *rest,
):
    place = Place()
    x, y, z = place.ring("x"), place.ring("y"), place.ring("z")
    hi = place.y // 2
    sib = place.sibling()
    ups, downs, ups_later, downs_later, sem = rest[:5], rest[5:10], rest[10:15], rest[15:20], rest[20:]
    net = Net(*sem)
    load_normed = net.local(normed_all, normed)
    load_cot = net.local(cotangent.at[pl.ds(pl.multiple_of(hi * 384, 384), 384), :], cot)
    load_up, load_down = [], []
    for c in range(4):
        at = pl.ds(c * 512, 512)
        load_up.append(net.local(up_w.at[:, at], w_up.at[:, at]))
        load_down.append(net.local(down_w.at[at, :], w_down.at[at, :]))
    greet([sib, x.plus, x.minus, y.plus, y.minus, z.plus, z.minus])

    def split(full, pair, other):
        for m in range(8):
            at = pl.ds(m * 128, 128)
            pair[0:384, at] = full[:, col_at(2 * m + place.core)]
            other[:, at] = full[:, col_at(2 * m + 1 - place.core)]
        return net.send(other, pair.at[pl.ds(384, 384), :], sib)

    load_normed.wait()
    swaps = [split(normed, normed_pair, normed_sib)]
    load_cot.wait()
    swaps.append(split(cot, cot_pair, cot_sib))
    for c in range(4):
        at = pl.ds(c * 512, 512)
        load_up[c].wait()
        load_down[c].wait()

        def some(r, carry):
            rows = pl.ds(pl.multiple_of(r * 192, 64), 192)
            upward = matmul(normed[rows, :], w_up[:, at]) + vecs[6:7, at]
            flow = contract_cols(cot[rows, :], w_down[at, :])
            square = upward * upward
            curve = jnp.tanh(0.7978845608028654 * upward * (1.0 + 0.044715 * square))
            hidden[rows, at] = (0.5 * upward * (1.0 + curve)).astype(bf16)
            steep = 0.5 * (1.0 + curve) + 0.5 * upward * (1.0 - curve * curve) * (
                0.7978845608028654 * (1.0 + 3.0 * 0.044715 * square)
            )
            slope[rows, at] = (flow * steep).astype(bf16)
            return carry

        lax.fori_loop(0, 2, some, 0)
        up_sum[0:1, at] = jnp.sum(slope[0:384, at].astype(f32), axis=0, keepdims=True)
        for pair in (hidden, slope):
            swaps.append(net.send(pair.at[pl.ds(0, 384), at], pair.at[pl.ds(384, 384), at], sib))

    for c in range(4):
        at = slice(c * 512, (c + 1) * 512)
        total = contract_cols(slope[0:384, :], w_up[at, :])
        for i in range(4):
            part_norm[i, :, at] = total[i * 96 : (i + 1) * 96].astype(bf16)

    def back():
        def done(own, one, two):
            sums[...] = jnp.zeros_like(sums)

            def some(at):
                grad = own[at, :].astype(f32) + one[at, :].astype(f32) + two[at, :].astype(f32)
                center, inv = spread(middle[at, :])
                norm = center * inv
                flow = grad * vecs[3:4, :]
                top = cot[pl.ds(pl.multiple_of(place.z * 96 + at.start, 16), 16), :].astype(f32)
                low = top + inv * (
                    flow
                    - jnp.mean(flow, axis=-1, keepdims=True)
                    - norm * jnp.mean(flow * norm, axis=-1, keepdims=True)
                )
                grad_mid[at, :] = low
                low = low.astype(bf16)
                mine[at, :] = low
                sums[0:1, :] += jnp.sum(grad * norm, axis=0, keepdims=True)
                sums[1:2, :] += jnp.sum(grad, axis=0, keepdims=True)
                sums[2:3, :] += jnp.sum(low.astype(f32), axis=0, keepdims=True)
                sums[3:4, :] += jnp.sum(top, axis=0, keepdims=True)

            for which in range(2):
                over_rows(48, 16, lambda r: some(pl.ds(pl.multiple_of(r.start + which * 48, 16), 16)))
                at = pl.ds(which * 48, 48)
                last.append(net.local(mine.at[at], grad_all.at[z.p, at]))
                net.spawn(
                    ag_ring(
                        net, z, lambda i, at=at: grad_all.at[i, at], mine.at[at], half=lanes_half
                    )
                )

        last = []
        yield from rs_ring(
            net, z, lambda i: part_norm.at[i], lambda i: ra.at[i], lambda i: rb.at[i], done
        )
        for keep in last:
            keep.wait()

    def fore():
        def done(own, one, two):
            def some(at):
                out_rows[at, :] = (
                    middle[at, :]
                    + own[at, :].astype(f32)
                    + one[at, :].astype(f32)
                    + two[at, :].astype(f32)
                    + vecs[5:6, :]
                ).astype(bf16)

            over_rows(96, 16, some)

        yield from rs_ring(
            net, z, lambda i: part_out.at[i], lambda i: rc.at[i], lambda i: rd.at[i], done
        )

    net.begin(back(), 1)
    for copy in swaps:
        copy.wait_recv()

    def up_terms_of(k, carry):
        rows = pl.ds(pl.multiple_of((k % 2) * 512, 512), 512)
        columns = pl.ds(pl.multiple_of((k // 2) * 1024, 1024), 1024)
        total = contract_rows(normed_pair[:, rows], slope[:, columns])
        for i in range(4):
            up_terms[k, i] = total[i * 128 : (i + 1) * 128, 0:512].astype(bf16)
            up_later[k, i] = total[i * 128 : (i + 1) * 128, 512:1024].astype(bf16)
        return carry

    lax.fori_loop(0, 4, up_terms_of, 0)
    net.begin(rs2d_sum(net, lambda a, b: up_terms.at[a, b], y, x, ups, up_grad), 2)
    net.begin(rs2d_sum(net, lambda a, b: up_later.at[b, a], x, y, ups_later, up_more), 5)
    net.pump(2, 5)
    net.pump(1)

    def down_terms_of(k, carry):
        rows = pl.ds(pl.multiple_of((k // 2) * 1024, 1024), 1024)
        columns = pl.ds(pl.multiple_of((k % 2) * 512, 512), 512)
        total = contract_rows(hidden[:, rows], cot_pair[:, columns])
        for i in range(4):
            down_terms[i, k] = total[0:512, i * 128 : (i + 1) * 128].astype(bf16)
            down_later[i, k] = total[512:1024, i * 128 : (i + 1) * 128].astype(bf16)
        return carry

    lax.fori_loop(0, 4, down_terms_of, 0)
    net.begin(rs2d_sum(net, lambda a, b: down_terms.at[a, b], x, y, downs, down_grad), 4)
    net.begin(rs2d_sum(net, lambda a, b: down_later.at[b, a], y, x, downs_later, down_more), 6)
    net.pump(4, 6)
    net.pump(2, 5)
    net.pump(1)
    for c in range(4):
        at = slice(c * 512, (c + 1) * 512)
        total = matmul(hidden[0:384, :], w_down[:, at])
        for i in range(4):
            part_out[i, :, at] = total[i * 96 : (i + 1) * 96].astype(bf16)
    net.pump(2, 5, 4)
    net.pump(1)
    net.begin(fore(), 3)
    for groups in ((5, 2, 6, 4, 1), (5, 2, 6, 4, 3)):
        net.pump(*groups)
    while any(net.todo[group] for group in (5, 2, 6, 4)):
        net.pump(5, 2, 6, 4)
    net.run()
    keeps = [
        net.local(up_grad, o_up.at[:, pl.ds(0, 512)]),
        net.local(up_more, o_up.at[:, pl.ds(512, 512)]),
        net.local(down_grad, o_down.at[pl.ds(0, 512), :]),
        net.local(down_more, o_down.at[pl.ds(512, 512), :]),
    ]
    for keep in keeps:
        keep.wait()


def device_of_block(place, block):
    d = block // 2
    return ((d // 8) * 8 + ((d // 2) % 4) * 2 + d % 2, (block % 2) * 4 + place.z)


def lanes_half(ref, which):
    n = ref.shape[-1] // 2
    return ref.at[:, pl.ds(which * n, n)]


def tail(
    grad_all, attended_all, query_all, window_all, lse_all, normed_all, query_w, keyval_w, out_w,
    tokens, out_rows, low, grad_mid, vecs, sums, up_sum,
    output, input_grad, query_grad, keyval_grad, out_grad, small_grad,
    grad, attended, query, window, lse, normed, w_query, w_keyval, w_out, tok,
    part_out, part_query, more_query, part_keyval, flow, scores, change, probs, slopes, d_keys, d_values,
    grad_query, part, ra, rb, pieces, rk, stage, rz, kv_rows, mine, six, tiles, part_small,
    small_own, small_in, kv_own, kv_in, query_own, out_own, keyval_sum, small_sum, *rest,
):
    place = Place()
    x, y, z = place.ring("x"), place.ring("y"), place.ring("z")
    hi = place.y // 2
    partner = y.others[0]
    block = ((place.y % 2) * 8 + place.x * 2 + place.core) * 2 + hi
    earlier = [device_of_block(place, (block + 32 - k) % 32) for k in (1, 2, 3, 4)]
    later = [device_of_block(place, (block + k) % 32) for k in (1, 2, 3, 4)]
    queries, queries_more, keyvals, outs, smalls, sem = (
        rest[:3], rest[3:6], rest[6:9], rest[9:12], rest[12:15], rest[15:],
    )
    net = Net(*sem)
    token_rows = pl.ds(pl.multiple_of(hi * 384 + place.z * 96, 96), 96)
    loads = {
        name: net.local(*pair)
        for name, pair in dict(
            grad=(grad_all, grad), attended=(attended_all, attended), out=(out_w, w_out),
            query=(query_all, query), window=(window_all, window), lse=(lse_all, lse),
            query_w=(query_w, w_query), normed=(normed_all, normed), keyval=(keyval_w, w_keyval),
            tok=(tokens.at[token_rows, :], tok),
        ).items()
    }
    greet([place.sibling()] + x.others + y.others + z.others + earlier + later)

    def y_first(own, slot, half):
        keep = net.local(own, slot(hi, z.p))
        swap = net.send(own, slot(hi, z.p), partner)
        net.spawn(ag_ring(net, z, lambda i: slot(hi, i), own, half=half))
        yield
        swap.wait_recv()
        net.spawn(ag_ring(net, z, lambda i: slot(1 - hi, i), slot(1 - hi, z.p), half=half))
        keep.wait()

    def z_first(own, slot, half):
        keep = net.local(own, slot(hi, z.p))
        swaps = [net.send(own, slot(hi, z.p), partner)]

        def have(i):
            swaps.append(net.send(slot(hi, i), slot(hi, i), partner))

        yield from ag_ring(net, z, lambda i: slot(hi, i), own, have, half)
        yield
        keep.wait()
        for swap in swaps:
            swap.wait_recv()

    net.pump(5, 1)
    net.begin(y_first(out_rows, lambda a, b: output.at[a, b], rows_half), 4)
    loads["grad"].wait()
    loads["attended"].wait()
    for n in range(4):
        total = contract_rows(attended[...], grad[:, n * 512 : (n + 1) * 512]).astype(bf16)
        for i in range(4):
            for which in range(2):
                part_out[i % 2, which * 2 + n // 2, (n % 2) * 2 + i // 2] = total[
                    which * 256 : (which + 1) * 256, i * 128 : (i + 1) * 128
                ]
    net.begin(rs2d_direct(net, place, part_out, "xy", outs, out_own), 2)
    loads["out"].wait()
    whole = contract_cols(grad[...], w_out[...]).astype(bf16)
    for i in range(4):
        for h in range(4):
            flow[i, h * 96 : (h + 1) * 96, :] = whole[
                i * 96 : (i + 1) * 96, h * 128 : (h + 1) * 128
            ]
    d_keys[...] = jnp.zeros_like(d_keys)
    d_values[...] = jnp.zeros_like(d_values)
    for name in ("query", "window", "lse", "query_w"):
        loads[name].wait()
    scale = 1.0 / math.sqrt(HD)
    lane = lax.broadcasted_iota(jnp.int32, (384, 128), 1)
    last = 1536 + lax.broadcasted_iota(jnp.int32, (32, 384), 1) % 96
    key = lax.broadcasted_iota(jnp.int32, (32, 384), 0)

    def attend(i):
        reach = pl.ds(pl.multiple_of(i * 96, 32), 1632)
        rows = pl.ds(pl.multiple_of(i * 96, 32), 96)
        for h in range(4):
            at = pl.ds(h * 96, 96)
            product = flow[i, at, :].astype(f32) * attended[
                rows, h * 128 : (h + 1) * 128
            ].astype(f32)
            lse[i, at, :] = jnp.where(
                lane[:96] == 0, lse[i, at, :], jnp.sum(product, axis=-1, keepdims=True)
            )
        across = jnp.transpose(lse[i])
        total, delta = across[0:1, :], across[1:2, :]
        first = low[pl.ds(i, 1), :]
        scores[...] = contract_cols(window[reach, 0:128], query[i])
        change[...] = contract_cols(window[reach, 128:256], flow[i])

        def soften(c, carry):
            at = pl.ds(pl.multiple_of(c * 32, 32), 32)
            where = key + c * 32
            some = jnp.where(
                (where >= first) & (where <= last), scores[at, :] * scale - total, NEG
            )
            some = jnp.exp(some)
            probs[at, :] = some.astype(bf16)
            slopes[at, :] = (some * (change[at, :] - delta)).astype(bf16)
            return carry

        lax.fori_loop(0, 51, soften, 0, unroll=3)
        d_values[reach, :] += matmul(probs[...], flow[i])
        d_keys[reach, :] += matmul(slopes[...], query[i])
        turned = jnp.transpose(contract_rows(window[reach, 0:128], slopes[...])) * scale
        for h in range(4):
            grad_query[rows, h * 128 : (h + 1) * 128] = turned[h * 96 : (h + 1) * 96].astype(bf16)
        for n in range(4):
            columns = slice(n * 512, (n + 1) * 512)
            part[i, :, columns] = contract_cols(grad_query[rows, :], w_query[columns, :]).astype(bf16)

    attend(z.across)
    a0 = net.send(rows_half(part.at[z.across], 0), ra.at[0], z.plus)
    a1 = net.send(rows_half(part.at[z.across], 1), ra.at[1], z.minus)
    net.pump(2)
    attend(z.after)
    after = part.at[z.after]
    b0 = net.send(rows_half(after, 1), rows_half(rb.at[0], 1), z.plus)
    net.pump(4)
    attend(z.before)
    before = part.at[z.before]
    b2 = net.send(rows_half(before, 0), rows_half(rb.at[1], 0), z.minus)
    a0.wait_recv()
    add_into(ra.at[0], rows_half(after, 0))
    b1 = net.send(ra.at[0], rows_half(rb.at[0], 0), z.plus)
    a1.wait_recv()
    add_into(ra.at[1], rows_half(before, 1))
    b3 = net.send(ra.at[1], rows_half(rb.at[1], 1), z.minus)
    attend(z.p)
    for j in range(5):
        at = slice(j * 384, (j + 1) * 384)
        pieces[j, :, 0:128] = (d_keys[at, :] * scale).astype(bf16)
        pieces[j, :, 128:256] = d_values[at, :].astype(bf16)

    def keys_values():
        sent = [net.send(pieces.at[4 - k], rk.at[k - 1], earlier[k - 1]) for k in (1, 2, 3, 4)]
        yield
        for copy in sent:
            copy.wait_recv()
        for i in range(4):
            at = pl.ds(i * 96, 96)
            add_into(pieces.at[4, at], *[rk.at[k, at] for k in range(4)], out=stage.at[i])
        sent = [
            net.send(stage.at[pos], rz.at[k], dev)
            for k, (pos, dev) in enumerate(zip((z.across, z.after, z.before), z.others))
        ]
        yield
        for copy in sent:
            copy.wait_recv()
        add_into(stage.at[place.z], *[rz.at[k] for k in range(3)], out=kv_rows)

    s_kv = net.begin(keys_values(), 1)
    loads["normed"].wait()
    for n in range(4):
        total = contract_rows(normed[:, n * 512 : (n + 1) * 512], grad_query[...]).astype(bf16)
        for i in range(4):
            for which in range(2):
                home = (i % 2, which * 2 + n // 2, (n % 2) * 2 + i // 2)
                columns = slice(which * 256, (which + 1) * 256)
                part_query[home] = total[i * 128 : i * 128 + 64, columns]
                more_query[home] = total[i * 128 + 64 : (i + 1) * 128, columns]
    net.begin(
        rs2d_direct(net, place, part_query, "xy", queries, query_own.at[pl.ds(0, 64)]), 3
    )
    net.begin(
        rs2d_direct(net, place, more_query, "yx", queries_more, query_own.at[pl.ds(64, 64)]), 3
    )
    net.pump(2)
    net.pump(1)
    net.pump(3)
    net.pump(4)
    loads["keyval"].wait()
    loads["tok"].wait()
    net.until((1, s_kv))
    quarter = pl.ds(pl.multiple_of(place.z * 96, 96), 96)
    for n in range(4):
        total = contract_rows(normed[quarter, n * 512 : (n + 1) * 512], kv_rows[...]).astype(bf16)
        for i in range(4):
            for which in range(2):
                part_keyval[i % 2, which * 2 + n // 2, (n % 2) * 2 + i // 2] = total[
                    i * 128 : (i + 1) * 128, :
                ]

    def keyval():
        yield from rs2d_direct(net, place, part_keyval, "xy", keyvals, kv_own)
        sent = [net.send(kv_own, kv_in.at[k], dev) for k, dev in enumerate(z.others)]
        yield
        for copy in sent:
            copy.wait_recv()
        add_into(kv_own, kv_in.at[0], kv_in.at[1], kv_in.at[2], out=keyval_sum)

    net.begin(keyval(), 7)
    for copy in (b0, b1, b2, b3):
        copy.wait_recv()
    six[...] = jnp.zeros_like(six)

    def norm_back(at):
        grad_norm = (
            part[place.z, at, :].astype(f32)
            + rb[0, at, :].astype(f32)
            + rb[1, at, :].astype(f32)
            + contract_cols(kv_rows[at, :], w_keyval[...])
        )
        center, inv = spread(tok[at, :].astype(f32))
        norm = center * inv
        down = grad_norm * vecs[0:1, :]
        mine[at, :] = (
            grad_mid[at, :]
            + inv
            * (
                down
                - jnp.mean(down, axis=-1, keepdims=True)
                - norm * jnp.mean(down * norm, axis=-1, keepdims=True)
            )
        ).astype(bf16)
        six[0:1, :] += jnp.sum(grad_norm * norm, axis=0, keepdims=True)
        six[1:2, :] += jnp.sum(grad_norm, axis=0, keepdims=True)

    for i in range(2):
        norm_back(pl.ds(i * 48, 48))
    top, bottom = pl.ds(0, 48), pl.ds(48, 48)
    net.begin(y_first(mine.at[top], lambda a, b: input_grad.at[a, b, top], lanes_half), 5)
    net.begin(z_first(mine.at[bottom], lambda a, b: input_grad.at[a, b, bottom], lanes_half), 5)
    six[2:3, :] = sums[2:3, :]
    six[3:4, :] = sums[0:1, :]
    six[4:5, :] = sums[1:2, :]
    six[5:6, :] = sums[3:4, :]
    bias_sum = jnp.sum(grad_query[...].astype(f32), axis=0, keepdims=True)
    value_sum = jnp.sum(kv_rows[:, 128:256].astype(f32), axis=0, keepdims=True)
    tiles[...] = jnp.zeros_like(tiles)
    for which in range(2):
        for h in range(2):
            at = (which * 2 + h) * 128
            tiles[which, 6 + h : 7 + h, :] = bias_sum[:, at : at + 128]
        for r in range(8):
            at = which * 1024 + r * 128
            tiles[which, 8 + r : 9 + r, :] = up_sum[0:1, at : at + 128]
    tiles[2, 6:7, :] = value_sum
    lane = lax.broadcasted_iota(jnp.int32, (16, 128), 1)

    def turn(tile, shift):
        shift = shift % 128
        return pltpu.roll(tile, shift, 1) if shift else tile

    for d in range(16):
        values = jnp.where((lane >= 8) & (lane < 16), turn(tiles[2], 136 - d * 8), 0.0)
        for which in range(2):
            piece = jnp.where(lane < 8, turn(tiles[which], 128 - d * 8), values)
            home = (d % 2, which * 2 + d // 8, (d // 2) % 4)
            part_small[home + (slice(6, 16),)] = piece[6:16]
            part_small[home + (slice(0, 6),)] = six[0:6, d * 128 : (d + 1) * 128]

    def small():
        yield from rs2d_direct(net, place, part_small, "xy", smalls, small_own)
        sent = [net.send(small_own, small_in.at[k], dev) for k, dev in enumerate(z.others)]
        yield
        for copy in sent:
            copy.wait_recv()
        total = small_own[...]
        whole = total + small_in[0] + small_in[1] + small_in[2]
        row = lax.broadcasted_iota(jnp.int32, (16, 128), 0)
        total = jnp.where((row < 6) | ((row == 6) & (lane >= 8)), whole, total)
        small_sum[0:16, :] = total
        small_sum[16:24, :] = turn(total[0:8], 120)

    net.begin(small(), 7)
    net.pump(7)
    while any(net.todo.values()):
        for group in (5, 7, 3, 2, 4):
            net.pump(group)
    net.run()
    keeps = [
        net.local(*pair)
        for pair in (
            (query_own, query_grad), (out_own, out_grad), (keyval_sum, keyval_grad),
            (small_sum, small_grad),
        )
    ]
    for keep in keeps:
        keep.wait()


def leave_kernel(
    output, input_grad, small, query, keyval, out, up, down,
    o_output, o_input, o_gain_one, o_shift_one, o_query, o_query_b, o_keyval, o_value_b, o_out,
    o_out_b, o_gain_two, o_shift_two, o_up, o_up_b, o_down, o_down_b,
):
    o_output[...] = output[...]
    o_input[...] = input_grad[...].astype(f32)

    @pl.when(pl.program_id(0) == 0)
    def _():
        rows = (o_gain_one, o_shift_one, o_out_b, o_gain_two, o_shift_two, o_down_b)
        for i, row in enumerate(rows):
            row[...] = small[i]
        o_query_b[...] = small[6:8, 0:8]
        o_value_b[...] = small[22, 0:8]
        o_up_b[...] = small[8:16, 0:8]
        o_query[...] = query[...]
        o_keyval[...] = keyval[...]
        o_out[...] = out[...]
        o_up[...] = up[...]
        o_down[...] = down[...]


def leave(output, input_grad, *rest):
    rows = pl.BlockSpec((128, 2048), lambda i: (i, 0))

    def fixed(shape):
        return pl.BlockSpec(shape, lambda i: (0,) * len(shape))

    shapes = [(128,), (128,), (128, 256), (2, 8), (128, 256), (8,), (256, 128), (128,), (128,),
              (128,), (128, 1024), (8, 8), (1024, 128), (128,)]
    return pl.pallas_call(
        leave_kernel,
        grid=(6,),
        out_shape=[jax.ShapeDtypeStruct((768, 2048), bf16), jax.ShapeDtypeStruct((768, 2048), f32)]
        + [jax.ShapeDtypeStruct(shape, f32) for shape in shapes],
        in_specs=[rows, rows] + [fixed(array.shape) for array in rest],
        out_specs=[rows, rows] + [fixed(shape) for shape in shapes],
        compiler_params=pltpu.CompilerParams(vmem_limit_bytes=60 << 20),
        cost_estimate=pl.CostEstimate(flops=0, bytes_accessed=16 << 20, transcendentals=0),
        name="leave",
    )(output, input_grad, *rest)


def matmul(left, right):
    return jnp.dot(left, right, preferred_element_type=f32)


def contract_rows(left, right):
    return lax.dot_general(left, right, (((0,), (0,)), ((), ())), preferred_element_type=f32)


def contract_cols(left, right):
    return lax.dot_general(left, right, (((1,), (1,)), ((), ())), preferred_element_type=f32)


def body(
    tokens, cotangent, segments, attn_norm_gain, attn_norm_bias, query_weight, query_bias,
    kv_weight, value_bias, out_weight, out_bias, mlp_norm_gain, mlp_norm_bias, up_weight,
    up_bias, down_weight, down_bias,
):
    dp = lax.axis_index("dp")
    tensor = lax.axis_index("tensor")
    hi, z = tensor // 4, tensor % 4
    half, heads = 384, 4

    start = dp * 768 + hi * half
    key_seg = lax.dynamic_slice_in_dim(
        jnp.concatenate([jnp.full((4 * half,), -1, jnp.int32), segments]), start, 5 * half
    )
    query_seg = key_seg[4 * half :]
    (
        query_w, keyval_w, out_w, up_w, down_w, vectors, normed_one, query_rows, window, lse,
        attended, normed_two, middle,
    ) = kernel_call(
        front, "front", 0,
        [tokens, jnp.stack([key_seg[i * 96 : i * 96 + 1632] for i in range(4)]),
         query_seg[:, None], attn_norm_gain[None], attn_norm_bias[None], out_bias[None],
         mlp_norm_gain[None], mlp_norm_bias[None], down_bias[None], query_bias, value_bias[None],
         up_bias, query_weight, kv_weight, out_weight, up_weight, down_weight],
        [ANY, VM, VM] + [ANY] * 14,
        [((2048, 512), bf16), ((2048, 256), bf16), ((512, 2048), bf16), ((2048, 2048), bf16),
         ((2048, 2048), bf16), ((8, 2048), f32), ((384, 2048), bf16), ((4, 384, 128), bf16),
         ((5, 4, 96, 256), bf16), ((4, 384, 128), f32), ((4, 96, 512), bf16),
         ((4, 96, 2048), bf16), ((96, 2048), f32)],
        [ANY] * 5 + [VM] + [ANY] * 6 + [VM],
        [pltpu.VMEM((2048, 512), bf16), pltpu.VMEM((2048, 256), bf16), pltpu.VMEM((512, 2048), bf16),
         pltpu.VMEM((2, 16, 24, 128), f32), pltpu.VMEM((384, 2048), bf16),
         pltpu.VMEM((384, 2048), bf16), pltpu.VMEM((4, 384, 128), bf16),
         pltpu.VMEM((5, 4, 96, 256), bf16), pltpu.VMEM((1920, 256), bf16),
         pltpu.VMEM((4, 384, 128), f32), pltpu.VMEM((4, 96, 512), bf16),
         pltpu.VMEM((4, 96, 1632), f32),
         pltpu.VMEM((128, 256), f32), pltpu.VMEM((64, 256), f32), pltpu.VMEM((256, 128), f32),
         pltpu.VMEM((128, 1024), f32), pltpu.VMEM((1024, 128), f32),
         pltpu.VMEM((128, 256), bf16), pltpu.VMEM((64, 256), bf16), pltpu.VMEM((256, 128), bf16),
         pltpu.VMEM((128, 1024), bf16), pltpu.VMEM((1024, 128), bf16),
         pltpu.VMEM((384, 2048), f32), pltpu.VMEM((384, 1632), f32), pltpu.VMEM((384, 1632), bf16),
         pltpu.VMEM((384, 128), bf16), pltpu.VMEM((4, 96, 2048), bf16),
         pltpu.VMEM((2, 48, 2048), bf16), pltpu.VMEM((2, 96, 2048), bf16), pltpu.VMEM((96, 2048), bf16),
         pltpu.VMEM((6, 1, 128), f32), pltpu.VMEM((2, 8), f32), pltpu.VMEM((1, 8), f32),
         pltpu.VMEM((8, 8), f32), pltpu.VMEM((24, 128), f32)]
        + sems(256, 40),
    )
    V = pltpu.VMEM
    (
        out_rows, grad_middle, grad_attn, sums, up_bias_sum, up_grad, down_grad,
    ) = kernel_call(
        mid, "mid", 2,
        [normed_two.reshape(half, 2048), cotangent, up_w, down_w, vectors, middle],
        [ANY, ANY, ANY, ANY, VM, VM],
        [((96, 2048), bf16), ((96, 2048), f32), ((4, 96, 2048), bf16), ((8, 2048), f32),
         ((1, 2048), f32), ((128, 1024), f32), ((1024, 128), f32)],
        [VM, VM, ANY, VM, VM, ANY, ANY],
        [V((2048, 2048), bf16), V((2048, 2048), bf16), V((384, 2048), bf16), V((384, 2048), bf16),
         V((768, 1024), bf16), V((768, 1024), bf16), V((384, 1024), bf16), V((384, 1024), bf16),
         V((768, 2048), bf16), V((768, 2048), bf16), V((4, 96, 2048), bf16),
         V((4, 96, 2048), bf16)]
        + [V((2, 48, 2048), bf16), V((2, 96, 2048), bf16)] * 2
        + [V((96, 2048), bf16)] + [V((4, 4, 128, 512), bf16), V((4, 4, 512, 128), bf16)] * 2
        + [V((128, 512), f32), V((512, 128), f32)] * 2
        + (ring_bufs((128, 512)) + ring_bufs((512, 128))) * 2 + sems(192, 16),
    )

    lows = jnp.sum(key_seg[None, :] < query_seg[:, None], axis=1, dtype=jnp.int32)
    lows = jnp.tile(lows.reshape(4, 96) - 96 * jnp.arange(4)[:, None], (1, heads))
    output, input_grad, query_grad, keyval_grad, out_grad, small_grad = kernel_call(
        tail, "tail", 3,
        [grad_attn.reshape(half, 2048), attended.reshape(half, 512), query_rows,
         window.reshape(5 * half, 256), lse, normed_one, query_w, keyval_w, out_w, tokens, out_rows,
         lows, grad_middle, vectors, sums, up_bias_sum],
        [ANY] * 11 + [VM] * 5,
        [((2, 4, 96, 2048), bf16), ((2, 4, 96, 2048), bf16), ((128, 256), f32), ((128, 256), f32),
         ((256, 128), f32), ((24, 128), f32)],
        [ANY] * 6,
        [V((384, 2048), bf16), V((384, 512), bf16), V((4, 384, 128), bf16), V((1920, 256), bf16),
         V((4, 384, 128), f32), V((384, 2048), bf16), V((2048, 512), bf16), V((2048, 256), bf16),
         V((512, 2048), bf16), V((96, 2048), bf16),
         V((2, 4, 4, 256, 128), bf16), V((2, 4, 4, 64, 256), bf16), V((2, 4, 4, 64, 256), bf16),
         V((2, 4, 4, 128, 256), bf16),
         V((4, 384, 128), bf16),
         V((1632, 384), f32), V((1632, 384), f32), V((1632, 384), bf16), V((1632, 384), bf16),
         V((1920, 128), f32), V((1920, 128), f32), V((384, 512), bf16), V((4, 96, 2048), bf16),
         V((2, 48, 2048), bf16), V((2, 96, 2048), bf16), V((5, 384, 256), bf16),
         V((4, 384, 256), bf16), V((4, 96, 256), bf16), V((3, 96, 256), bf16), V((96, 256), bf16),
         V((96, 2048), bf16), V((8, 2048), f32), V((3, 16, 128), f32), V((2, 4, 4, 16, 128), f32),
         V((16, 128), f32), V((3, 16, 128), f32), V((128, 256), f32),
         V((3, 128, 256), f32), V((128, 256), f32), V((256, 128), f32),
         V((128, 256), f32), V((24, 128), f32)]
        + direct_bufs((64, 256)) * 2 + direct_bufs((128, 256)) + direct_bufs((256, 128))
        + direct_bufs((16, 128), f32) + sems(128, 24),
    )
    return leave(
        output.reshape(768, 2048), input_grad.reshape(768, 2048), small_grad, query_grad,
        keyval_grad, out_grad, up_grad, down_grad,
    )


def solution(mesh):
    return jax.shard_map(
        body,
        mesh=mesh,
        in_specs=(
            P("dp", None), P("dp", None), P(), P("dp"), P("dp"), P("dp", "tensor"),
            P("tensor", "dp"), P("dp", None), P("dp"), P("tensor", "dp"), P("dp"), P("dp"),
            P("dp"), P("dp", "tensor"), P("tensor", "dp"), P("tensor", "dp"), P("dp"),
        ),
        out_specs=(
            P("dp", None), P("dp", None), P("dp"), P("dp"), P("dp", "tensor"),
            P("tensor", "dp"), P("dp", None), P("dp"), P("tensor", "dp"), P("dp"), P("dp"),
            P("dp"), P("dp", "tensor"), P("tensor", "dp"), P("tensor", "dp"), P("dp"),
        ),
        check_vma=False,
    )
```

```python
import functools
import math

import jax
import jax.numpy as jnp
from jax import lax
from jax.experimental import pallas as pl
from jax.experimental.pallas import tpu as pltpu
from jax.sharding import PartitionSpec as P

HD = 128
EPS = 1e-05
NEG = -1e30
MESH = pl.DeviceIdType.MESH
bf16 = jnp.bfloat16
f32 = jnp.float32


class Place:
    def __init__(self):
        dp = lax.axis_index("dp")
        tensor = lax.axis_index("tensor")
        self.core = dp % 2
        self.x = (dp // 2) % 4
        self.y = (tensor // 4) * 2 + dp // 8
        self.z = tensor % 4

    def dev(self, x=None, y=None, z=None, core=None):
        x = self.x if x is None else x
        y = self.y if y is None else y
        z = self.z if z is None else z
        core = self.core if core is None else core
        return ((y % 2) * 8 + x * 2 + core, (y // 2) * 4 + z)

    def sibling(self):
        return self.dev(core=1 - self.core)

    def ring(self, axis):
        return Ring(self, axis)


class Ring:
    def __init__(self, place, axis):
        self.p = getattr(place, axis)
        self.plus = place.dev(**{axis: (self.p + 1) % 4})
        self.minus = place.dev(**{axis: (self.p + 3) % 4})
        self.after = (self.p + 1) % 4
        self.before = (self.p + 3) % 4
        self.across = (self.p + 2) % 4
        self.others = [place.dev(**{axis: self.across}), self.plus, self.minus]
        self.sources = [self.across, self.before, self.after]


class Net:
    def __init__(self, ssem, rsem, lsem):
        self.ssem, self.rsem, self.lsem = ssem, rsem, lsem
        self.n = 0
        self.m = 0
        self.sent = []
        self.group = 0
        self.todo = {}

    def send(self, src, dst, dev):
        i = self.n
        self.n += 1
        copy = pltpu.make_async_remote_copy(
            src_ref=src,
            dst_ref=dst,
            send_sem=self.ssem.at[i],
            recv_sem=self.rsem.at[i],
            device_id=dev,
            device_id_type=MESH,
        )
        copy.start()
        self.sent.append(copy)
        return copy

    def local(self, src, dst):
        i = self.m
        self.m += 1
        copy = pltpu.make_async_copy(src, dst, self.lsem.at[i])
        copy.start()
        return copy

    def spawn(self, gen):
        place = self.todo.setdefault(self.group, [])
        place.append(gen)
        self.step(gen, place)

    def begin(self, gen, group=0):
        state = [False]

        def whole():
            yield from gen
            state[0] = True

        self.group = group
        self.spawn(whole())
        return state

    def step(self, gen, place):
        try:
            next(gen)
        except StopIteration:
            place.remove(gen)

    def pump(self, *groups):
        for group in groups:
            self.group = group
            place = self.todo.setdefault(group, [])
            for gen in list(place):
                self.step(gen, place)

    def until(self, *states):
        for group, state in states:
            while not state[0]:
                self.pump(group)

    def run(self, *gens):
        for gen in gens:
            self.spawn(gen)
        while any(self.todo.values()):
            self.pump(*self.todo)
        for copy in self.sent:
            copy.wait_send()


def greet(devices):
    barrier = pltpu.get_barrier_semaphore()
    for device in devices:
        pl.semaphore_signal(barrier, inc=1, device_id=device, device_id_type=MESH)
    pl.semaphore_wait(barrier, len(devices))


def rows_half(ref, which):
    n = ref.shape[-2] // 2
    if len(ref.shape) == 2:
        return ref.at[pl.ds(which * n, n), :]
    return ref.at[:, pl.ds(which * n, n), :]


def lane_step(shape):
    return max(16, min(shape[0], 32768 // shape[1]))


def over_rows(rows, step, fn):
    def one(i, carry):
        fn(pl.ds(pl.multiple_of(i * step, step), step))
        return carry

    lax.fori_loop(0, rows // step, one, 0)


def add_into(dst, *srcs, out=None):
    out = dst if out is None else out
    rows, step = dst.shape[0], lane_step(dst.shape)
    if rows % step:
        step = 16 if rows % 16 == 0 else rows

    def one(at):
        total = dst[at, :].astype(f32)
        for src in srcs:
            total = total + src[at, :].astype(f32)
        out[at, :] = total.astype(out.dtype)

    over_rows(rows, step, one)


def ag_ring(net, ring, slot, own, have=None, half=rows_half):
    have = have or (lambda pos: None)
    c0 = net.send(own, slot(ring.p), ring.plus)
    c1 = net.send(own, slot(ring.p), ring.minus)
    yield
    c0.wait_recv()
    one = half(slot(ring.before), 0)
    c2 = net.send(one, one, ring.plus)
    have(ring.before)
    c1.wait_recv()
    two = half(slot(ring.after), 1)
    c3 = net.send(two, two, ring.minus)
    have(ring.after)
    yield
    c2.wait_recv()
    c3.wait_recv()
    have(ring.across)


def ag2d(net, place, own, slot, first, second):
    sib = place.sibling()
    pairs = []

    def give(a, b, src=None):
        ref = slot(a, b)
        pairs.append(net.send(ref if src is None else src, ref, sib))

    def column(a, src):
        return ag_ring(net, second, lambda b: slot(a, b), src, lambda b: give(a, b))

    def main():
        keep = net.local(own, slot(first.p, second.p))
        c0 = net.send(own, slot(first.p, second.p), first.plus)
        c1 = net.send(own, slot(first.p, second.p), first.minus)
        yield
        net.spawn(column(first.p, own))
        give(first.p, second.p, own)
        c0.wait_recv()
        one = rows_half(slot(first.before, second.p), 0)
        c2 = net.send(one, one, first.plus)
        net.spawn(column(first.before, slot(first.before, second.p)))
        c1.wait_recv()
        two = rows_half(slot(first.after, second.p), 1)
        c3 = net.send(two, two, first.minus)
        net.spawn(column(first.after, slot(first.after, second.p)))
        give(first.before, second.p)
        give(first.after, second.p)
        yield
        c2.wait_recv()
        c3.wait_recv()
        net.spawn(column(first.across, slot(first.across, second.p)))
        give(first.across, second.p)
        keep.wait()
        while len(pairs) < 16:
            yield
        for pair in pairs:
            pair.wait_recv()

    return main()


def ag2d_direct(net, place, own, slot, first, second):
    sib = place.sibling()
    pairs = []

    def give(a, b, src=None):
        ref = slot(a, b)
        pairs.append(net.send(ref if src is None else src, ref, sib))

    def column(a, src):
        return [net.send(src, slot(a, second.p), dev) for dev in second.others]

    keep = net.local(own, slot(first.p, second.p))
    rows = [net.send(own, slot(first.p, second.p), dev) for dev in first.others]
    columns = [(first.p, column(first.p, own))]
    give(first.p, second.p, own)
    yield
    for a, copy in zip(first.sources, rows):
        copy.wait_recv()
        columns.append((a, column(a, slot(a, second.p))))
        give(a, second.p)
    yield
    for a, copies in columns:
        for b, copy in zip(second.sources, copies):
            copy.wait_recv()
            give(a, b)
    yield
    keep.wait()
    for pair in pairs:
        pair.wait_recv()


def rs_ring(net, ring, src, ra, rb, done):
    across, after, before = src(ring.across), src(ring.after), src(ring.before)
    a0 = net.send(rows_half(across, 0), ra(0), ring.plus)
    a1 = net.send(rows_half(across, 1), ra(1), ring.minus)
    b0 = net.send(rows_half(after, 1), rows_half(rb(0), 1), ring.plus)
    b1 = net.send(rows_half(before, 0), rows_half(rb(1), 0), ring.minus)
    yield
    a0.wait_recv()
    add_into(ra(0), rows_half(after, 0))
    b2 = net.send(ra(0), rows_half(rb(0), 0), ring.plus)
    a1.wait_recv()
    add_into(ra(1), rows_half(before, 1))
    b3 = net.send(ra(1), rows_half(rb(1), 1), ring.minus)
    yield
    for copy in (b0, b1, b2, b3):
        copy.wait_recv()
    done(src(ring.p), rb(0), rb(1))


def rs2d_direct(net, place, part, order, bufs, out):
    rv, ra, rb = bufs
    first, second = (place.ring(axis) for axis in order)
    own = part.at[place.core]

    def along(a):
        return own.at[:, a] if order == "xy" else own.at[a]

    def one(a, b):
        return own.at[b, a] if order == "xy" else own.at[a, b]

    pair = net.send(part.at[1 - place.core], rv, place.sibling())
    yield
    pair.wait_recv()

    def add_pair(i, carry):
        add_into(own.at[i // 4, i % 4], rv.at[i // 4, i % 4])
        return carry

    lax.fori_loop(0, 16, add_pair, 0)
    sent = [
        net.send(along(pos), ra.at[k], dev)
        for k, (pos, dev) in enumerate(zip((first.across, first.after, first.before), first.others))
    ]
    yield
    for copy in sent:
        copy.wait_recv()
    for b in range(4):
        add_into(one(first.p, b), ra.at[0, b], ra.at[1, b], ra.at[2, b])
    sent = [
        net.send(one(first.p, pos), rb.at[k], dev)
        for k, (pos, dev) in enumerate(
            zip((second.across, second.after, second.before), second.others)
        )
    ]
    yield
    for copy in sent:
        copy.wait_recv()
    add_into(one(first.p, second.p), rb.at[0], rb.at[1], rb.at[2], out=out)


def direct_bufs(shape, dtype=bf16):
    return [
        pltpu.VMEM((4, 4) + shape, dtype),
        pltpu.VMEM((3, 4) + shape, dtype),
        pltpu.VMEM((3,) + shape, dtype),
    ]


def rs2d_sum(net, r0, first, second, bufs, out):
    ra, rb, r1, sa, sb = bufs
    firsts = (first.across, first.after, first.before, first.p)
    seconds = (second.across, second.after, second.before, second.p)

    def term(i, j):
        return r0(firsts[i], seconds[j])

    halves, wholes = {}, {}
    for j in range(4):
        halves[0, j] = net.send(rows_half(term(0, j), 0), ra.at[0, j], first.plus)
        halves[1, j] = net.send(rows_half(term(0, j), 1), ra.at[1, j], first.minus)
    yield
    for j in range(4):
        wholes[0, j] = net.send(rows_half(term(1, j), 1), rows_half(rb.at[0, j], 1), first.plus)
        wholes[1, j] = net.send(rows_half(term(2, j), 0), rows_half(rb.at[1, j], 0), first.minus)
    yield
    for j in range(4):
        halves[0, j].wait_recv()
        add_into(ra.at[0, j], rows_half(term(1, j), 0))
        wholes[2, j] = net.send(ra.at[0, j], rows_half(rb.at[0, j], 0), first.plus)
        halves[1, j].wait_recv()
        add_into(ra.at[1, j], rows_half(term(2, j), 1))
        wholes[3, j] = net.send(ra.at[1, j], rows_half(rb.at[1, j], 1), first.minus)
        if j == 1:
            yield
    yield

    def settle(j):
        for k in range(4):
            wholes[k, j].wait_recv()
        add_into(term(3, j), rb.at[0, j], rb.at[1, j], out=r1.at[j])

    settle(0)
    a0 = net.send(rows_half(r1.at[0], 0), sa.at[0], second.plus)
    a1 = net.send(rows_half(r1.at[0], 1), sa.at[1], second.minus)
    settle(1)
    b0 = net.send(rows_half(r1.at[1], 1), rows_half(sb.at[0], 1), second.plus)
    yield
    settle(2)
    b1 = net.send(rows_half(r1.at[2], 0), rows_half(sb.at[1], 0), second.minus)
    settle(3)
    yield
    a0.wait_recv()
    add_into(sa.at[0], rows_half(r1.at[1], 0))
    b2 = net.send(sa.at[0], rows_half(sb.at[0], 0), second.plus)
    a1.wait_recv()
    add_into(sa.at[1], rows_half(r1.at[2], 1))
    b3 = net.send(sa.at[1], rows_half(sb.at[1], 1), second.minus)
    yield
    for copy in (b0, b1, b2, b3):
        copy.wait_recv()
    add_into(r1.at[3], sb.at[0], sb.at[1], out=out)


def ring_bufs(shape, dtype=bf16):
    rows, cols = shape
    half = (rows // 2, cols)
    return [
        pltpu.VMEM((2, 4) + half, dtype),
        pltpu.VMEM((2, 4) + shape, dtype),
        pltpu.VMEM((4,) + shape, dtype),
        pltpu.VMEM((2,) + half, dtype),
        pltpu.VMEM((2,) + shape, dtype),
    ]


def sems(count, local):
    return [
        pltpu.SemaphoreType.DMA((count,)),
        pltpu.SemaphoreType.DMA((count,)),
        pltpu.SemaphoreType.DMA((local,)),
    ]


ANY = pl.BlockSpec(memory_space=pl.ANY)
VM = pl.BlockSpec(memory_space=pltpu.VMEM)


def kernel_call(body, name, cid, ins, in_specs, outs, out_specs, scratch, nbytes=1 << 20):
    return pl.pallas_call(
        body,
        out_shape=[jax.ShapeDtypeStruct(s, d) for s, d in outs],
        in_specs=in_specs,
        out_specs=out_specs,
        scratch_shapes=scratch,
        compiler_params=pltpu.CompilerParams(
            collective_id=cid, has_side_effects=True, vmem_limit_bytes=58 << 20
        ),
        cost_estimate=pl.CostEstimate(flops=0, bytes_accessed=nbytes, transcendentals=0),
        name=name,
    )(*ins)


def block_of(x, y, core):
    return (y % 2) * 8 + x * 2 + core


def col_at(d):
    return pl.ds(pl.multiple_of(d * 128, 128), 128)


def row_at(start, size):
    return pl.ds(pl.multiple_of(start, size), size)


def at_query(ref, x, y, core):
    return ref.at[row_at(block_of(x, y, core) * 128, 128), row_at((y // 2) * 256, 256)]


def at_keyval(ref, x, y, core):
    return ref.at[row_at(block_of(x, y, core) * 128 + (y // 2) * 64, 64), :]


def at_out(ref, x, y, core):
    return ref.at[row_at((y // 2) * 256, 256), col_at(block_of(x, y, core))]


def at_up(ref, x, y, core):
    return ref.at[row_at(block_of(x, y, core) * 128, 128), row_at((y // 2) * 1024, 1024)]


def at_down(ref, x, y, core):
    return ref.at[row_at((y // 2) * 1024, 1024), col_at(block_of(x, y, core))]


def at_small(ref, x, y, core):
    return ref.at[y // 2, block_of(x, y, core)]


def gather(net, place, at, own, whole, order, how=ag2d):
    x, y = place.ring("x"), place.ring("y")
    if order == "xy":
        return how(net, place, own, lambda a, b: at(whole, a, b, place.core), x, y)
    return how(net, place, own, lambda a, b: at(whole, b, a, place.core), y, x)


def plane_peers(place):
    x, y = place.ring("x"), place.ring("y")
    return [place.sibling(), x.plus, x.minus, y.plus, y.minus]


def spread(values):
    center = values - jnp.mean(values, axis=-1, keepdims=True)
    return center, lax.rsqrt(jnp.mean(center * center, axis=-1, keepdims=True) + EPS)


def cast_into(dst, src):
    step = lane_step(dst.shape)
    step = step if dst.shape[0] % step == 0 else 16

    def one(at):
        dst[at, :] = src[at, :].astype(dst.dtype)

    over_rows(dst.shape[0], step, one)


def front(
    tokens, key_seg, query_seg, v0, v1, v2, v3, v4, v5, query_bias, value_bias, up_bias,
    query_w, keyval_w, out_w, up_w, down_w,
    o_query_w, o_keyval_w, o_out_w, g_up, g_down, vecs, o_normed, o_query, o_window, o_lse,
    o_attended, normed_two, middle,
    g_query, g_keyval, g_out, g_small, tok, normed, query, window, take, lse, attended, bias,
    f_query, f_keyval, f_out, f_up, f_down, b_query, b_keyval, b_out, b_up, b_down,
    unit, scores, weights, mixed, part, ra, rb, mine, rows6, short_q, short_v, short_u, small_own,
    *sem,
):
    place = Place()
    z = place.ring("z")
    hi = place.y // 2
    block = ((place.y % 2) * 8 + place.x * 2 + place.core) * 2 + hi
    earlier = [device_of_block(place, (block + 32 - k) % 32) for k in (1, 2, 3, 4)]
    later = [device_of_block(place, (block + k) % 32) for k in (1, 2, 3, 4)]
    net = Net(*sem)
    half_rows = pl.ds(pl.multiple_of(hi * 64, 64), 64)
    shorts = [net.local(v, rows6.at[i]) for i, v in enumerate((v0, v1, v2, v3, v4, v5))]
    shorts += [net.local(query_bias, short_q), net.local(value_bias, short_v), net.local(up_bias, short_u)]
    loads = [
        net.local(keyval_w.at[half_rows, :], f_keyval),
        net.local(query_w, f_query),
        net.local(out_w, f_out),
        net.local(tokens.at[pl.ds(pl.multiple_of(hi * 384, 384), 384), :], tok),
        net.local(up_w, f_up),
        net.local(down_w, f_down),
    ]
    x, y = place.ring("x"), place.ring("y")
    greet([place.sibling()] + x.others + y.others + z.others + earlier + later)
    for short in shorts:
        short.wait()

    def rounded(values):
        return values.astype(bf16).astype(f32)

    small_own[...] = jnp.zeros_like(small_own)
    for i in range(6):
        small_own[i : i + 1, :] = rounded(rows6[i])
    small_own[6:8, 0:8] = rounded(short_q[...])
    small_own[8:16, 0:8] = rounded(short_u[...])
    small_own[16:17, 0:8] = rounded(short_v[...])
    s_small = net.begin(gather(net, place, at_small, small_own, g_small, "yx", ag2d_direct), 1)
    loads[0].wait()
    cast_into(b_keyval, f_keyval)
    s_keyval = net.begin(gather(net, place, at_keyval, b_keyval, g_keyval, "xy", ag2d_direct), 1)
    loads[3].wait()

    def norm_some(at):
        center, inv = spread(tok[at, :].astype(f32))
        unit[at, :] = center * inv

    over_rows(192, 16, norm_some)
    net.pump(1)
    loads[1].wait()
    cast_into(b_query, f_query)
    s_query = net.begin(gather(net, place, at_query, b_query, g_query, "xy", ag2d_direct), 2)
    loads[2].wait()
    cast_into(b_out, f_out)
    s_out = net.begin(gather(net, place, at_out, b_out, g_out, "yx", ag2d_direct), 2)
    loads[4].wait()
    cast_into(b_up, f_up)
    loads[5].wait()
    cast_into(b_down, f_down)
    net.begin(gather(net, place, at_up, b_up, g_up, "xy"), 3)
    net.begin(gather(net, place, at_down, b_down, g_down, "yx"), 3)
    over_rows(192, 16, lambda at: norm_some(pl.ds(pl.multiple_of(at.start + 192, 16), 16)))
    net.pump(1)
    net.until((1, s_small), (1, s_keyval))

    for d in range(16):
        vecs[0:6, d * 128 : (d + 1) * 128] = g_small[0, d, 0:6, :]
    lane = lax.broadcasted_iota(jnp.int32, (8, 128), 1)

    def collect(which, rows):
        total = jnp.zeros((8, 128), f32)
        for d in range(16):
            piece = jnp.where(lane < 8, g_small[which, d, rows : rows + 8, :], 0.0)
            total = total + (pltpu.roll(piece, d * 8, 1) if d else piece)
        return total

    biases = []
    for which in range(2):
        ups = collect(which, 8)
        for r in range(8):
            at = which * 1024 + r * 128
            vecs[6:7, at : at + 128] = ups[r : r + 1, :]
        biases.append(collect(which, 0))
    query_b = [biases[0][6:7], biases[0][7:8], biases[1][6:7], biases[1][7:8]]
    value_b = collect(0, 16)[0:1]

    def apply_some(at):
        normed[at, :] = (unit[at, :] * vecs[0:1, :] + vecs[1:2, :]).astype(bf16)

    over_rows(384, 16, apply_some)
    kv = jnp.dot(normed[...], g_keyval[...], preferred_element_type=f32)
    kv = (kv + jnp.concatenate([jnp.zeros((1, 128), f32), value_b], 1)).astype(bf16)
    for i in range(4):
        window[4, i] = kv[i * 96 : (i + 1) * 96]

    def keys_values():
        own = window.at[4, place.z]
        sent = [net.send(own, window.at[4 - k, place.z], later[k - 1]) for k in (1, 2, 3, 4)]
        yield
        for copy in sent:
            copy.wait_recv()
        mine = window.at[pl.ds(0, 4), place.z]
        sent = [net.send(mine, mine, dev) for dev in z.others]
        yield
        for copy in sent:
            copy.wait_recv()

    s_window = net.begin(keys_values(), 1)
    net.pump(2)
    row = lax.broadcasted_iota(jnp.int32, (96, 1632), 0)
    column = lax.broadcasted_iota(jnp.int32, (96, 1632), 1)
    for i in range(4):
        same = query_seg[i * 96 : (i + 1) * 96, :] == key_seg[i : i + 1, :]
        bias[i] = jnp.where(same & (column <= row + 1536), 0.0, NEG)
    net.pump(1)
    net.pump(3)
    net.pump(2)
    net.until((2, s_query))
    for i in range(4):
        rows = jnp.dot(normed[i * 96 : (i + 1) * 96, :], g_query[...], preferred_element_type=f32)
        for h in range(4):
            query[i, h * 96 : (h + 1) * 96, :] = (
                rows[:, h * 128 : (h + 1) * 128] + query_b[h]
            ).astype(bf16)
    net.until((1, s_window), (2, s_out))
    keeps = [
        net.local(*pair)
        for pair in (
            (g_query, o_query_w), (g_keyval, o_keyval_w), (g_out, o_out_w), (normed, o_normed),
            (query, o_query), (window, o_window),
        )
    ]
    for j in range(5):
        for i in range(4):
            take[pl.ds((j * 4 + i) * 96, 96), :] = window[j, i]
    scale = 1.0 / math.sqrt(HD)

    def attend(i):
        reach = pl.ds(pl.multiple_of(i * 96, 32), 1632)
        scores[...] = lax.dot_general(
            query[i], take[reach, 0:128], (((1,), (1,)), ((), ())), preferred_element_type=f32
        )

        def soften(c, carry):
            at = pl.ds(pl.multiple_of(c * 16, 16), 16)
            mask = pl.ds(pl.multiple_of((c % 6) * 16, 16), 16)
            some = scores[at, :] * scale + bias[i, mask, :]
            top = jnp.max(some, axis=-1, keepdims=True)
            some = jnp.exp(some - top)
            total = jnp.sum(some, axis=-1, keepdims=True)
            weights[at, :] = (some * (1.0 / total)).astype(bf16)
            lse[i, at, :] = jnp.broadcast_to(top + jnp.log(total), (16, 128))
            return carry

        lax.fori_loop(0, 24, soften, 0, unroll=8)
        mixed[...] = jnp.dot(
            weights[...], take[reach, 128:256], preferred_element_type=f32
        ).astype(bf16)
        for h in range(4):
            attended[i, :, h * 128 : (h + 1) * 128] = mixed[h * 96 : (h + 1) * 96, :]
        for n in range(4):
            columns = slice(n * 512, (n + 1) * 512)
            part[i, :, columns] = jnp.dot(
                attended[i], g_out[:, columns], preferred_element_type=f32
            ).astype(bf16)

    attend(z.across)
    a0 = net.send(rows_half(part.at[z.across], 0), ra.at[0], z.plus)
    a1 = net.send(rows_half(part.at[z.across], 1), ra.at[1], z.minus)
    attend(z.after)
    after = part.at[z.after]
    b0 = net.send(rows_half(after, 1), rows_half(rb.at[0], 1), z.plus)
    attend(z.before)
    before = part.at[z.before]
    b2 = net.send(rows_half(before, 0), rows_half(rb.at[1], 0), z.minus)
    a0.wait_recv()
    add_into(ra.at[0], rows_half(after, 0))
    b1 = net.send(ra.at[0], rows_half(rb.at[0], 0), z.plus)
    a1.wait_recv()
    add_into(ra.at[1], rows_half(before, 1))
    b3 = net.send(ra.at[1], rows_half(rb.at[1], 1), z.minus)
    net.pump(3)
    attend(z.p)
    keeps += [net.local(attended, o_attended), net.local(lse, o_lse)]

    def residual(at):
        mid = (
            tok[pl.ds(pl.multiple_of(place.z * 96 + at.start, 16), 16), :].astype(f32)
            + part[place.z, at, :].astype(f32)
            + rb[0, at, :].astype(f32)
            + rb[1, at, :].astype(f32)
            + vecs[2:3, :]
        )
        middle[at, :] = mid
        center, inv = spread(mid)
        mine[at, :] = (center * inv * vecs[3:4, :] + vecs[4:5, :]).astype(bf16)

    for which, copies in ((0, (b1, b2)), (1, (b0, b3))):
        for copy in copies:
            copy.wait_recv()
        at = pl.ds(which * 48, 48)
        over_rows(48, 16, lambda r: residual(pl.ds(pl.multiple_of(r.start + which * 48, 16), 16)))
        keeps.append(net.local(mine.at[at], normed_two.at[z.p, at]))
        net.begin(
            ag_ring(net, z, lambda i, at=at: normed_two.at[i, at], mine.at[at], half=lanes_half), 1
        )
    net.pump(3)
    net.pump(1)
    while any(net.todo[group] for group in (1, 3)):
        net.pump(3, 1)
    net.run()
    for keep in keeps:
        keep.wait()


def mid(
    normed_all, cotangent, up_w, down_w, vecs, middle,
    out_rows, grad_mid, grad_all, sums, up_sum, o_up, o_down,
    w_up, w_down, normed, cot, normed_pair, cot_pair, normed_sib, cot_sib, hidden, slope,
    part_norm, part_out, ra, rb, rc, rd, mine, up_terms, down_terms, up_later, down_later, up_grad, down_grad, up_more, down_more,
    *rest,
):
    place = Place()
    x, y, z = place.ring("x"), place.ring("y"), place.ring("z")
    hi = place.y // 2
    sib = place.sibling()
    ups, downs, ups_later, downs_later, sem = rest[:5], rest[5:10], rest[10:15], rest[15:20], rest[20:]
    net = Net(*sem)
    load_normed = net.local(normed_all, normed)
    load_cot = net.local(cotangent.at[pl.ds(pl.multiple_of(hi * 384, 384), 384), :], cot)
    load_up, load_down = [], []
    for c in range(4):
        at = pl.ds(c * 512, 512)
        load_up.append(net.local(up_w.at[:, at], w_up.at[:, at]))
        load_down.append(net.local(down_w.at[at, :], w_down.at[at, :]))
    greet([sib, x.plus, x.minus, y.plus, y.minus, z.plus, z.minus])

    def split(full, pair, other):
        for m in range(8):
            at = pl.ds(m * 128, 128)
            pair[0:384, at] = full[:, col_at(2 * m + place.core)]
            other[:, at] = full[:, col_at(2 * m + 1 - place.core)]
        return net.send(other, pair.at[pl.ds(384, 384), :], sib)

    load_normed.wait()
    swaps = [split(normed, normed_pair, normed_sib)]
    load_cot.wait()
    swaps.append(split(cot, cot_pair, cot_sib))
    for c in range(4):
        at = pl.ds(c * 512, 512)
        load_up[c].wait()
        load_down[c].wait()

        def some(r, carry):
            rows = pl.ds(pl.multiple_of(r * 192, 64), 192)
            upward = matmul(normed[rows, :], w_up[:, at]) + vecs[6:7, at]
            flow = contract_cols(cot[rows, :], w_down[at, :])
            square = upward * upward
            curve = jnp.tanh(0.7978845608028654 * upward * (1.0 + 0.044715 * square))
            hidden[rows, at] = (0.5 * upward * (1.0 + curve)).astype(bf16)
            steep = 0.5 * (1.0 + curve) + 0.5 * upward * (1.0 - curve * curve) * (
                0.7978845608028654 * (1.0 + 3.0 * 0.044715 * square)
            )
            slope[rows, at] = (flow * steep).astype(bf16)
            return carry

        lax.fori_loop(0, 2, some, 0)
        up_sum[0:1, at] = jnp.sum(slope[0:384, at].astype(f32), axis=0, keepdims=True)
        for pair in (hidden, slope):
            swaps.append(net.send(pair.at[pl.ds(0, 384), at], pair.at[pl.ds(384, 384), at], sib))

    def back():
        def done(own, one, two):
            sums[...] = jnp.zeros_like(sums)

            def some(at):
                grad = own[at, :].astype(f32) + one[at, :].astype(f32) + two[at, :].astype(f32)
                center, inv = spread(middle[at, :])
                norm = center * inv
                flow = grad * vecs[3:4, :]
                top = cot[pl.ds(pl.multiple_of(place.z * 96 + at.start, 16), 16), :].astype(f32)
                low = top + inv * (
                    flow
                    - jnp.mean(flow, axis=-1, keepdims=True)
                    - norm * jnp.mean(flow * norm, axis=-1, keepdims=True)
                )
                grad_mid[at, :] = low
                low = low.astype(bf16)
                mine[at, :] = low
                sums[0:1, :] += jnp.sum(grad * norm, axis=0, keepdims=True)
                sums[1:2, :] += jnp.sum(grad, axis=0, keepdims=True)
                sums[2:3, :] += jnp.sum(low.astype(f32), axis=0, keepdims=True)
                sums[3:4, :] += jnp.sum(top, axis=0, keepdims=True)

            for which in range(2):
                over_rows(48, 16, lambda r: some(pl.ds(pl.multiple_of(r.start + which * 48, 16), 16)))
                at = pl.ds(which * 48, 48)
                last.append(net.local(mine.at[at], grad_all.at[z.p, at]))
                net.spawn(
                    ag_ring(
                        net, z, lambda i, at=at: grad_all.at[i, at], mine.at[at], half=lanes_half
                    )
                )

        last = []
        yield from rs_ring(
            net, z, lambda i: part_norm.at[i], lambda i: ra.at[i], lambda i: rb.at[i], done
        )
        for keep in last:
            keep.wait()

    def fore():
        def done(own, one, two):
            def some(at):
                out_rows[at, :] = (
                    middle[at, :]
                    + own[at, :].astype(f32)
                    + one[at, :].astype(f32)
                    + two[at, :].astype(f32)
                    + vecs[5:6, :]
                ).astype(bf16)

            over_rows(96, 16, some)

        yield from rs_ring(
            net, z, lambda i: part_out.at[i], lambda i: rc.at[i], lambda i: rd.at[i], done
        )

    for copy in swaps:
        copy.wait_recv()

    def up_terms_of(k, carry):
        rows = pl.ds(pl.multiple_of((k % 2) * 512, 512), 512)
        columns = pl.ds(pl.multiple_of((k // 2) * 1024, 1024), 1024)
        total = contract_rows(normed_pair[:, rows], slope[:, columns])
        for i in range(4):
            up_terms[k, i] = total[i * 128 : (i + 1) * 128, 0:512].astype(bf16)
            up_later[k, i] = total[i * 128 : (i + 1) * 128, 512:1024].astype(bf16)
        return carry

    lax.fori_loop(0, 4, up_terms_of, 0)
    net.begin(rs2d_sum(net, lambda a, b: up_terms.at[a, b], y, x, ups, up_grad), 2)
    net.begin(rs2d_sum(net, lambda a, b: up_later.at[b, a], x, y, ups_later, up_more), 5)
    net.pump(2, 5)
    for c in range(4):
        at = slice(c * 512, (c + 1) * 512)
        total = contract_cols(slope[0:384, :], w_up[at, :])
        for i in range(4):
            part_norm[i, :, at] = total[i * 96 : (i + 1) * 96].astype(bf16)

    net.begin(back(), 1)

    def down_terms_of(k, carry):
        rows = pl.ds(pl.multiple_of((k // 2) * 1024, 1024), 1024)
        columns = pl.ds(pl.multiple_of((k % 2) * 512, 512), 512)
        total = contract_rows(hidden[:, rows], cot_pair[:, columns])
        for i in range(4):
            down_terms[i, k] = total[0:512, i * 128 : (i + 1) * 128].astype(bf16)
            down_later[i, k] = total[512:1024, i * 128 : (i + 1) * 128].astype(bf16)
        return carry

    lax.fori_loop(0, 4, down_terms_of, 0)
    net.begin(rs2d_sum(net, lambda a, b: down_terms.at[a, b], x, y, downs, down_grad), 4)
    net.begin(rs2d_sum(net, lambda a, b: down_later.at[b, a], y, x, downs_later, down_more), 6)
    net.pump(4, 6)
    net.pump(2, 5)
    net.pump(1)
    for c in range(4):
        at = slice(c * 512, (c + 1) * 512)
        total = matmul(hidden[0:384, :], w_down[:, at])
        for i in range(4):
            part_out[i, :, at] = total[i * 96 : (i + 1) * 96].astype(bf16)
    net.pump(2, 5, 4)
    net.pump(1)
    net.begin(fore(), 3)
    for groups in ((5, 2, 6, 4, 1), (5, 2, 6, 4, 3)):
        net.pump(*groups)
    while any(net.todo[group] for group in (5, 2, 6, 4)):
        net.pump(5, 2, 6, 4)
    net.run()
    keeps = [
        net.local(up_grad, o_up.at[:, pl.ds(0, 512)]),
        net.local(up_more, o_up.at[:, pl.ds(512, 512)]),
        net.local(down_grad, o_down.at[pl.ds(0, 512), :]),
        net.local(down_more, o_down.at[pl.ds(512, 512), :]),
    ]
    for keep in keeps:
        keep.wait()


def device_of_block(place, block):
    d = block // 2
    return ((d // 8) * 8 + ((d // 2) % 4) * 2 + d % 2, (block % 2) * 4 + place.z)


def lanes_half(ref, which):
    n = ref.shape[-1] // 2
    return ref.at[:, pl.ds(which * n, n)]


def tail(
    grad_all, attended_all, query_all, window_all, lse_all, normed_all, query_w, keyval_w, out_w,
    tokens, out_rows, low, grad_mid, vecs, sums, up_sum,
    output, input_grad, query_grad, keyval_grad, out_grad, small_grad,
    grad, attended, query, window, lse, normed, w_query, w_keyval, w_out, tok,
    part_out, part_query, more_query, part_keyval, flow, scores, change, probs, slopes, d_keys, d_values,
    grad_query, part, ra, rb, pieces, rk, stage, rz, kv_rows, mine, six, tiles, part_small,
    small_own, small_in, kv_own, kv_in, query_own, out_own, keyval_sum, small_sum, *rest,
):
    place = Place()
    x, y, z = place.ring("x"), place.ring("y"), place.ring("z")
    hi = place.y // 2
    partner = y.others[0]
    block = ((place.y % 2) * 8 + place.x * 2 + place.core) * 2 + hi
    earlier = [device_of_block(place, (block + 32 - k) % 32) for k in (1, 2, 3, 4)]
    later = [device_of_block(place, (block + k) % 32) for k in (1, 2, 3, 4)]
    queries, queries_more, keyvals, outs, smalls, sem = (
        rest[:3], rest[3:6], rest[6:9], rest[9:12], rest[12:15], rest[15:],
    )
    net = Net(*sem)
    token_rows = pl.ds(pl.multiple_of(hi * 384 + place.z * 96, 96), 96)
    loads = {
        name: net.local(*pair)
        for name, pair in dict(
            grad=(grad_all, grad), attended=(attended_all, attended), out=(out_w, w_out),
            query=(query_all, query), window=(window_all, window), lse=(lse_all, lse),
            query_w=(query_w, w_query), normed=(normed_all, normed), keyval=(keyval_w, w_keyval),
            tok=(tokens.at[token_rows, :], tok),
        ).items()
    }
    twins = [place.dev(y=y.across, z=(place.z + k) % 4) for k in (1, 2, 3)]
    greet([place.sibling()] + x.others + y.others + z.others + twins + earlier + later)

    def y_first(own, slot, half):
        keep = net.local(own, slot(hi, z.p))
        swap = net.send(own, slot(hi, z.p), partner)
        net.spawn(ag_ring(net, z, lambda i: slot(hi, i), own, half=half))
        yield
        swap.wait_recv()
        net.spawn(ag_ring(net, z, lambda i: slot(1 - hi, i), slot(1 - hi, z.p), half=half))
        keep.wait()

    def z_first(own, slot, half):
        keep = net.local(own, slot(hi, z.p))
        swaps = [net.send(own, slot(hi, z.p), partner)]

        def have(i):
            swaps.append(net.send(slot(hi, i), slot(hi, i), partner))

        yield from ag_ring(net, z, lambda i: slot(hi, i), own, have, half)
        yield
        keep.wait()
        for swap in swaps:
            swap.wait_recv()

    net.pump(5, 1)
    top, bottom = pl.ds(0, 48), pl.ds(48, 48)
    net.begin(y_first(out_rows.at[top], lambda a, b: output.at[a, b, top], lanes_half), 4)
    net.begin(z_first(out_rows.at[bottom], lambda a, b: output.at[a, b, bottom], lanes_half), 8)
    loads["grad"].wait()
    loads["attended"].wait()
    for n in range(4):
        total = contract_rows(attended[...], grad[:, n * 512 : (n + 1) * 512]).astype(bf16)
        for i in range(4):
            for which in range(2):
                part_out[i % 2, which * 2 + n // 2, (n % 2) * 2 + i // 2] = total[
                    which * 256 : (which + 1) * 256, i * 128 : (i + 1) * 128
                ]
    net.begin(rs2d_direct(net, place, part_out, "xy", outs, out_own), 2)
    loads["out"].wait()
    whole = contract_cols(grad[...], w_out[...]).astype(bf16)
    for i in range(4):
        for h in range(4):
            flow[i, h * 96 : (h + 1) * 96, :] = whole[
                i * 96 : (i + 1) * 96, h * 128 : (h + 1) * 128
            ]
    d_keys[...] = jnp.zeros_like(d_keys)
    d_values[...] = jnp.zeros_like(d_values)
    for name in ("query", "window", "lse", "query_w"):
        loads[name].wait()
    scale = 1.0 / math.sqrt(HD)
    lane = lax.broadcasted_iota(jnp.int32, (384, 128), 1)
    last = 1536 + lax.broadcasted_iota(jnp.int32, (32, 384), 1) % 96
    key = lax.broadcasted_iota(jnp.int32, (32, 384), 0)

    def attend(i):
        reach = pl.ds(pl.multiple_of(i * 96, 32), 1632)
        rows = pl.ds(pl.multiple_of(i * 96, 32), 96)
        for h in range(4):
            at = pl.ds(h * 96, 96)
            product = flow[i, at, :].astype(f32) * attended[
                rows, h * 128 : (h + 1) * 128
            ].astype(f32)
            lse[i, at, :] = jnp.where(
                lane[:96] == 0, lse[i, at, :], jnp.sum(product, axis=-1, keepdims=True)
            )
        across = jnp.transpose(lse[i])
        total, delta = across[0:1, :], across[1:2, :]
        first = low[pl.ds(i, 1), :]
        scores[...] = contract_cols(window[reach, 0:128], query[i])
        change[...] = contract_cols(window[reach, 128:256], flow[i])

        def soften(c, carry):
            at = pl.ds(pl.multiple_of(c * 32, 32), 32)
            where = key + c * 32
            some = jnp.where(
                (where >= first) & (where <= last), scores[at, :] * scale - total, NEG
            )
            some = jnp.exp(some)
            probs[at, :] = some.astype(bf16)
            slopes[at, :] = (some * (change[at, :] - delta)).astype(bf16)
            return carry

        lax.fori_loop(0, 51, soften, 0, unroll=3)
        d_values[reach, :] += matmul(probs[...], flow[i])
        d_keys[reach, :] += matmul(slopes[...], query[i])
        turned = jnp.transpose(contract_rows(window[reach, 0:128], slopes[...])) * scale
        for h in range(4):
            grad_query[rows, h * 128 : (h + 1) * 128] = turned[h * 96 : (h + 1) * 96].astype(bf16)
        for n in range(4):
            columns = slice(n * 512, (n + 1) * 512)
            part[i, :, columns] = contract_cols(grad_query[rows, :], w_query[columns, :]).astype(bf16)

    attend(z.across)
    a0 = net.send(rows_half(part.at[z.across], 0), ra.at[0], z.plus)
    a1 = net.send(rows_half(part.at[z.across], 1), ra.at[1], z.minus)
    net.pump(2)
    attend(z.after)
    after = part.at[z.after]
    b0 = net.send(rows_half(after, 1), rows_half(rb.at[0], 1), z.plus)
    net.pump(4, 8)
    attend(z.before)
    before = part.at[z.before]
    b2 = net.send(rows_half(before, 0), rows_half(rb.at[1], 0), z.minus)
    a0.wait_recv()
    add_into(ra.at[0], rows_half(after, 0))
    b1 = net.send(ra.at[0], rows_half(rb.at[0], 0), z.plus)
    a1.wait_recv()
    add_into(ra.at[1], rows_half(before, 1))
    b3 = net.send(ra.at[1], rows_half(rb.at[1], 1), z.minus)
    attend(z.p)
    for j in range(5):
        at = slice(j * 384, (j + 1) * 384)
        pieces[j, :, 0:128] = (d_keys[at, :] * scale).astype(bf16)
        pieces[j, :, 128:256] = d_values[at, :].astype(bf16)

    def keys_values():
        sent = [net.send(pieces.at[4 - k], rk.at[k - 1], earlier[k - 1]) for k in (1, 2, 3, 4)]
        yield
        for copy in sent:
            copy.wait_recv()
        for i in range(4):
            at = pl.ds(i * 96, 96)
            add_into(pieces.at[4, at], *[rk.at[k, at] for k in range(4)], out=stage.at[i])
        sent = [
            net.send(stage.at[pos], rz.at[k], dev)
            for k, (pos, dev) in enumerate(zip((z.across, z.after, z.before), z.others))
        ]
        yield
        for copy in sent:
            copy.wait_recv()
        add_into(stage.at[place.z], *[rz.at[k] for k in range(3)], out=kv_rows)

    s_kv = net.begin(keys_values(), 1)
    net.pump(8)
    loads["normed"].wait()
    for n in range(4):
        total = contract_rows(normed[:, n * 512 : (n + 1) * 512], grad_query[...]).astype(bf16)
        for i in range(4):
            for which in range(2):
                home = (i % 2, which * 2 + n // 2, (n % 2) * 2 + i // 2)
                columns = slice(which * 256, (which + 1) * 256)
                part_query[home] = total[i * 128 : i * 128 + 64, columns]
                more_query[home] = total[i * 128 + 64 : (i + 1) * 128, columns]
    net.begin(
        rs2d_direct(net, place, part_query, "xy", queries, query_own.at[pl.ds(0, 64)]), 3
    )
    net.begin(
        rs2d_direct(net, place, more_query, "xy", queries_more, query_own.at[pl.ds(64, 64)]), 3
    )
    net.pump(2)
    net.pump(1)
    net.pump(3)
    net.pump(4)
    loads["keyval"].wait()
    loads["tok"].wait()
    net.until((1, s_kv))
    quarter = pl.ds(pl.multiple_of(place.z * 96, 96), 96)
    for n in range(4):
        total = contract_rows(normed[quarter, n * 512 : (n + 1) * 512], kv_rows[...]).astype(bf16)
        for i in range(4):
            for which in range(2):
                part_keyval[i % 2, which * 2 + n // 2, (n % 2) * 2 + i // 2] = total[
                    i * 128 + which * 64 : i * 128 + (which + 1) * 64, :
                ]

    def keyval():
        yield from rs2d_direct(net, place, part_keyval, "xy", keyvals, kv_own)
        sent = [
            net.send(kv_own, kv_in.at[k], place.dev(y=y.p if k < 3 else y.across, z=(place.z + k + 1) % 4))
            for k in range(7)
        ]
        yield
        for copy in sent:
            copy.wait_recv()
        own, other = pl.ds(pl.multiple_of(hi * 64, 64), 64), pl.ds(pl.multiple_of(64 - hi * 64, 64), 64)
        add_into(kv_own, kv_in.at[0], kv_in.at[1], kv_in.at[2], out=keyval_sum.at[own])
        add_into(kv_in.at[3], kv_in.at[4], kv_in.at[5], kv_in.at[6], out=keyval_sum.at[other])

    net.begin(keyval(), 7)
    for copy in (b0, b1, b2, b3):
        copy.wait_recv()
    six[...] = jnp.zeros_like(six)

    def norm_back(at):
        grad_norm = (
            part[place.z, at, :].astype(f32)
            + rb[0, at, :].astype(f32)
            + rb[1, at, :].astype(f32)
            + contract_cols(kv_rows[at, :], w_keyval[...])
        )
        center, inv = spread(tok[at, :].astype(f32))
        norm = center * inv
        down = grad_norm * vecs[0:1, :]
        mine[at, :] = (
            grad_mid[at, :]
            + inv
            * (
                down
                - jnp.mean(down, axis=-1, keepdims=True)
                - norm * jnp.mean(down * norm, axis=-1, keepdims=True)
            )
        ).astype(bf16)
        six[0:1, :] += jnp.sum(grad_norm * norm, axis=0, keepdims=True)
        six[1:2, :] += jnp.sum(grad_norm, axis=0, keepdims=True)

    for i in range(2):
        norm_back(pl.ds(i * 48, 48))
    net.begin(y_first(mine.at[top], lambda a, b: input_grad.at[a, b, top], lanes_half), 5)
    net.begin(z_first(mine.at[bottom], lambda a, b: input_grad.at[a, b, bottom], lanes_half), 5)
    six[2:3, :] = sums[2:3, :]
    six[3:4, :] = sums[0:1, :]
    six[4:5, :] = sums[1:2, :]
    six[5:6, :] = sums[3:4, :]
    bias_sum = jnp.sum(grad_query[...].astype(f32), axis=0, keepdims=True)
    value_sum = jnp.sum(kv_rows[:, 128:256].astype(f32), axis=0, keepdims=True)
    tiles[...] = jnp.zeros_like(tiles)
    for which in range(2):
        for h in range(2):
            at = (which * 2 + h) * 128
            tiles[which, 6 + h : 7 + h, :] = bias_sum[:, at : at + 128]
        for r in range(8):
            at = which * 1024 + r * 128
            tiles[which, 8 + r : 9 + r, :] = up_sum[0:1, at : at + 128]
    tiles[2, 6:7, :] = value_sum
    lane = lax.broadcasted_iota(jnp.int32, (16, 128), 1)

    def turn(tile, shift):
        shift = shift % 128
        return pltpu.roll(tile, shift, 1) if shift else tile

    for d in range(16):
        values = jnp.where((lane >= 8) & (lane < 16), turn(tiles[2], 136 - d * 8), 0.0)
        for which in range(2):
            piece = jnp.where(lane < 8, turn(tiles[which], 128 - d * 8), values)
            home = (d % 2, which * 2 + d // 8, (d // 2) % 4)
            part_small[home + (slice(6, 16),)] = piece[6:16]
            part_small[home + (slice(0, 6),)] = six[0:6, d * 128 : (d + 1) * 128]

    def small():
        yield from rs2d_direct(net, place, part_small, "xy", smalls, small_own)
        sent = [net.send(small_own, small_in.at[k], dev) for k, dev in enumerate(z.others)]
        yield
        for copy in sent:
            copy.wait_recv()
        total = small_own[...]
        whole = total + small_in[0] + small_in[1] + small_in[2]
        row = lax.broadcasted_iota(jnp.int32, (16, 128), 0)
        total = jnp.where((row < 6) | ((row == 6) & (lane >= 8)), whole, total)
        small_sum[0:16, :] = total
        small_sum[16:24, :] = turn(total[0:8], 120)

    net.begin(small(), 7)
    net.pump(7)
    while any(net.todo.values()):
        for group in (5, 7, 3, 7, 2, 4, 8):
            net.pump(group)
    net.run()
    keeps = [
        net.local(*pair)
        for pair in (
            (query_own, query_grad), (out_own, out_grad), (keyval_sum, keyval_grad),
            (small_sum, small_grad),
        )
    ]
    for keep in keeps:
        keep.wait()


def leave_kernel(
    input_grad, small, query, keyval, out, up, down,
    o_input, o_gain_one, o_shift_one, o_query, o_query_b, o_keyval, o_value_b, o_out,
    o_out_b, o_gain_two, o_shift_two, o_up, o_up_b, o_down, o_down_b,
):
    o_input[...] = input_grad[...].astype(f32)

    @pl.when(pl.program_id(0) == 0)
    def _():
        rows = (o_gain_one, o_shift_one, o_out_b, o_gain_two, o_shift_two, o_down_b)
        for i, row in enumerate(rows):
            row[...] = small[i]
        o_query_b[...] = small[6:8, 0:8]
        o_value_b[...] = small[22, 0:8]
        o_up_b[...] = small[8:16, 0:8]
        o_query[...] = query[...]
        o_keyval[...] = keyval[...]
        o_out[...] = out[...]
        o_up[...] = up[...]
        o_down[...] = down[...]


def leave(input_grad, *rest):
    rows = pl.BlockSpec((256, 2048), lambda i: (i, 0))

    def fixed(shape):
        return pl.BlockSpec(shape, lambda i: (0,) * len(shape))

    shapes = [(128,), (128,), (128, 256), (2, 8), (128, 256), (8,), (256, 128), (128,), (128,),
              (128,), (128, 1024), (8, 8), (1024, 128), (128,)]
    return pl.pallas_call(
        leave_kernel,
        grid=(3,),
        out_shape=[jax.ShapeDtypeStruct((768, 2048), f32)]
        + [jax.ShapeDtypeStruct(shape, f32) for shape in shapes],
        in_specs=[rows] + [fixed(array.shape) for array in rest],
        out_specs=[rows] + [fixed(shape) for shape in shapes],
        compiler_params=pltpu.CompilerParams(vmem_limit_bytes=60 << 20),
        cost_estimate=pl.CostEstimate(flops=0, bytes_accessed=16 << 20, transcendentals=0),
        name="leave",
    )(input_grad, *rest)


def matmul(left, right):
    return jnp.dot(left, right, preferred_element_type=f32)


def contract_rows(left, right):
    return lax.dot_general(left, right, (((0,), (0,)), ((), ())), preferred_element_type=f32)


def contract_cols(left, right):
    return lax.dot_general(left, right, (((1,), (1,)), ((), ())), preferred_element_type=f32)


def body(
    tokens, cotangent, segments, attn_norm_gain, attn_norm_bias, query_weight, query_bias,
    kv_weight, value_bias, out_weight, out_bias, mlp_norm_gain, mlp_norm_bias, up_weight,
    up_bias, down_weight, down_bias,
):
    dp = lax.axis_index("dp")
    tensor = lax.axis_index("tensor")
    hi, z = tensor // 4, tensor % 4
    half, heads = 384, 4

    start = dp * 768 + hi * half
    key_seg = lax.dynamic_slice_in_dim(
        jnp.concatenate([jnp.full((4 * half,), -1, jnp.int32), segments]), start, 5 * half
    )
    query_seg = key_seg[4 * half :]
    (
        query_w, keyval_w, out_w, up_w, down_w, vectors, normed_one, query_rows, window, lse,
        attended, normed_two, middle,
    ) = kernel_call(
        front, "front", 0,
        [tokens, jnp.stack([key_seg[i * 96 : i * 96 + 1632] for i in range(4)]),
         query_seg[:, None], attn_norm_gain[None], attn_norm_bias[None], out_bias[None],
         mlp_norm_gain[None], mlp_norm_bias[None], down_bias[None], query_bias, value_bias[None],
         up_bias, query_weight, kv_weight, out_weight, up_weight, down_weight],
        [ANY, VM, VM] + [ANY] * 14,
        [((2048, 512), bf16), ((2048, 256), bf16), ((512, 2048), bf16), ((2048, 2048), bf16),
         ((2048, 2048), bf16), ((8, 2048), f32), ((384, 2048), bf16), ((4, 384, 128), bf16),
         ((5, 4, 96, 256), bf16), ((4, 384, 128), f32), ((4, 96, 512), bf16),
         ((4, 96, 2048), bf16), ((96, 2048), f32)],
        [ANY] * 5 + [VM] + [ANY] * 6 + [VM],
        [pltpu.VMEM((2048, 512), bf16), pltpu.VMEM((2048, 256), bf16), pltpu.VMEM((512, 2048), bf16),
         pltpu.VMEM((2, 16, 24, 128), f32), pltpu.VMEM((384, 2048), bf16),
         pltpu.VMEM((384, 2048), bf16), pltpu.VMEM((4, 384, 128), bf16),
         pltpu.VMEM((5, 4, 96, 256), bf16), pltpu.VMEM((1920, 256), bf16),
         pltpu.VMEM((4, 384, 128), f32), pltpu.VMEM((4, 96, 512), bf16),
         pltpu.VMEM((4, 96, 1632), f32),
         pltpu.VMEM((128, 256), f32), pltpu.VMEM((64, 256), f32), pltpu.VMEM((256, 128), f32),
         pltpu.VMEM((128, 1024), f32), pltpu.VMEM((1024, 128), f32),
         pltpu.VMEM((128, 256), bf16), pltpu.VMEM((64, 256), bf16), pltpu.VMEM((256, 128), bf16),
         pltpu.VMEM((128, 1024), bf16), pltpu.VMEM((1024, 128), bf16),
         pltpu.VMEM((384, 2048), f32), pltpu.VMEM((384, 1632), f32), pltpu.VMEM((384, 1632), bf16),
         pltpu.VMEM((384, 128), bf16), pltpu.VMEM((4, 96, 2048), bf16),
         pltpu.VMEM((2, 48, 2048), bf16), pltpu.VMEM((2, 96, 2048), bf16), pltpu.VMEM((96, 2048), bf16),
         pltpu.VMEM((6, 1, 128), f32), pltpu.VMEM((2, 8), f32), pltpu.VMEM((1, 8), f32),
         pltpu.VMEM((8, 8), f32), pltpu.VMEM((24, 128), f32)]
        + sems(256, 40),
    )
    V = pltpu.VMEM
    (
        out_rows, grad_middle, grad_attn, sums, up_bias_sum, up_grad, down_grad,
    ) = kernel_call(
        mid, "mid", 2,
        [normed_two.reshape(half, 2048), cotangent, up_w, down_w, vectors, middle],
        [ANY, ANY, ANY, ANY, VM, VM],
        [((96, 2048), bf16), ((96, 2048), f32), ((4, 96, 2048), bf16), ((8, 2048), f32),
         ((1, 2048), f32), ((128, 1024), f32), ((1024, 128), f32)],
        [VM, VM, ANY, VM, VM, ANY, ANY],
        [V((2048, 2048), bf16), V((2048, 2048), bf16), V((384, 2048), bf16), V((384, 2048), bf16),
         V((768, 1024), bf16), V((768, 1024), bf16), V((384, 1024), bf16), V((384, 1024), bf16),
         V((768, 2048), bf16), V((768, 2048), bf16), V((4, 96, 2048), bf16),
         V((4, 96, 2048), bf16)]
        + [V((2, 48, 2048), bf16), V((2, 96, 2048), bf16)] * 2
        + [V((96, 2048), bf16)] + [V((4, 4, 128, 512), bf16), V((4, 4, 512, 128), bf16)] * 2
        + [V((128, 512), f32), V((512, 128), f32)] * 2
        + (ring_bufs((128, 512)) + ring_bufs((512, 128))) * 2 + sems(192, 16),
    )

    lows = jnp.sum(key_seg[None, :] < query_seg[:, None], axis=1, dtype=jnp.int32)
    lows = jnp.tile(lows.reshape(4, 96) - 96 * jnp.arange(4)[:, None], (1, heads))
    output, input_grad, query_grad, keyval_grad, out_grad, small_grad = kernel_call(
        tail, "tail", 3,
        [grad_attn.reshape(half, 2048), attended.reshape(half, 512), query_rows,
         window.reshape(5 * half, 256), lse, normed_one, query_w, keyval_w, out_w, tokens, out_rows,
         lows, grad_middle, vectors, sums, up_bias_sum],
        [ANY] * 11 + [VM] * 5,
        [((2, 4, 96, 2048), bf16), ((2, 4, 96, 2048), bf16), ((128, 256), f32), ((128, 256), f32),
         ((256, 128), f32), ((24, 128), f32)],
        [ANY] * 6,
        [V((384, 2048), bf16), V((384, 512), bf16), V((4, 384, 128), bf16), V((1920, 256), bf16),
         V((4, 384, 128), f32), V((384, 2048), bf16), V((2048, 512), bf16), V((2048, 256), bf16),
         V((512, 2048), bf16), V((96, 2048), bf16),
         V((2, 4, 4, 256, 128), bf16), V((2, 4, 4, 64, 256), bf16), V((2, 4, 4, 64, 256), bf16),
         V((2, 4, 4, 64, 256), bf16),
         V((4, 384, 128), bf16),
         V((1632, 384), f32), V((1632, 384), f32), V((1632, 384), bf16), V((1632, 384), bf16),
         V((1920, 128), f32), V((1920, 128), f32), V((384, 512), bf16), V((4, 96, 2048), bf16),
         V((2, 48, 2048), bf16), V((2, 96, 2048), bf16), V((5, 384, 256), bf16),
         V((4, 384, 256), bf16), V((4, 96, 256), bf16), V((3, 96, 256), bf16), V((96, 256), bf16),
         V((96, 2048), bf16), V((8, 2048), f32), V((3, 16, 128), f32), V((2, 4, 4, 16, 128), f32),
         V((16, 128), f32), V((3, 16, 128), f32), V((64, 256), f32),
         V((7, 64, 256), f32), V((128, 256), f32), V((256, 128), f32),
         V((128, 256), f32), V((24, 128), f32)]
        + direct_bufs((64, 256)) * 3 + direct_bufs((256, 128))
        + direct_bufs((16, 128), f32) + sems(128, 24),
    )
    return output.reshape(768, 2048), *leave(
        input_grad.reshape(768, 2048), small_grad, query_grad, keyval_grad, out_grad, up_grad,
        down_grad,
    )


def solution(mesh):
    return jax.shard_map(
        body,
        mesh=mesh,
        in_specs=(
            P("dp", None), P("dp", None), P(), P("dp"), P("dp"), P("dp", "tensor"),
            P("tensor", "dp"), P("dp", None), P("dp"), P("tensor", "dp"), P("dp"), P("dp"),
            P("dp"), P("dp", "tensor"), P("tensor", "dp"), P("tensor", "dp"), P("dp"),
        ),
        out_specs=(
            P("dp", None), P("dp", None), P("dp"), P("dp"), P("dp", "tensor"),
            P("tensor", "dp"), P("dp", None), P("dp"), P("tensor", "dp"), P("dp"), P("dp"),
            P("dp"), P("dp", "tensor"), P("tensor", "dp"), P("tensor", "dp"), P("dp"),
        ),
        check_vma=False,
    )
```

```python
import functools
import math

import jax
import jax.numpy as jnp
from jax import lax
from jax.experimental import pallas as pl
from jax.experimental.pallas import tpu as pltpu
from jax.sharding import PartitionSpec as P

HD = 128
EPS = 1e-05
NEG = -1e30
MESH = pl.DeviceIdType.MESH
bf16 = jnp.bfloat16
f32 = jnp.float32


class Place:
    def __init__(self):
        dp = lax.axis_index("dp")
        tensor = lax.axis_index("tensor")
        self.core = dp % 2
        self.x = (dp // 2) % 4
        self.y = (tensor // 4) * 2 + dp // 8
        self.z = tensor % 4

    def dev(self, x=None, y=None, z=None, core=None):
        x = self.x if x is None else x
        y = self.y if y is None else y
        z = self.z if z is None else z
        core = self.core if core is None else core
        return ((y % 2) * 8 + x * 2 + core, (y // 2) * 4 + z)

    def sibling(self):
        return self.dev(core=1 - self.core)

    def ring(self, axis):
        return Ring(self, axis)


class Ring:
    def __init__(self, place, axis):
        self.p = getattr(place, axis)
        self.plus = place.dev(**{axis: (self.p + 1) % 4})
        self.minus = place.dev(**{axis: (self.p + 3) % 4})
        self.after = (self.p + 1) % 4
        self.before = (self.p + 3) % 4
        self.across = (self.p + 2) % 4
        self.others = [place.dev(**{axis: self.across}), self.plus, self.minus]
        self.sources = [self.across, self.before, self.after]


class Net:
    def __init__(self, ssem, rsem, lsem):
        self.ssem, self.rsem, self.lsem = ssem, rsem, lsem
        self.n = 0
        self.m = 0
        self.sent = []
        self.group = 0
        self.todo = {}

    def send(self, src, dst, dev):
        i = self.n
        self.n += 1
        copy = pltpu.make_async_remote_copy(
            src_ref=src,
            dst_ref=dst,
            send_sem=self.ssem.at[i],
            recv_sem=self.rsem.at[i],
            device_id=dev,
            device_id_type=MESH,
        )
        copy.start()
        self.sent.append(copy)
        return copy

    def local(self, src, dst):
        i = self.m
        self.m += 1
        copy = pltpu.make_async_copy(src, dst, self.lsem.at[i])
        copy.start()
        return copy

    def spawn(self, gen):
        place = self.todo.setdefault(self.group, [])
        place.append(gen)
        self.step(gen, place)

    def begin(self, gen, group=0):
        state = [False]

        def whole():
            yield from gen
            state[0] = True

        self.group = group
        self.spawn(whole())
        return state

    def step(self, gen, place):
        try:
            next(gen)
        except StopIteration:
            place.remove(gen)

    def pump(self, *groups):
        for group in groups:
            self.group = group
            place = self.todo.setdefault(group, [])
            for gen in list(place):
                self.step(gen, place)

    def until(self, *states):
        for group, state in states:
            while not state[0]:
                self.pump(group)

    def run(self, *gens):
        for gen in gens:
            self.spawn(gen)
        while any(self.todo.values()):
            self.pump(*self.todo)
        for copy in self.sent:
            copy.wait_send()


def greet(devices):
    barrier = pltpu.get_barrier_semaphore()
    for device in devices:
        pl.semaphore_signal(barrier, inc=1, device_id=device, device_id_type=MESH)
    pl.semaphore_wait(barrier, len(devices))


def rows_half(ref, which):
    n = ref.shape[-2] // 2
    if len(ref.shape) == 2:
        return ref.at[pl.ds(which * n, n), :]
    return ref.at[:, pl.ds(which * n, n), :]


def lane_step(shape):
    return max(16, min(shape[0], 32768 // shape[1]))


def over_rows(rows, step, fn):
    def one(i, carry):
        fn(pl.ds(pl.multiple_of(i * step, step), step))
        return carry

    lax.fori_loop(0, rows // step, one, 0)


def add_into(dst, *srcs, out=None):
    out = dst if out is None else out
    rows, step = dst.shape[0], lane_step(dst.shape)
    if rows % step:
        step = 16 if rows % 16 == 0 else rows

    def one(at):
        total = dst[at, :].astype(f32)
        for src in srcs:
            total = total + src[at, :].astype(f32)
        out[at, :] = total.astype(out.dtype)

    over_rows(rows, step, one)


def ag_ring(net, ring, slot, own, have=None, half=rows_half):
    have = have or (lambda pos: None)
    c0 = net.send(own, slot(ring.p), ring.plus)
    c1 = net.send(own, slot(ring.p), ring.minus)
    yield
    c0.wait_recv()
    one = half(slot(ring.before), 0)
    c2 = net.send(one, one, ring.plus)
    have(ring.before)
    c1.wait_recv()
    two = half(slot(ring.after), 1)
    c3 = net.send(two, two, ring.minus)
    have(ring.after)
    yield
    c2.wait_recv()
    c3.wait_recv()
    have(ring.across)


def ag2d(net, place, own, slot, first, second):
    sib = place.sibling()
    pairs = []

    def give(a, b, src=None):
        ref = slot(a, b)
        pairs.append(net.send(ref if src is None else src, ref, sib))

    def column(a, src):
        return ag_ring(net, second, lambda b: slot(a, b), src, lambda b: give(a, b))

    def main():
        keep = net.local(own, slot(first.p, second.p))
        c0 = net.send(own, slot(first.p, second.p), first.plus)
        c1 = net.send(own, slot(first.p, second.p), first.minus)
        yield
        net.spawn(column(first.p, own))
        give(first.p, second.p, own)
        c0.wait_recv()
        one = rows_half(slot(first.before, second.p), 0)
        c2 = net.send(one, one, first.plus)
        net.spawn(column(first.before, slot(first.before, second.p)))
        c1.wait_recv()
        two = rows_half(slot(first.after, second.p), 1)
        c3 = net.send(two, two, first.minus)
        net.spawn(column(first.after, slot(first.after, second.p)))
        give(first.before, second.p)
        give(first.after, second.p)
        yield
        c2.wait_recv()
        c3.wait_recv()
        net.spawn(column(first.across, slot(first.across, second.p)))
        give(first.across, second.p)
        keep.wait()
        while len(pairs) < 16:
            yield
        for pair in pairs:
            pair.wait_recv()

    return main()


def ag2d_direct(net, place, own, slot, first, second):
    sib = place.sibling()
    pairs = []

    def give(a, b, src=None):
        ref = slot(a, b)
        pairs.append(net.send(ref if src is None else src, ref, sib))

    def column(a, src):
        return [net.send(src, slot(a, second.p), dev) for dev in second.others]

    keep = net.local(own, slot(first.p, second.p))
    rows = [net.send(own, slot(first.p, second.p), dev) for dev in first.others]
    columns = [(first.p, column(first.p, own))]
    give(first.p, second.p, own)
    yield
    for a, copy in zip(first.sources, rows):
        copy.wait_recv()
        columns.append((a, column(a, slot(a, second.p))))
        give(a, second.p)
    yield
    for a, copies in columns:
        for b, copy in zip(second.sources, copies):
            copy.wait_recv()
            give(a, b)
    yield
    keep.wait()
    for pair in pairs:
        pair.wait_recv()


def rs_ring(net, ring, src, ra, rb, done):
    across, after, before = src(ring.across), src(ring.after), src(ring.before)
    a0 = net.send(rows_half(across, 0), ra(0), ring.plus)
    a1 = net.send(rows_half(across, 1), ra(1), ring.minus)
    b0 = net.send(rows_half(after, 1), rows_half(rb(0), 1), ring.plus)
    b1 = net.send(rows_half(before, 0), rows_half(rb(1), 0), ring.minus)
    yield
    a0.wait_recv()
    add_into(ra(0), rows_half(after, 0))
    b2 = net.send(ra(0), rows_half(rb(0), 0), ring.plus)
    a1.wait_recv()
    add_into(ra(1), rows_half(before, 1))
    b3 = net.send(ra(1), rows_half(rb(1), 1), ring.minus)
    yield
    for copy in (b0, b1, b2, b3):
        copy.wait_recv()
    done(src(ring.p), rb(0), rb(1))


def rs2d_direct(net, place, part, order, bufs, out):
    rv, ra, rb = bufs
    first, second = (place.ring(axis) for axis in order)
    own = part.at[place.core]

    def along(a):
        return own.at[:, a] if order == "xy" else own.at[a]

    def one(a, b):
        return own.at[b, a] if order == "xy" else own.at[a, b]

    pair = net.send(part.at[1 - place.core], rv, place.sibling())
    yield
    pair.wait_recv()

    def add_pair(i, carry):
        add_into(own.at[i // 4, i % 4], rv.at[i // 4, i % 4])
        return carry

    lax.fori_loop(0, 16, add_pair, 0)
    sent = [
        net.send(along(pos), ra.at[k], dev)
        for k, (pos, dev) in enumerate(zip((first.across, first.after, first.before), first.others))
    ]
    yield
    for copy in sent:
        copy.wait_recv()
    for b in range(4):
        add_into(one(first.p, b), ra.at[0, b], ra.at[1, b], ra.at[2, b])
    sent = [
        net.send(one(first.p, pos), rb.at[k], dev)
        for k, (pos, dev) in enumerate(
            zip((second.across, second.after, second.before), second.others)
        )
    ]
    yield
    for copy in sent:
        copy.wait_recv()
    add_into(one(first.p, second.p), rb.at[0], rb.at[1], rb.at[2], out=out)


def direct_bufs(shape, dtype=bf16):
    return [
        pltpu.VMEM((4, 4) + shape, dtype),
        pltpu.VMEM((3, 4) + shape, dtype),
        pltpu.VMEM((3,) + shape, dtype),
    ]


def rs2d_sum(net, r0, first, second, bufs, out):
    ra, rb, r1, sa, sb = bufs
    firsts = (first.across, first.after, first.before, first.p)
    seconds = (second.across, second.after, second.before, second.p)

    def term(i, j):
        return r0(firsts[i], seconds[j])

    halves, wholes = {}, {}
    for j in range(4):
        halves[0, j] = net.send(rows_half(term(0, j), 0), ra.at[0, j], first.plus)
        halves[1, j] = net.send(rows_half(term(0, j), 1), ra.at[1, j], first.minus)
    yield
    for j in range(4):
        wholes[0, j] = net.send(rows_half(term(1, j), 1), rows_half(rb.at[0, j], 1), first.plus)
        wholes[1, j] = net.send(rows_half(term(2, j), 0), rows_half(rb.at[1, j], 0), first.minus)
    yield
    for j in range(4):
        halves[0, j].wait_recv()
        add_into(ra.at[0, j], rows_half(term(1, j), 0))
        wholes[2, j] = net.send(ra.at[0, j], rows_half(rb.at[0, j], 0), first.plus)
        halves[1, j].wait_recv()
        add_into(ra.at[1, j], rows_half(term(2, j), 1))
        wholes[3, j] = net.send(ra.at[1, j], rows_half(rb.at[1, j], 1), first.minus)
        if j == 1:
            yield
    yield

    def settle(j):
        for k in range(4):
            wholes[k, j].wait_recv()
        add_into(term(3, j), rb.at[0, j], rb.at[1, j], out=r1.at[j])

    settle(0)
    a0 = net.send(rows_half(r1.at[0], 0), sa.at[0], second.plus)
    a1 = net.send(rows_half(r1.at[0], 1), sa.at[1], second.minus)
    settle(1)
    b0 = net.send(rows_half(r1.at[1], 1), rows_half(sb.at[0], 1), second.plus)
    yield
    settle(2)
    b1 = net.send(rows_half(r1.at[2], 0), rows_half(sb.at[1], 0), second.minus)
    settle(3)
    yield
    a0.wait_recv()
    add_into(sa.at[0], rows_half(r1.at[1], 0))
    b2 = net.send(sa.at[0], rows_half(sb.at[0], 0), second.plus)
    a1.wait_recv()
    add_into(sa.at[1], rows_half(r1.at[2], 1))
    b3 = net.send(sa.at[1], rows_half(sb.at[1], 1), second.minus)
    yield
    for copy in (b0, b1, b2, b3):
        copy.wait_recv()
    add_into(r1.at[3], sb.at[0], sb.at[1], out=out)


def ring_bufs(shape, dtype=bf16):
    rows, cols = shape
    half = (rows // 2, cols)
    return [
        pltpu.VMEM((2, 4) + half, dtype),
        pltpu.VMEM((2, 4) + shape, dtype),
        pltpu.VMEM((4,) + shape, dtype),
        pltpu.VMEM((2,) + half, dtype),
        pltpu.VMEM((2,) + shape, dtype),
    ]


def sems(count, local):
    return [
        pltpu.SemaphoreType.DMA((count,)),
        pltpu.SemaphoreType.DMA((count,)),
        pltpu.SemaphoreType.DMA((local,)),
    ]


ANY = pl.BlockSpec(memory_space=pl.ANY)
VM = pl.BlockSpec(memory_space=pltpu.VMEM)


def kernel_call(body, name, cid, ins, in_specs, outs, out_specs, scratch, nbytes=1 << 20):
    return pl.pallas_call(
        body,
        out_shape=[jax.ShapeDtypeStruct(s, d) for s, d in outs],
        in_specs=in_specs,
        out_specs=out_specs,
        scratch_shapes=scratch,
        compiler_params=pltpu.CompilerParams(
            collective_id=cid, has_side_effects=True, vmem_limit_bytes=58 << 20
        ),
        cost_estimate=pl.CostEstimate(flops=0, bytes_accessed=nbytes, transcendentals=0),
        name=name,
    )(*ins)


def block_of(x, y, core):
    return (y % 2) * 8 + x * 2 + core


def col_at(d):
    return pl.ds(pl.multiple_of(d * 128, 128), 128)


def row_at(start, size):
    return pl.ds(pl.multiple_of(start, size), size)


def at_query(ref, x, y, core):
    return ref.at[row_at(block_of(x, y, core) * 128, 128), row_at((y // 2) * 256, 256)]


def at_keyval(ref, x, y, core):
    return ref.at[row_at(block_of(x, y, core) * 128 + (y // 2) * 64, 64), :]


def at_out(ref, x, y, core):
    return ref.at[row_at((y // 2) * 256, 256), col_at(block_of(x, y, core))]


def at_up(ref, x, y, core):
    return ref.at[row_at(block_of(x, y, core) * 128, 128), row_at((y // 2) * 1024, 1024)]


def at_down(ref, x, y, core):
    return ref.at[row_at((y // 2) * 1024, 1024), col_at(block_of(x, y, core))]


def at_small(ref, x, y, core):
    return ref.at[y // 2, block_of(x, y, core)]


def gather(net, place, at, own, whole, order, how=ag2d):
    x, y = place.ring("x"), place.ring("y")
    if order == "xy":
        return how(net, place, own, lambda a, b: at(whole, a, b, place.core), x, y)
    return how(net, place, own, lambda a, b: at(whole, b, a, place.core), y, x)


def plane_peers(place):
    x, y = place.ring("x"), place.ring("y")
    return [place.sibling(), x.plus, x.minus, y.plus, y.minus]


def spread(values):
    center = values - jnp.mean(values, axis=-1, keepdims=True)
    return center, lax.rsqrt(jnp.mean(center * center, axis=-1, keepdims=True) + EPS)


def cast_into(dst, src):
    step = lane_step(dst.shape)
    step = step if dst.shape[0] % step == 0 else 16

    def one(at):
        dst[at, :] = src[at, :].astype(dst.dtype)

    over_rows(dst.shape[0], step, one)


def front(
    tokens, key_seg, v0, v1, v2, v3, v4, v5, query_bias, value_bias, up_bias,
    query_w, keyval_w, out_w, up_w, down_w,
    o_query_w, o_keyval_w, o_out_w, g_up, g_down, vecs, o_normed, o_query, o_window, o_lse,
    o_attended, normed_two, middle,
    g_query, g_keyval, g_out, g_small, tok, normed, query, window, take, lse, attended, bias,
    f_query, f_keyval, f_out, f_up, f_down, b_query, b_keyval, b_out, b_up, b_down,
    unit, scores, weights, mixed, part, ra, rb, mine, rows6, short_q, short_v, short_u, small_own,
    *sem,
):
    place = Place()
    z = place.ring("z")
    hi = place.y // 2
    block = ((place.y % 2) * 8 + place.x * 2 + place.core) * 2 + hi
    earlier = [device_of_block(place, (block + 32 - k) % 32) for k in (1, 2, 3, 4)]
    later = [device_of_block(place, (block + k) % 32) for k in (1, 2, 3, 4)]
    net = Net(*sem)
    half_rows = pl.ds(pl.multiple_of(hi * 64, 64), 64)
    shorts = [net.local(v, rows6.at[i]) for i, v in enumerate((v0, v1, v2, v3, v4, v5))]
    shorts += [net.local(query_bias, short_q), net.local(value_bias, short_v), net.local(up_bias, short_u)]
    loads = [
        net.local(keyval_w.at[half_rows, :], f_keyval),
        net.local(query_w, f_query),
        net.local(out_w, f_out),
        net.local(tokens.at[pl.ds(pl.multiple_of(hi * 384, 384), 384), :], tok),
        net.local(up_w, f_up),
        net.local(down_w, f_down),
    ]
    x, y = place.ring("x"), place.ring("y")
    greet([place.sibling()] + x.others + y.others + z.others + earlier + later)
    for short in shorts:
        short.wait()

    def rounded(values):
        return values.astype(bf16).astype(f32)

    small_own[...] = jnp.zeros_like(small_own)
    for i in range(6):
        small_own[i : i + 1, :] = rounded(rows6[i])
    small_own[6:8, 0:8] = rounded(short_q[...])
    small_own[8:16, 0:8] = rounded(short_u[...])
    small_own[16:17, 0:8] = rounded(short_v[...])
    s_small = net.begin(gather(net, place, at_small, small_own, g_small, "yx", ag2d_direct), 1)
    loads[0].wait()
    cast_into(b_keyval, f_keyval)
    s_keyval = net.begin(gather(net, place, at_keyval, b_keyval, g_keyval, "xy", ag2d_direct), 1)
    loads[3].wait()

    def norm_some(at):
        center, inv = spread(tok[at, :].astype(f32))
        unit[at, :] = center * inv

    over_rows(192, 16, norm_some)
    net.pump(1)
    loads[1].wait()
    cast_into(b_query, f_query)
    s_query = net.begin(gather(net, place, at_query, b_query, g_query, "xy", ag2d_direct), 2)
    loads[2].wait()
    cast_into(b_out, f_out)
    s_out = net.begin(gather(net, place, at_out, b_out, g_out, "yx", ag2d_direct), 2)
    loads[4].wait()
    cast_into(b_up, f_up)
    loads[5].wait()
    cast_into(b_down, f_down)
    net.begin(gather(net, place, at_up, b_up, g_up, "xy"), 3)
    net.begin(gather(net, place, at_down, b_down, g_down, "yx"), 3)
    over_rows(192, 16, lambda at: norm_some(pl.ds(pl.multiple_of(at.start + 192, 16), 16)))
    net.pump(1)
    net.until((1, s_small), (1, s_keyval))

    for d in range(16):
        vecs[0:6, d * 128 : (d + 1) * 128] = g_small[0, d, 0:6, :]
    lane = lax.broadcasted_iota(jnp.int32, (8, 128), 1)

    def collect(which, rows):
        total = jnp.zeros((8, 128), f32)
        for d in range(16):
            piece = jnp.where(lane < 8, g_small[which, d, rows : rows + 8, :], 0.0)
            total = total + (pltpu.roll(piece, d * 8, 1) if d else piece)
        return total

    biases = []
    for which in range(2):
        ups = collect(which, 8)
        for r in range(8):
            at = which * 1024 + r * 128
            vecs[6:7, at : at + 128] = ups[r : r + 1, :]
        biases.append(collect(which, 0))
    query_b = [biases[0][6:7], biases[0][7:8], biases[1][6:7], biases[1][7:8]]
    value_b = collect(0, 16)[0:1]

    def apply_some(at):
        normed[at, :] = (unit[at, :] * vecs[0:1, :] + vecs[1:2, :]).astype(bf16)

    over_rows(384, 16, apply_some)
    kv = jnp.dot(normed[...], g_keyval[...], preferred_element_type=f32)
    kv = (kv + jnp.concatenate([jnp.zeros((1, 128), f32), value_b], 1)).astype(bf16)
    for i in range(4):
        window[4, i] = kv[i * 96 : (i + 1) * 96]

    def keys_values():
        own = window.at[4, place.z]
        sent = [net.send(own, window.at[4 - k, place.z], later[k - 1]) for k in (1, 2, 3, 4)]
        yield
        for copy in sent:
            copy.wait_recv()
        mine = window.at[pl.ds(0, 4), place.z]
        sent = [net.send(mine, mine, dev) for dev in z.others]
        yield
        for copy in sent:
            copy.wait_recv()

    s_window = net.begin(keys_values(), 1)
    net.pump(2)
    diagonal = lax.broadcasted_iota(jnp.int32, (96, 96), 0) == lax.broadcasted_iota(
        jnp.int32, (96, 96), 1
    )
    row = lax.broadcasted_iota(jnp.int32, (96, 1632), 0)
    column = lax.broadcasted_iota(jnp.int32, (96, 1632), 1)
    for i in range(4):
        ids = jnp.where(diagonal, key_seg[i : i + 1, 1536:1632].astype(f32), 0.0)
        same = jnp.sum(ids, axis=-1, keepdims=True) == key_seg[i : i + 1, :].astype(f32)
        bias[i] = jnp.where(same & (column <= row + 1536), 0.0, NEG)
    net.pump(1)
    net.pump(3)
    net.pump(2)
    net.until((2, s_query))
    for i in range(4):
        rows = jnp.dot(normed[i * 96 : (i + 1) * 96, :], g_query[...], preferred_element_type=f32)
        for h in range(4):
            query[i, h * 96 : (h + 1) * 96, :] = (
                rows[:, h * 128 : (h + 1) * 128] + query_b[h]
            ).astype(bf16)
    net.until((1, s_window), (2, s_out))
    keeps = [
        net.local(*pair)
        for pair in (
            (g_query, o_query_w), (g_keyval, o_keyval_w), (g_out, o_out_w), (normed, o_normed),
            (query, o_query), (window, o_window),
        )
    ]
    for j in range(5):
        for i in range(4):
            take[pl.ds((j * 4 + i) * 96, 96), :] = window[j, i]
    scale = 1.0 / math.sqrt(HD)

    def attend(i):
        reach = pl.ds(pl.multiple_of(i * 96, 32), 1632)
        scores[...] = lax.dot_general(
            query[i], take[reach, 0:128], (((1,), (1,)), ((), ())), preferred_element_type=f32
        )

        def soften(c, carry):
            at = pl.ds(pl.multiple_of(c * 16, 16), 16)
            mask = pl.ds(pl.multiple_of((c % 6) * 16, 16), 16)
            some = scores[at, :] * scale + bias[i, mask, :]
            top = jnp.max(some, axis=-1, keepdims=True)
            some = jnp.exp(some - top)
            total = jnp.sum(some, axis=-1, keepdims=True)
            weights[at, :] = (some * (1.0 / total)).astype(bf16)
            lse[i, at, :] = jnp.broadcast_to(top + jnp.log(total), (16, 128))
            return carry

        lax.fori_loop(0, 24, soften, 0, unroll=8)
        mixed[...] = jnp.dot(
            weights[...], take[reach, 128:256], preferred_element_type=f32
        ).astype(bf16)
        for h in range(4):
            attended[i, :, h * 128 : (h + 1) * 128] = mixed[h * 96 : (h + 1) * 96, :]
        for n in range(4):
            columns = slice(n * 512, (n + 1) * 512)
            part[i, :, columns] = jnp.dot(
                attended[i], g_out[:, columns], preferred_element_type=f32
            ).astype(bf16)

    attend(z.across)
    a0 = net.send(rows_half(part.at[z.across], 0), ra.at[0], z.plus)
    a1 = net.send(rows_half(part.at[z.across], 1), ra.at[1], z.minus)
    attend(z.after)
    after = part.at[z.after]
    b0 = net.send(rows_half(after, 1), rows_half(rb.at[0], 1), z.plus)
    attend(z.before)
    before = part.at[z.before]
    b2 = net.send(rows_half(before, 0), rows_half(rb.at[1], 0), z.minus)
    a0.wait_recv()
    add_into(ra.at[0], rows_half(after, 0))
    b1 = net.send(ra.at[0], rows_half(rb.at[0], 0), z.plus)
    a1.wait_recv()
    add_into(ra.at[1], rows_half(before, 1))
    b3 = net.send(ra.at[1], rows_half(rb.at[1], 1), z.minus)
    net.pump(3)
    attend(z.p)
    keeps += [net.local(attended, o_attended), net.local(lse, o_lse)]

    def residual(at):
        mid = (
            tok[pl.ds(pl.multiple_of(place.z * 96 + at.start, 16), 16), :].astype(f32)
            + part[place.z, at, :].astype(f32)
            + rb[0, at, :].astype(f32)
            + rb[1, at, :].astype(f32)
            + vecs[2:3, :]
        )
        middle[at, :] = mid
        center, inv = spread(mid)
        mine[at, :] = (center * inv * vecs[3:4, :] + vecs[4:5, :]).astype(bf16)

    for which, copies in ((0, (b1, b2)), (1, (b0, b3))):
        for copy in copies:
            copy.wait_recv()
        at = pl.ds(which * 48, 48)
        over_rows(48, 16, lambda r: residual(pl.ds(pl.multiple_of(r.start + which * 48, 16), 16)))
        keeps.append(net.local(mine.at[at], normed_two.at[z.p, at]))
        net.begin(
            ag_ring(net, z, lambda i, at=at: normed_two.at[i, at], mine.at[at], half=lanes_half), 1
        )
    net.pump(3)
    net.pump(1)
    while any(net.todo[group] for group in (1, 3)):
        net.pump(3, 1)
    net.run()
    for keep in keeps:
        keep.wait()


def mid(
    normed_all, cotangent, up_w, down_w, vecs, middle,
    out_rows, grad_mid, grad_all, sums, up_sum, o_up, o_down,
    w_up, w_down, normed, cot, normed_pair, cot_pair, normed_sib, cot_sib, hidden, slope,
    part_norm, part_out, ra, rb, rc, rd, mine, up_terms, down_terms, up_later, down_later, up_grad, down_grad, up_more, down_more,
    *rest,
):
    place = Place()
    x, y, z = place.ring("x"), place.ring("y"), place.ring("z")
    hi = place.y // 2
    sib = place.sibling()
    ups, downs, ups_later, downs_later, sem = rest[:5], rest[5:10], rest[10:15], rest[15:20], rest[20:]
    net = Net(*sem)
    load_normed = net.local(normed_all, normed)
    load_cot = net.local(cotangent.at[pl.ds(pl.multiple_of(hi * 384, 384), 384), :], cot)
    load_up, load_down = [], []
    for c in range(4):
        at = pl.ds(c * 512, 512)
        load_up.append(net.local(up_w.at[:, at], w_up.at[:, at]))
        load_down.append(net.local(down_w.at[at, :], w_down.at[at, :]))
    greet([sib, x.plus, x.minus, y.plus, y.minus, z.plus, z.minus])

    def split(full, pair, other):
        for m in range(8):
            at = pl.ds(m * 128, 128)
            pair[0:384, at] = full[:, col_at(2 * m + place.core)]
            other[:, at] = full[:, col_at(2 * m + 1 - place.core)]
        return net.send(other, pair.at[pl.ds(384, 384), :], sib)

    load_normed.wait()
    swaps = [split(normed, normed_pair, normed_sib)]
    load_cot.wait()
    swaps.append(split(cot, cot_pair, cot_sib))
    for c in range(4):
        at = pl.ds(c * 512, 512)
        load_up[c].wait()
        load_down[c].wait()

        def some(r, carry):
            rows = pl.ds(pl.multiple_of(r * 192, 64), 192)
            upward = matmul(normed[rows, :], w_up[:, at]) + vecs[6:7, at]
            flow = contract_cols(cot[rows, :], w_down[at, :])
            square = upward * upward
            curve = jnp.tanh(0.7978845608028654 * upward * (1.0 + 0.044715 * square))
            hidden[rows, at] = (0.5 * upward * (1.0 + curve)).astype(bf16)
            steep = 0.5 * (1.0 + curve) + 0.5 * upward * (1.0 - curve * curve) * (
                0.7978845608028654 * (1.0 + 3.0 * 0.044715 * square)
            )
            slope[rows, at] = (flow * steep).astype(bf16)
            return carry

        lax.fori_loop(0, 2, some, 0, unroll=2)
        up_sum[0:1, at] = jnp.sum(slope[0:384, at].astype(f32), axis=0, keepdims=True)
        for pair in (hidden, slope):
            swaps.append(net.send(pair.at[pl.ds(0, 384), at], pair.at[pl.ds(384, 384), at], sib))

    def back():
        def done(own, one, two):
            sums[...] = jnp.zeros_like(sums)

            def some(at):
                grad = own[at, :].astype(f32) + one[at, :].astype(f32) + two[at, :].astype(f32)
                center, inv = spread(middle[at, :])
                norm = center * inv
                flow = grad * vecs[3:4, :]
                top = cot[pl.ds(pl.multiple_of(place.z * 96 + at.start, 16), 16), :].astype(f32)
                low = top + inv * (
                    flow
                    - jnp.mean(flow, axis=-1, keepdims=True)
                    - norm * jnp.mean(flow * norm, axis=-1, keepdims=True)
                )
                grad_mid[at, :] = low
                low = low.astype(bf16)
                mine[at, :] = low
                sums[0:1, :] += jnp.sum(grad * norm, axis=0, keepdims=True)
                sums[1:2, :] += jnp.sum(grad, axis=0, keepdims=True)
                sums[2:3, :] += jnp.sum(low.astype(f32), axis=0, keepdims=True)
                sums[3:4, :] += jnp.sum(top, axis=0, keepdims=True)

            for which in range(2):
                over_rows(48, 16, lambda r: some(pl.ds(pl.multiple_of(r.start + which * 48, 16), 16)))
                at = pl.ds(which * 48, 48)
                last.append(net.local(mine.at[at], grad_all.at[z.p, at]))
                net.spawn(
                    ag_ring(
                        net, z, lambda i, at=at: grad_all.at[i, at], mine.at[at], half=lanes_half
                    )
                )

        last = []
        yield from rs_ring(
            net, z, lambda i: part_norm.at[i], lambda i: ra.at[i], lambda i: rb.at[i], done
        )
        for keep in last:
            keep.wait()

    def fore():
        def done(own, one, two):
            def some(at):
                out_rows[at, :] = (
                    middle[at, :]
                    + own[at, :].astype(f32)
                    + one[at, :].astype(f32)
                    + two[at, :].astype(f32)
                    + vecs[5:6, :]
                ).astype(bf16)

            over_rows(96, 16, some)

        yield from rs_ring(
            net, z, lambda i: part_out.at[i], lambda i: rc.at[i], lambda i: rd.at[i], done
        )

    for copy in swaps:
        copy.wait_recv()

    def up_terms_of(k, carry):
        rows = pl.ds(pl.multiple_of((k % 2) * 512, 512), 512)
        columns = pl.ds(pl.multiple_of((k // 2) * 1024, 1024), 1024)
        total = contract_rows(normed_pair[:, rows], slope[:, columns])
        for i in range(4):
            up_terms[k, i] = total[i * 128 : (i + 1) * 128, 0:512].astype(bf16)
            up_later[k, i] = total[i * 128 : (i + 1) * 128, 512:1024].astype(bf16)
        return carry

    lax.fori_loop(0, 4, up_terms_of, 0)
    net.begin(rs2d_sum(net, lambda a, b: up_terms.at[a, b], y, x, ups, up_grad), 2)
    net.begin(rs2d_sum(net, lambda a, b: up_later.at[b, a], x, y, ups_later, up_more), 5)
    net.pump(2, 5)
    for c in range(4):
        at = slice(c * 512, (c + 1) * 512)
        total = contract_cols(slope[0:384, :], w_up[at, :])
        for i in range(4):
            part_norm[i, :, at] = total[i * 96 : (i + 1) * 96].astype(bf16)

    net.begin(back(), 1)

    def down_terms_of(k, carry):
        rows = pl.ds(pl.multiple_of((k // 2) * 1024, 1024), 1024)
        columns = pl.ds(pl.multiple_of((k % 2) * 512, 512), 512)
        total = contract_rows(hidden[:, rows], cot_pair[:, columns])
        for i in range(4):
            down_terms[i, k] = total[0:512, i * 128 : (i + 1) * 128].astype(bf16)
            down_later[i, k] = total[512:1024, i * 128 : (i + 1) * 128].astype(bf16)
        return carry

    lax.fori_loop(0, 4, down_terms_of, 0)
    net.begin(rs2d_sum(net, lambda a, b: down_terms.at[a, b], x, y, downs, down_grad), 4)
    net.begin(rs2d_sum(net, lambda a, b: down_later.at[b, a], y, x, downs_later, down_more), 6)
    net.pump(4, 6)
    net.pump(2, 5)
    net.pump(1)
    for c in range(4):
        at = slice(c * 512, (c + 1) * 512)
        total = matmul(hidden[0:384, :], w_down[:, at])
        for i in range(4):
            part_out[i, :, at] = total[i * 96 : (i + 1) * 96].astype(bf16)
    net.pump(2, 5, 4)
    net.pump(1)
    net.begin(fore(), 3)
    for groups in ((5, 2, 6, 4, 1), (5, 2, 6, 4, 3)):
        net.pump(*groups)
    while any(net.todo[group] for group in (5, 2, 6, 4)):
        net.pump(5, 2, 6, 4)
    net.run()
    keeps = [
        net.local(up_grad, o_up.at[:, pl.ds(0, 512)]),
        net.local(up_more, o_up.at[:, pl.ds(512, 512)]),
        net.local(down_grad, o_down.at[pl.ds(0, 512), :]),
        net.local(down_more, o_down.at[pl.ds(512, 512), :]),
    ]
    for keep in keeps:
        keep.wait()


def device_of_block(place, block):
    d = block // 2
    return ((d // 8) * 8 + ((d // 2) % 4) * 2 + d % 2, (block % 2) * 4 + place.z)


def lanes_half(ref, which):
    n = ref.shape[-1] // 2
    return ref.at[:, pl.ds(which * n, n)]


def tail(
    grad_all, attended_all, query_all, window_all, lse_all, normed_all, query_w, keyval_w, out_w,
    tokens, out_rows, low, grad_mid, vecs, sums, up_sum,
    output, input_grad, query_grad, keyval_grad, out_grad, small_grad,
    grad, attended, query, window, lse, normed, w_query, w_keyval, w_out, tok,
    part_out, part_query, more_query, part_keyval, flow, scores, change, probs, slopes, d_keys, d_values,
    grad_query, part, ra, rb, pieces, rk, stage, rz, kv_rows, mine, six, tiles, part_small,
    small_own, small_in, kv_own, kv_in, lows, query_own, out_own, keyval_sum, small_sum, *rest,
):
    place = Place()
    x, y, z = place.ring("x"), place.ring("y"), place.ring("z")
    hi = place.y // 2
    partner = y.others[0]
    block = ((place.y % 2) * 8 + place.x * 2 + place.core) * 2 + hi
    earlier = [device_of_block(place, (block + 32 - k) % 32) for k in (1, 2, 3, 4)]
    later = [device_of_block(place, (block + k) % 32) for k in (1, 2, 3, 4)]
    queries, queries_more, keyvals, outs, smalls, sem = (
        rest[:3], rest[3:6], rest[6:9], rest[9:12], rest[12:15], rest[15:],
    )
    net = Net(*sem)
    token_rows = pl.ds(pl.multiple_of(hi * 384 + place.z * 96, 96), 96)
    loads = {
        name: net.local(*pair)
        for name, pair in dict(
            grad=(grad_all, grad), attended=(attended_all, attended), out=(out_w, w_out),
            query=(query_all, query), window=(window_all, window), lse=(lse_all, lse),
            query_w=(query_w, w_query), normed=(normed_all, normed), keyval=(keyval_w, w_keyval),
            tok=(tokens.at[token_rows, :], tok),
        ).items()
    }
    twins = [place.dev(y=y.across, z=(place.z + k) % 4) for k in (1, 2, 3)]
    greet([place.sibling()] + x.others + y.others + z.others + twins + earlier + later)

    def y_first(own, slot, half):
        keep = net.local(own, slot(hi, z.p))
        swap = net.send(own, slot(hi, z.p), partner)
        net.spawn(ag_ring(net, z, lambda i: slot(hi, i), own, half=half))
        yield
        swap.wait_recv()
        net.spawn(ag_ring(net, z, lambda i: slot(1 - hi, i), slot(1 - hi, z.p), half=half))
        keep.wait()

    def z_first(own, slot, half):
        keep = net.local(own, slot(hi, z.p))
        swaps = [net.send(own, slot(hi, z.p), partner)]

        def have(i):
            swaps.append(net.send(slot(hi, i), slot(hi, i), partner))

        yield from ag_ring(net, z, lambda i: slot(hi, i), own, have, half)
        yield
        keep.wait()
        for swap in swaps:
            swap.wait_recv()

    net.pump(5, 1)
    top, bottom = pl.ds(0, 48), pl.ds(48, 48)
    net.begin(y_first(out_rows.at[top], lambda a, b: output.at[a, b, top], lanes_half), 4)
    net.begin(z_first(out_rows.at[bottom], lambda a, b: output.at[a, b, bottom], lanes_half), 8)
    loads["grad"].wait()
    loads["attended"].wait()
    for n in range(4):
        total = contract_rows(attended[...], grad[:, n * 512 : (n + 1) * 512]).astype(bf16)
        for i in range(4):
            for which in range(2):
                part_out[i % 2, which * 2 + n // 2, (n % 2) * 2 + i // 2] = total[
                    which * 256 : (which + 1) * 256, i * 128 : (i + 1) * 128
                ]
    net.begin(rs2d_direct(net, place, part_out, "xy", outs, out_own), 2)
    loads["out"].wait()
    whole = contract_cols(grad[...], w_out[...]).astype(bf16)
    for i in range(4):
        for h in range(4):
            flow[i, h * 96 : (h + 1) * 96, :] = whole[
                i * 96 : (i + 1) * 96, h * 128 : (h + 1) * 128
            ]
    d_keys[...] = jnp.zeros_like(d_keys)
    d_values[...] = jnp.zeros_like(d_values)
    for name in ("query", "window", "lse", "query_w"):
        loads[name].wait()
    scale = 1.0 / math.sqrt(HD)
    lane = lax.broadcasted_iota(jnp.int32, (384, 128), 1)
    for h in range(4):
        lows[:, h * 96 : (h + 1) * 96] = low[...]
    last = 1536 + lax.broadcasted_iota(jnp.int32, (32, 384), 1) % 96
    key = lax.broadcasted_iota(jnp.int32, (32, 384), 0)

    def attend(i):
        reach = pl.ds(pl.multiple_of(i * 96, 32), 1632)
        rows = pl.ds(pl.multiple_of(i * 96, 32), 96)
        for h in range(4):
            at = pl.ds(h * 96, 96)
            product = flow[i, at, :].astype(f32) * attended[
                rows, h * 128 : (h + 1) * 128
            ].astype(f32)
            lse[i, at, :] = jnp.where(
                lane[:96] == 0, lse[i, at, :], jnp.sum(product, axis=-1, keepdims=True)
            )
        across = jnp.transpose(lse[i])
        total, delta = across[0:1, :], across[1:2, :]
        first = lows[pl.ds(i, 1), :]
        scores[...] = contract_cols(window[reach, 0:128], query[i])
        change[...] = contract_cols(window[reach, 128:256], flow[i])

        def soften(c, carry):
            at = pl.ds(pl.multiple_of(c * 32, 32), 32)
            where = key + c * 32
            some = jnp.where(
                (where >= first) & (where <= last), scores[at, :] * scale - total, NEG
            )
            some = jnp.exp(some)
            probs[at, :] = some.astype(bf16)
            slopes[at, :] = (some * (change[at, :] - delta)).astype(bf16)
            return carry

        lax.fori_loop(0, 51, soften, 0, unroll=3)
        d_values[reach, :] += matmul(probs[...], flow[i])
        d_keys[reach, :] += matmul(slopes[...], query[i])
        turned = jnp.transpose(contract_rows(window[reach, 0:128], slopes[...])) * scale
        for h in range(4):
            grad_query[rows, h * 128 : (h + 1) * 128] = turned[h * 96 : (h + 1) * 96].astype(bf16)
        for n in range(4):
            columns = slice(n * 512, (n + 1) * 512)
            part[i, :, columns] = contract_cols(grad_query[rows, :], w_query[columns, :]).astype(bf16)

    attend(z.across)
    a0 = net.send(rows_half(part.at[z.across], 0), ra.at[0], z.plus)
    a1 = net.send(rows_half(part.at[z.across], 1), ra.at[1], z.minus)
    net.pump(2)
    attend(z.after)
    after = part.at[z.after]
    b0 = net.send(rows_half(after, 1), rows_half(rb.at[0], 1), z.plus)
    net.pump(4, 8)
    attend(z.before)
    before = part.at[z.before]
    b2 = net.send(rows_half(before, 0), rows_half(rb.at[1], 0), z.minus)
    a0.wait_recv()
    add_into(ra.at[0], rows_half(after, 0))
    b1 = net.send(ra.at[0], rows_half(rb.at[0], 0), z.plus)
    a1.wait_recv()
    add_into(ra.at[1], rows_half(before, 1))
    b3 = net.send(ra.at[1], rows_half(rb.at[1], 1), z.minus)
    attend(z.p)
    for j in range(5):
        at = slice(j * 384, (j + 1) * 384)
        pieces[j, :, 0:128] = (d_keys[at, :] * scale).astype(bf16)
        pieces[j, :, 128:256] = d_values[at, :].astype(bf16)

    def keys_values():
        sent = [net.send(pieces.at[4 - k], rk.at[k - 1], earlier[k - 1]) for k in (1, 2, 3, 4)]
        yield
        for copy in sent:
            copy.wait_recv()
        for i in range(4):
            at = pl.ds(i * 96, 96)
            add_into(pieces.at[4, at], *[rk.at[k, at] for k in range(4)], out=stage.at[i])
        sent = [
            net.send(stage.at[pos], rz.at[k], dev)
            for k, (pos, dev) in enumerate(zip((z.across, z.after, z.before), z.others))
        ]
        yield
        for copy in sent:
            copy.wait_recv()
        add_into(stage.at[place.z], *[rz.at[k] for k in range(3)], out=kv_rows)

    s_kv = net.begin(keys_values(), 1)
    net.pump(8)
    loads["normed"].wait()
    for n in range(4):
        total = contract_rows(normed[:, n * 512 : (n + 1) * 512], grad_query[...]).astype(bf16)
        for i in range(4):
            for which in range(2):
                home = (i % 2, which * 2 + n // 2, (n % 2) * 2 + i // 2)
                columns = slice(which * 256, (which + 1) * 256)
                part_query[home] = total[i * 128 : i * 128 + 64, columns]
                more_query[home] = total[i * 128 + 64 : (i + 1) * 128, columns]
    net.begin(
        rs2d_direct(net, place, part_query, "xy", queries, query_own.at[pl.ds(0, 64)]), 3
    )
    net.begin(
        rs2d_direct(net, place, more_query, "xy", queries_more, query_own.at[pl.ds(64, 64)]), 3
    )
    net.pump(2)
    net.pump(1)
    net.pump(3)
    net.pump(4)
    loads["keyval"].wait()
    loads["tok"].wait()
    net.until((1, s_kv))
    quarter = pl.ds(pl.multiple_of(place.z * 96, 96), 96)
    for n in range(4):
        total = contract_rows(normed[quarter, n * 512 : (n + 1) * 512], kv_rows[...]).astype(bf16)
        for i in range(4):
            for which in range(2):
                part_keyval[i % 2, which * 2 + n // 2, (n % 2) * 2 + i // 2] = total[
                    i * 128 + which * 64 : i * 128 + (which + 1) * 64, :
                ]

    def keyval():
        yield from rs2d_direct(net, place, part_keyval, "xy", keyvals, kv_own)
        sent = [
            net.send(kv_own, kv_in.at[k], place.dev(y=y.p if k < 3 else y.across, z=(place.z + k + 1) % 4))
            for k in range(7)
        ]
        yield
        for copy in sent:
            copy.wait_recv()
        own, other = pl.ds(pl.multiple_of(hi * 64, 64), 64), pl.ds(pl.multiple_of(64 - hi * 64, 64), 64)
        add_into(kv_own, kv_in.at[0], kv_in.at[1], kv_in.at[2], out=keyval_sum.at[own])
        add_into(kv_in.at[3], kv_in.at[4], kv_in.at[5], kv_in.at[6], out=keyval_sum.at[other])

    net.begin(keyval(), 7)
    for copy in (b0, b1, b2, b3):
        copy.wait_recv()
    six[...] = jnp.zeros_like(six)

    def norm_back(at):
        grad_norm = (
            part[place.z, at, :].astype(f32)
            + rb[0, at, :].astype(f32)
            + rb[1, at, :].astype(f32)
            + contract_cols(kv_rows[at, :], w_keyval[...])
        )
        center, inv = spread(tok[at, :].astype(f32))
        norm = center * inv
        down = grad_norm * vecs[0:1, :]
        mine[at, :] = (
            grad_mid[at, :]
            + inv
            * (
                down
                - jnp.mean(down, axis=-1, keepdims=True)
                - norm * jnp.mean(down * norm, axis=-1, keepdims=True)
            )
        ).astype(bf16)
        six[0:1, :] += jnp.sum(grad_norm * norm, axis=0, keepdims=True)
        six[1:2, :] += jnp.sum(grad_norm, axis=0, keepdims=True)

    for i in range(2):
        norm_back(pl.ds(i * 48, 48))
    net.begin(y_first(mine.at[top], lambda a, b: input_grad.at[a, b, top], lanes_half), 5)
    net.begin(z_first(mine.at[bottom], lambda a, b: input_grad.at[a, b, bottom], lanes_half), 5)
    six[2:3, :] = sums[2:3, :]
    six[3:4, :] = sums[0:1, :]
    six[4:5, :] = sums[1:2, :]
    six[5:6, :] = sums[3:4, :]
    bias_sum = jnp.sum(grad_query[...].astype(f32), axis=0, keepdims=True)
    value_sum = jnp.sum(kv_rows[:, 128:256].astype(f32), axis=0, keepdims=True)
    tiles[...] = jnp.zeros_like(tiles)
    for which in range(2):
        for h in range(2):
            at = (which * 2 + h) * 128
            tiles[which, 6 + h : 7 + h, :] = bias_sum[:, at : at + 128]
        for r in range(8):
            at = which * 1024 + r * 128
            tiles[which, 8 + r : 9 + r, :] = up_sum[0:1, at : at + 128]
    tiles[2, 6:7, :] = value_sum
    lane = lax.broadcasted_iota(jnp.int32, (16, 128), 1)

    def turn(tile, shift):
        shift = shift % 128
        return pltpu.roll(tile, shift, 1) if shift else tile

    for d in range(16):
        values = jnp.where((lane >= 8) & (lane < 16), turn(tiles[2], 136 - d * 8), 0.0)
        for which in range(2):
            piece = jnp.where(lane < 8, turn(tiles[which], 128 - d * 8), values)
            home = (d % 2, which * 2 + d // 8, (d // 2) % 4)
            part_small[home + (slice(6, 16),)] = piece[6:16]
            part_small[home + (slice(0, 6),)] = six[0:6, d * 128 : (d + 1) * 128]

    def small():
        yield from rs2d_direct(net, place, part_small, "xy", smalls, small_own)
        sent = [net.send(small_own, small_in.at[k], dev) for k, dev in enumerate(z.others)]
        yield
        for copy in sent:
            copy.wait_recv()
        total = small_own[...]
        whole = total + small_in[0] + small_in[1] + small_in[2]
        row = lax.broadcasted_iota(jnp.int32, (16, 128), 0)
        total = jnp.where((row < 6) | ((row == 6) & (lane >= 8)), whole, total)
        small_sum[0:16, :] = total
        small_sum[16:24, :] = turn(total[0:8], 120)

    net.begin(small(), 7)
    net.pump(7)
    while any(net.todo.values()):
        for group in (5, 7, 3, 7, 2, 4, 8):
            net.pump(group)
    net.run()
    keeps = [
        net.local(*pair)
        for pair in (
            (query_own, query_grad), (out_own, out_grad), (keyval_sum, keyval_grad),
            (small_sum, small_grad),
        )
    ]
    for keep in keeps:
        keep.wait()


def leave_kernel(
    input_grad, small, query, keyval, out, up, down,
    o_input, o_gain_one, o_shift_one, o_query, o_query_b, o_keyval, o_value_b, o_out,
    o_out_b, o_gain_two, o_shift_two, o_up, o_up_b, o_down, o_down_b,
):
    o_input[...] = input_grad[...].astype(f32)

    @pl.when(pl.program_id(0) == 0)
    def _():
        rows = (o_gain_one, o_shift_one, o_out_b, o_gain_two, o_shift_two, o_down_b)
        for i, row in enumerate(rows):
            row[...] = small[i]
        o_query_b[...] = small[6:8, 0:8]
        o_value_b[...] = small[22, 0:8]
        o_up_b[...] = small[8:16, 0:8]
        o_query[...] = query[...]
        o_keyval[...] = keyval[...]
        o_out[...] = out[...]
        o_up[...] = up[...]
        o_down[...] = down[...]


def leave(input_grad, *rest):
    rows = pl.BlockSpec((256, 2048), lambda i: (i, 0))

    def fixed(shape):
        return pl.BlockSpec(shape, lambda i: (0,) * len(shape))

    shapes = [(128,), (128,), (128, 256), (2, 8), (128, 256), (8,), (256, 128), (128,), (128,),
              (128,), (128, 1024), (8, 8), (1024, 128), (128,)]
    return pl.pallas_call(
        leave_kernel,
        grid=(3,),
        out_shape=[jax.ShapeDtypeStruct((768, 2048), f32)]
        + [jax.ShapeDtypeStruct(shape, f32) for shape in shapes],
        in_specs=[rows] + [fixed(array.shape) for array in rest],
        out_specs=[rows] + [fixed(shape) for shape in shapes],
        compiler_params=pltpu.CompilerParams(vmem_limit_bytes=60 << 20),
        cost_estimate=pl.CostEstimate(flops=0, bytes_accessed=16 << 20, transcendentals=0),
        name="leave",
    )(input_grad, *rest)


def matmul(left, right):
    return jnp.dot(left, right, preferred_element_type=f32)


def contract_rows(left, right):
    return lax.dot_general(left, right, (((0,), (0,)), ((), ())), preferred_element_type=f32)


def contract_cols(left, right):
    return lax.dot_general(left, right, (((1,), (1,)), ((), ())), preferred_element_type=f32)


def body(
    tokens, cotangent, segments, attn_norm_gain, attn_norm_bias, query_weight, query_bias,
    kv_weight, value_bias, out_weight, out_bias, mlp_norm_gain, mlp_norm_bias, up_weight,
    up_bias, down_weight, down_bias,
):
    dp = lax.axis_index("dp")
    tensor = lax.axis_index("tensor")
    hi, z = tensor // 4, tensor % 4
    half, heads = 384, 4

    start = dp * 768 + hi * half
    key_seg = lax.dynamic_slice_in_dim(
        jnp.concatenate([jnp.full((4 * half,), -1, jnp.int32), segments]), start, 5 * half
    )
    query_seg = key_seg[4 * half :]
    (
        query_w, keyval_w, out_w, up_w, down_w, vectors, normed_one, query_rows, window, lse,
        attended, normed_two, middle,
    ) = kernel_call(
        front, "front", 0,
        [tokens, jnp.stack([key_seg[i * 96 : i * 96 + 1632] for i in range(4)]),
         attn_norm_gain[None], attn_norm_bias[None], out_bias[None],
         mlp_norm_gain[None], mlp_norm_bias[None], down_bias[None], query_bias, value_bias[None],
         up_bias, query_weight, kv_weight, out_weight, up_weight, down_weight],
        [ANY, VM] + [ANY] * 14,
        [((2048, 512), bf16), ((2048, 256), bf16), ((512, 2048), bf16), ((2048, 2048), bf16),
         ((2048, 2048), bf16), ((8, 2048), f32), ((384, 2048), bf16), ((4, 384, 128), bf16),
         ((5, 4, 96, 256), bf16), ((4, 384, 128), f32), ((4, 96, 512), bf16),
         ((4, 96, 2048), bf16), ((96, 2048), f32)],
        [ANY] * 5 + [VM] + [ANY] * 6 + [VM],
        [pltpu.VMEM((2048, 512), bf16), pltpu.VMEM((2048, 256), bf16), pltpu.VMEM((512, 2048), bf16),
         pltpu.VMEM((2, 16, 24, 128), f32), pltpu.VMEM((384, 2048), bf16),
         pltpu.VMEM((384, 2048), bf16), pltpu.VMEM((4, 384, 128), bf16),
         pltpu.VMEM((5, 4, 96, 256), bf16), pltpu.VMEM((1920, 256), bf16),
         pltpu.VMEM((4, 384, 128), f32), pltpu.VMEM((4, 96, 512), bf16),
         pltpu.VMEM((4, 96, 1632), f32),
         pltpu.VMEM((128, 256), f32), pltpu.VMEM((64, 256), f32), pltpu.VMEM((256, 128), f32),
         pltpu.VMEM((128, 1024), f32), pltpu.VMEM((1024, 128), f32),
         pltpu.VMEM((128, 256), bf16), pltpu.VMEM((64, 256), bf16), pltpu.VMEM((256, 128), bf16),
         pltpu.VMEM((128, 1024), bf16), pltpu.VMEM((1024, 128), bf16),
         pltpu.VMEM((384, 2048), f32), pltpu.VMEM((384, 1632), f32), pltpu.VMEM((384, 1632), bf16),
         pltpu.VMEM((384, 128), bf16), pltpu.VMEM((4, 96, 2048), bf16),
         pltpu.VMEM((2, 48, 2048), bf16), pltpu.VMEM((2, 96, 2048), bf16), pltpu.VMEM((96, 2048), bf16),
         pltpu.VMEM((6, 1, 128), f32), pltpu.VMEM((2, 8), f32), pltpu.VMEM((1, 8), f32),
         pltpu.VMEM((8, 8), f32), pltpu.VMEM((24, 128), f32)]
        + sems(256, 40),
    )
    V = pltpu.VMEM
    (
        out_rows, grad_middle, grad_attn, sums, up_bias_sum, up_grad, down_grad,
    ) = kernel_call(
        mid, "mid", 2,
        [normed_two.reshape(half, 2048), cotangent, up_w, down_w, vectors, middle],
        [ANY, ANY, ANY, ANY, VM, VM],
        [((96, 2048), bf16), ((96, 2048), f32), ((4, 96, 2048), bf16), ((8, 2048), f32),
         ((1, 2048), f32), ((128, 1024), f32), ((1024, 128), f32)],
        [VM, VM, ANY, VM, VM, ANY, ANY],
        [V((2048, 2048), bf16), V((2048, 2048), bf16), V((384, 2048), bf16), V((384, 2048), bf16),
         V((768, 1024), bf16), V((768, 1024), bf16), V((384, 1024), bf16), V((384, 1024), bf16),
         V((768, 2048), bf16), V((768, 2048), bf16), V((4, 96, 2048), bf16),
         V((4, 96, 2048), bf16)]
        + [V((2, 48, 2048), bf16), V((2, 96, 2048), bf16)] * 2
        + [V((96, 2048), bf16)] + [V((4, 4, 128, 512), bf16), V((4, 4, 512, 128), bf16)] * 2
        + [V((128, 512), f32), V((512, 128), f32)] * 2
        + (ring_bufs((128, 512)) + ring_bufs((512, 128))) * 2 + sems(192, 16),
    )

    lows = jnp.sum(key_seg[None, :] < query_seg[:, None], axis=1, dtype=jnp.int32)
    lows = lows.reshape(4, 96) - 96 * jnp.arange(4)[:, None]
    output, input_grad, query_grad, keyval_grad, out_grad, small_grad = kernel_call(
        tail, "tail", 3,
        [grad_attn.reshape(half, 2048), attended.reshape(half, 512), query_rows,
         window.reshape(5 * half, 256), lse, normed_one, query_w, keyval_w, out_w, tokens, out_rows,
         lows, grad_middle, vectors, sums, up_bias_sum],
        [ANY] * 11 + [VM] * 5,
        [((2, 4, 96, 2048), bf16), ((2, 4, 96, 2048), bf16), ((128, 256), f32), ((128, 256), f32),
         ((256, 128), f32), ((24, 128), f32)],
        [ANY] * 6,
        [V((384, 2048), bf16), V((384, 512), bf16), V((4, 384, 128), bf16), V((1920, 256), bf16),
         V((4, 384, 128), f32), V((384, 2048), bf16), V((2048, 512), bf16), V((2048, 256), bf16),
         V((512, 2048), bf16), V((96, 2048), bf16),
         V((2, 4, 4, 256, 128), bf16), V((2, 4, 4, 64, 256), bf16), V((2, 4, 4, 64, 256), bf16),
         V((2, 4, 4, 64, 256), bf16),
         V((4, 384, 128), bf16),
         V((1632, 384), f32), V((1632, 384), f32), V((1632, 384), bf16), V((1632, 384), bf16),
         V((1920, 128), f32), V((1920, 128), f32), V((384, 512), bf16), V((4, 96, 2048), bf16),
         V((2, 48, 2048), bf16), V((2, 96, 2048), bf16), V((5, 384, 256), bf16),
         V((4, 384, 256), bf16), V((4, 96, 256), bf16), V((3, 96, 256), bf16), V((96, 256), bf16),
         V((96, 2048), bf16), V((8, 2048), f32), V((3, 16, 128), f32), V((2, 4, 4, 16, 128), f32),
         V((16, 128), f32), V((3, 16, 128), f32), V((64, 256), f32),
         V((7, 64, 256), f32), V((4, 384), jnp.int32), V((128, 256), f32), V((256, 128), f32),
         V((128, 256), f32), V((24, 128), f32)]
        + direct_bufs((64, 256)) * 3 + direct_bufs((256, 128))
        + direct_bufs((16, 128), f32) + sems(128, 24),
    )
    return output.reshape(768, 2048), *leave(
        input_grad.reshape(768, 2048), small_grad, query_grad, keyval_grad, out_grad, up_grad,
        down_grad,
    )


def solution(mesh):
    return jax.shard_map(
        body,
        mesh=mesh,
        in_specs=(
            P("dp", None), P("dp", None), P(), P("dp"), P("dp"), P("dp", "tensor"),
            P("tensor", "dp"), P("dp", None), P("dp"), P("tensor", "dp"), P("dp"), P("dp"),
            P("dp"), P("dp", "tensor"), P("tensor", "dp"), P("tensor", "dp"), P("dp"),
        ),
        out_specs=(
            P("dp", None), P("dp", None), P("dp"), P("dp"), P("dp", "tensor"),
            P("tensor", "dp"), P("dp", None), P("dp"), P("tensor", "dp"), P("dp"), P("dp"),
            P("dp"), P("dp", "tensor"), P("tensor", "dp"), P("tensor", "dp"), P("dp"),
        ),
        check_vma=False,
    )
```
